32 devices in a mesh: case: 2 (over y), brick: 4 (over z), sect: 2 (over x), slab: 2 (over core).
Axes of the slice: x: 2, y: 2, z: 4, core: 2. Of those that a mesh axis runs over, the one named last changes fastest.
Arguments:
- geometry: bfloat16 [64, 32, 32, 128], P(None, ('case', 'brick'), ('sect', 'slab')), parts along dimension 1, may hold values from -6 to 6
- conv_kernels: bfloat16 [1, 3, 3, 3, 64, 64], replicated, may hold values from -0.15625 to 0.15625
- point_place: float32 [3, 8192], P(None, ('case', 'brick', 'sect', 'slab')), parts along dimension 1, may hold values from 0 to 1
- point_attr: bfloat16 [8192, 64], P(('case', 'brick', 'sect', 'slab')), parts along dimension 0, may hold values from -6 to 6
- destination: int32 [8192, 1], P(('case', 'brick', 'sect', 'slab')), parts along dimension 0, may hold values from 0 to 7; in each aligned block of 256 rows (0 to 255, 256 to 511, ...) at most 40 rows name the same one
- dense_first: bfloat16 [2, 128, 512], replicated, may hold values from -1 to 1
- dense_middle: bfloat16 [2, 3, 512, 512], replicated, may hold values from -0.5 to 0.5
- dense_last: bfloat16 [2, 4, 512], replicated, may hold values from -0.25 to 0.25
Outputs:
- prediction: float32 [4, 10240], P(None, ('case', 'brick', 'sect', 'slab')), parts along dimension 1
The draws below stay inside these ranges and needn't reach their ends.
There are 2 independent parts, one for each index of `case`. The reference program is written for one: setup_inputs(seed, part) draws one part's arguments, and reference() takes and returns one part's arrays. A program takes and returns all parts, laid end to end along the dimension named above; an argument that names none is the same for every part. Nothing has to cross between parts.
Inputs may be any that keep to these rules, and one draw needn't show every extreme that they name: A destination names a brick index and a sect index as brick * 2 + sect; its sect index fixes the point's section. No destination is named by more than 40 of the points of one device, and some device names some destination exactly 40 times.
All inputs are finite; a program needn't handle non-finite values.
Results may differ from the reference program's by a relative error of at most 0.0075.
Values may be sent and summed in bfloat16 or wider, within the bound.
No kernel may reach another device: no remote copies, remote signals or barrier semaphores. Data moves between devices by JAX's collectives and lax.ppermute only.
A program may use at most 64 MiB of HBM per device.

```python
import math
import jax
import jax.numpy as jnp
import numpy as np
from jax import lax

C = 64
ATTR = 64
HID = 512
OUTC = 4
NMID = 3
NCONV = 1
BX = 4
BY = 8
GZ = 128
PTS_DEV = 256
F = 128
CAP = 40
BUF = 320
GX = 16
GY = 32
PTS = 4096
ROWS = 5120
N_BRICK = 4
N_SECT = 2
N_SLAB = 2


def steps_of(rng, dims, cuts, low, high):
    def one(dim, shards_of):
        steps = jax.random.uniform(jax.random.fold_in(jax.random.fold_in(rng, 6), dim), (shards_of,), jnp.float32, low / len(cuts), high / len(cuts))
        return jnp.repeat(jnp.exp(steps), dims[dim] // shards_of).reshape((-1,) + (1,) * (len(dims) - dim - 1))

    gain = one(*cuts[0])
    for cut in cuts[1:]:
        gain = gain * one(*cut)
    return gain


def deal_out(rng, own, number, rows, number_of, top, bound, skew):
    order = jax.random.permutation(rng, number_of)
    crowded, common = load_shares(number_of, rows * top, bound, skew, True), load_shares(number_of, rows * top, bound, skew, False)
    places = jnp.arange(number_of)

    def named(lengths, offset_by):
        used = int((lengths > 0).sum())
        fixed = max(1, used // 4)
        shifted = fixed + (places - fixed + offset_by * (used - fixed)) % max(1, number_of - fixed)
        return jnp.zeros((number_of,), jnp.int32).at[order[jnp.where(places < fixed, places, shifted)]].set(jnp.asarray(lengths, jnp.int32))

    lengths = jnp.where(number % 4 == 0, named(crowded, number // 4), named(common, number - number // 4 - 1))
    mixed = jax.random.permutation(jax.random.fold_in(own, 3), number_of)
    giver, receiver = mixed[0:number_of // 2 * 2:2], mixed[1:number_of // 2 * 2:2]
    slack = jnp.minimum(lengths[giver] - 1, bound - lengths[receiver]) // 2
    slack = jnp.where((giver == order[0]) | (receiver == order[0]) | (lengths[receiver] == 0), 0, jnp.maximum(slack, 0))
    shifted = jax.random.randint(jax.random.fold_in(own, 4), (number_of // 2,), 0, 1 << 20) % (slack + 1)
    lengths = lengths.at[giver].add(-shifted).at[receiver].add(shifted)
    items = jnp.searchsorted(jnp.cumsum(lengths), jnp.arange(rows * top), side="right").astype(jnp.int32)
    listing = items.reshape(top, rows).T
    listing = listing[jax.random.permutation(jax.random.fold_in(own, 1), rows)]
    offset_by = jax.random.randint(jax.random.fold_in(own, 2), (rows, 1), 0, top)
    return jnp.take_along_axis(listing, (jnp.arange(top)[None, :] + offset_by) % top, axis=1)


def load_shares(count, total, bound, slope, full):
    portions = [(1 << 20) // math.isqrt(rank ** slope) + 1 for rank in range(1, count + 1)]
    largest = bound if full else min(bound, max(-(-total // count), total * portions[0] // sum(portions)))
    least = 1 if total - largest >= count - 1 else 0
    counts, spare = [largest] + [least] * (count - 1), total - largest - least * (count - 1)
    while spare > 0:
        movable = [i for i in range(1, count) if counts[i] < largest] or [i for i in range(1, count) if counts[i] < bound]
        whole, left = sum([portions[i] for i in movable]), spare
        for i in movable:
            extra = min(bound - counts[i], max(1, left * portions[i] // whole), spare)
            counts[i] = counts[i] + extra
            spare = spare - extra
    return np.array(counts)


def noise(own_key, shape, spread, most, shards=(), kind=jnp.bfloat16):
    loudness = steps_of(own_key, shape, shards, -0.22, 0.18) if shards else 1.0
    array = jax.random.normal(own_key, shape, jnp.float32) * spread * loudness
    return jnp.minimum(jnp.maximum(array, -most), most).astype(kind)


def setup_inputs(seed: int = 0, part: int = 0) -> dict:
    streams_of = jax.random.split(jax.random.key(seed), 9)
    part_splits = jax.random.split(jax.random.fold_in(streams_of[8], part), 9)
    geometry = noise(part_splits[0], (C, GX, GY, GZ), 1.0, 6.0, ((1, 4), (2, 4)))
    conv_kernels = noise(streams_of[1], (NCONV, 3, 3, 3, C, C), (27 * C) ** -0.5, 0.15625)
    point_place = jnp.clip(1.0 * jax.random.uniform(part_splits[2], (3, PTS), jnp.float32) ** steps_of(part_splits[2], (3, PTS), ((1, 16),), -0.2, 0.2), 0.0, 1.0)
    point_attr = noise(part_splits[3], (PTS, ATTR), 1.0, 6.0, ((0, 16),))
    destination_keys = jax.random.split(jax.random.fold_in(part_splits[4], 1), PTS // PTS_DEV)
    destination_turns = jax.random.permutation(jax.random.fold_in(part_splits[4], 3), PTS // PTS_DEV)
    destination = jax.vmap(lambda own, number: deal_out(jax.random.fold_in(part_splits[4], 2), own, number, PTS_DEV, N_BRICK * N_SECT, 1, CAP, 2))(destination_keys, destination_turns).reshape((PTS, 1))
    dense_first = noise(streams_of[5], (2, F, HID), (F // 4) ** -0.5, 1.0)
    dense_middle = noise(streams_of[6], (2, NMID, HID, HID), (HID // 4) ** -0.5, 0.5)
    dense_last = noise(streams_of[7], (2, OUTC, HID), HID ** -0.5, 0.25)
    return {"geometry": geometry, "conv_kernels": conv_kernels, "point_place": point_place, "point_attr": point_attr, "destination": destination, "dense_first": dense_first, "dense_middle": dense_middle, "dense_last": dense_last}


def convolve(features_now, kernel):
    response = lax.conv_general_dilated(features_now[None], kernel, (1, 1, 1), ((1, 1), (1, 1), (1, 1)), dimension_numbers=("NCDHW", "DHWIO", "NCDHW"), preferred_element_type=jnp.float32)
    return response[0]


def hat(offset):
    return jnp.maximum(0.0, 1.0 - jnp.abs(offset))


def network(table_rows, first_weights, middle_weights, last_weights):
    activity = jax.nn.gelu(jnp.dot(table_rows, first_weights, preferred_element_type=jnp.float32), approximate=True).astype(jnp.bfloat16)
    for ordinal in range(NMID):
        activity = jax.nn.gelu(jnp.dot(activity, middle_weights[ordinal], preferred_element_type=jnp.float32), approximate=True).astype(jnp.bfloat16)
    return lax.dot_general(last_weights, activity, (((1,), (1,)), ((), ())), preferred_element_type=jnp.float32)


def reference(geometry, conv_kernels, point_place, point_attr, destination, dense_first, dense_middle, dense_last):
    features_now = geometry
    for ordinal in range(NCONV):
        response = convolve(features_now, conv_kernels[ordinal])
        features_now = (features_now.astype(jnp.float32) + jax.nn.gelu(response, approximate=True)).astype(jnp.bfloat16)
    padded = jnp.pad(features_now, ((0, 0), (1, 1), (1, 1), (1, 1)))
    owner = jnp.arange(PTS, dtype=jnp.int32) // PTS_DEV
    brick_of = owner // (N_SECT * N_SLAB)
    column_of = owner % (N_SECT * N_SLAB)
    local_x = point_place[0] * BX
    local_y = point_place[1] * BY
    local_z = point_place[2] * GZ
    base_x = jnp.floor(local_x - 0.5).astype(jnp.int32)
    base_y = jnp.floor(local_y - 0.5).astype(jnp.int32)
    base_z = jnp.floor(local_z - 0.5).astype(jnp.int32)
    feature = jnp.zeros((C, PTS), jnp.float32)
    for shift_x in (0, 1):
        cell_x = base_x + shift_x
        weight_x = hat(local_x - (cell_x.astype(jnp.float32) + 0.5))
        for shift_y in (0, 1):
            cell_y = base_y + shift_y
            weight_y = hat(local_y - (cell_y.astype(jnp.float32) + 0.5))
            for shift_z in (0, 1):
                cell_z = base_z + shift_z
                rounded_z = lax.optimization_barrier(hat(local_z - (cell_z.astype(jnp.float32) + 0.5)).astype(jnp.bfloat16))
                weight_z = rounded_z.astype(jnp.float32)
                values = padded[:, brick_of * BX + cell_x + 1, column_of * BY + cell_y + 1, cell_z + 1].astype(jnp.float32)
                feature = feature + values * (weight_z * weight_x * weight_y)
    feature = feature.T.astype(jnp.bfloat16)
    table_rows = jnp.concatenate([feature, point_attr], axis=1)
    target = destination[:, 0]
    blocked = target.reshape(PTS // PTS_DEV, PTS_DEV)
    targets_all = jnp.arange(N_BRICK * N_SECT, dtype=jnp.int32)
    onehot = (blocked[:, :, None] == targets_all[None, None, :]).astype(jnp.int32)
    before = (jnp.cumsum(onehot, axis=1) - onehot).astype(jnp.int32)
    arrival = jnp.sum(before * onehot, axis=2).astype(jnp.int32).reshape(PTS)
    slot_index = (target * N_SLAB + owner % N_SLAB) * BUF + (owner // N_SLAB) * CAP + arrival
    upper = (target % N_SECT) >= (N_SECT // 2)
    surface_value = network(table_rows, dense_first[0], dense_middle[0], dense_last[0])
    volume_value = network(table_rows, dense_first[1], dense_middle[1], dense_last[1])
    chosen = jnp.where(upper[None, :], volume_value, surface_value)
    prediction = jnp.zeros((OUTC, ROWS), jnp.float32).at[:, slot_index.astype(jnp.int32)].set(chosen)
    return prediction
```

```python
import jax
import jax.numpy as jnp
from jax import lax
from jax.experimental import pallas as pl
from jax.experimental.pallas import tpu as pltpu
from jax.sharding import PartitionSpec as P

F32 = jnp.float32
BF16 = jnp.bfloat16
HALO = 2


def hat(offset):
    return jnp.maximum(0.0, 1.0 - jnp.abs(offset))


def gelu(value):
    return jax.nn.gelu(value, approximate=True)


def iota(shape, axis):
    return lax.broadcasted_iota(jnp.int32, shape, axis)


def call(body, outs, scratch, name, n_smem=0, n_any=0):
    def run(*args):
        spaces = (
            [pltpu.SMEM] * n_smem
            + [pltpu.VMEM] * (len(args) - n_smem - n_any)
            + [pl.ANY] * n_any
        )
        return pl.pallas_call(
            body,
            out_shape=outs,
            in_specs=[pl.BlockSpec(memory_space=s) for s in spaces],
            out_specs=jax.tree.map(lambda _: pl.BlockSpec(memory_space=pltpu.VMEM), outs),
            scratch_shapes=scratch,
            name=name,
            compiler_params=pltpu.CompilerParams(vmem_limit_bytes=48 << 20),
        )(*args)

    return run


def columns_body(g_ref, own_ref, up_ref, down_ref):
    span_x = g_ref.shape[1]
    for x in range(span_x):
        layer = jnp.swapaxes(g_ref[:, x].astype(F32), 0, 1).astype(BF16)
        own_ref[x] = layer
        if x < HALO:
            down_ref[x] = layer
        if x >= span_x - HALO:
            up_ref[x - (span_x - HALO)] = layer


def edges_body(own_ref, before_ref, after_ref, right_ref, left_ref):
    span_x, span_y = own_ref.shape[:2]
    for ref, base, span in (
        (before_ref, 0, HALO),
        (own_ref, HALO, span_x),
        (after_ref, HALO + span_x, HALO),
    ):
        right_ref[base : base + span] = ref[:, span_y - HALO :]
        left_ref[base : base + span] = ref[:, :HALO]


def make_points_body(span_x, span_y, bricks, sects, capacity):
    def body(flags_ref, place_ref, dest_ref, attr_ref, first_ref, pick_ref, wz_ref, wxy_ref, pre_ref):
        count = place_ref.shape[1]
        span_z = wz_ref.shape[0]
        slots = pick_ref.shape[0]
        half = slots // 2
        local_x = place_ref[0:1, :] * span_x
        local_y = place_ref[1:2, :] * span_y
        local_z = place_ref[2:3, :] * span_z
        cell_z = iota((span_z, count), 0).astype(F32) + 0.5
        wz_ref[...] = hat(local_z - cell_z).astype(BF16)
        weight_y = []
        for y in range(span_y + 2):
            w = hat(local_y - (y - 0.5))
            if y == 0:
                w = w * flags_ref[2].astype(F32)
            if y == span_y + 1:
                w = w * flags_ref[3].astype(F32)
            weight_y.append(w)
        for x in range(span_x + 2):
            w = hat(local_x - (x - 0.5))
            if x == 0:
                w = w * flags_ref[0].astype(F32)
            if x == span_x + 1:
                w = w * flags_ref[1].astype(F32)
            for y in range(span_y + 2):
                row = x * (span_y + 2) + y
                wxy_ref[row : row + 1, :] = w * weight_y[y]
        along = jnp.broadcast_to(dest_ref[...].astype(F32), (count, count))
        earlier, later = iota((count, count), 0), iota((count, count), 1)
        row = jnp.sum(jnp.where(earlier == later, along, 0.0), axis=0, keepdims=True)
        same = jnp.where((along == row) & (earlier < later), 1.0, 0.0)
        arrival = jnp.sum(same, axis=0, keepdims=True).astype(jnp.int32)
        target = row.astype(jnp.int32)
        brick, sect = target // sects, target % sects
        slot = (sect * bricks + brick) * capacity + arrival
        pick = jnp.where(iota((slots, count), 0) == slot, 1.0, 0.0).astype(BF16)
        pick_ref[...] = pick
        attr = jnp.dot(pick, attr_ref[...], preferred_element_type=F32).astype(BF16)
        channels = first_ref.shape[1] - attr.shape[1]
        for s in range(2):
            pre_ref[s * half : (s + 1) * half] = jnp.dot(
                attr[s * half : (s + 1) * half], first_ref[s, channels:], preferred_element_type=F32
            )

    return body


def main_body(
    own_ref, before_ref, after_ref, right_ref, left_ref, kernel_ref,
    pick_ref, wz_ref, wxy_ref, pre_ref, first_ref, last_ref, middle_hbm,
    value_ref, shifted, latent, middle_ref, sem,
):
    span_x, span_y, channels, span_z = own_ref.shape
    wide_x, wide_y = span_x + 2 * HALO, span_y + 2 * HALO
    out_x, out_y = span_x + 2, span_y + 2
    fetch = pltpu.make_async_copy(middle_hbm, middle_ref, sem)
    fetch.start()
    lane = iota((channels, span_z), 1)

    def column(x, y):
        if y < HALO:
            return left_ref[x, y]
        if y >= HALO + span_y:
            return right_ref[x, y - HALO - span_y]
        if x < HALO:
            return before_ref[x, y - HALO]
        if x >= HALO + span_x:
            return after_ref[x - HALO - span_x, y - HALO]
        return own_ref[x - HALO, y - HALO]

    def put(x):
        for y in range(wide_y):
            tile = column(x, y)
            wide = tile.astype(F32)
            lower = jnp.where(lane == 0, 0.0, pltpu.roll(wide, 1, 1)).astype(BF16)
            upper = jnp.where(lane == span_z - 1, 0.0, pltpu.roll(wide, span_z - 1, 1)).astype(BF16)
            for e, piece in enumerate((lower, tile, upper)):
                base = (x * 3 + e) * channels
                shifted[base : base + channels, y * span_z : (y + 1) * span_z] = piece

    put(0)
    put(1)
    total = jnp.zeros((channels, wz_ref.shape[1]), F32)
    for x in range(out_x):
        put(x + 2)
        rows = shifted[x * 3 * channels : (x + 3) * 3 * channels, :]
        part = jnp.dot(kernel_ref[...], rows, preferred_element_type=F32)
        for y in range(out_y):
            response = sum(
                part[b * channels : (b + 1) * channels, (y + b) * span_z : (y + b + 1) * span_z]
                for b in range(3)
            )
            centre = column(x + 1, y + 1).astype(F32)
            latent[y * channels : (y + 1) * channels, :] = (centre + gelu(response)).astype(BF16)
        sampled = jnp.dot(latent[...], wz_ref[...], preferred_element_type=F32)
        for y in range(out_y):
            row = x * out_y + y
            total += sampled[y * channels : (y + 1) * channels] * wxy_ref[row : row + 1, :]
    feature = lax.dot_general(
        pick_ref[...], total.astype(BF16), (((1,), (1,)), ((), ())), preferred_element_type=F32
    ).astype(BF16)
    fetch.wait()
    half = feature.shape[0] // 2
    for s in range(2):
        span = slice(s * half, (s + 1) * half)
        act = gelu(
            jnp.dot(feature[span], first_ref[s, :channels], preferred_element_type=F32)
            + pre_ref[span]
        ).astype(BF16)
        for i in range(middle_ref.shape[1]):
            act = gelu(jnp.dot(act, middle_ref[s, i], preferred_element_type=F32)).astype(BF16)
        value_ref[s] = lax.dot_general(
            last_ref[s], act, (((1,), (1,)), ((), ())), preferred_element_type=F32
        )


def shift(array, axes, step):
    size = lax.axis_size(axes)
    pairs = [(i, i + step) for i in range(size) if 0 <= i + step < size]
    return lax.ppermute(array, axes, pairs)


def swap_blocks(blocks, axis, dim):
    size = blocks.shape[dim]
    me = lax.axis_index(axis)
    lead, tail = blocks.shape[:dim], blocks.shape[dim + 1 :]
    step = size // 2
    while step:
        bit = (me // step) % 2
        split = blocks.reshape(lead + (size // (2 * step), 2, step) + tail)
        at = dim + 1
        sent = lax.dynamic_index_in_dim(split, 1 - bit, at, False)
        kept = lax.dynamic_index_in_dim(split, bit, at, False)
        got = lax.ppermute(sent, axis, [(i, i ^ step) for i in range(size)])
        split = jnp.stack(
            [jnp.where(bit == 0, kept, got), jnp.where(bit == 0, got, kept)], axis=at
        )
        blocks = split.reshape(lead + (size,) + tail)
        step //= 2
    return blocks


def on_device(
    geometry,
    conv_kernels,
    point_place,
    point_attr,
    destination,
    dense_first,
    dense_middle,
    dense_last,
):
    channels, span_x, span_y, span_z = geometry.shape
    count = point_place.shape[1]
    hidden = dense_first.shape[2]
    bricks, sects = lax.axis_size("brick"), lax.axis_size("sect")
    capacity = 5 * count // (4 * bricks * sects)
    slots = bricks * sects * capacity
    outputs = dense_last.shape[1]
    lines = ("sect", "slab")
    brick, line = lax.axis_index("brick"), lax.axis_index(lines)
    flags = jnp.stack(
        [brick > 0, brick < bricks - 1, line > 0, line < lax.axis_size(lines) - 1]
    ).astype(jnp.int32)
    kernel = conv_kernels[0].transpose(1, 4, 0, 2, 3).reshape(3 * channels, 9 * channels)

    def block(*shape):
        return jax.ShapeDtypeStruct(shape, BF16)

    own, up, down = call(
        columns_body,
        [
            block(span_x, span_y, channels, span_z),
            block(HALO, span_y, channels, span_z),
            block(HALO, span_y, channels, span_z),
        ],
        [],
        "columns",
    )(geometry)
    before = shift(up, "brick", 1)
    after = shift(down, "brick", -1)
    to_right, to_left = call(
        edges_body, [block(span_x + 2 * HALO, HALO, channels, span_z)] * 2, [], "edges"
    )(own, before, after)
    left = shift(to_right, lines, 1)
    right = shift(to_left, lines, -1)
    pick, wz, wxy, pre = call(
        make_points_body(span_x, span_y, bricks, sects, capacity),
        [
            block(slots, count),
            block(span_z, count),
            jax.ShapeDtypeStruct(((span_x + 2) * (span_y + 2), count), F32),
            jax.ShapeDtypeStruct((slots, hidden), F32),
        ],
        [],
        "points",
        n_smem=1,
    )(flags, point_place, destination, point_attr, dense_first)
    wide = (span_x + 2 * HALO) * 3 * channels
    value = call(
        main_body,
        jax.ShapeDtypeStruct((2, outputs, slots // 2), F32),
        [
            pltpu.VMEM((wide, (span_y + 2 * HALO) * span_z), BF16),
            pltpu.VMEM(((span_y + 2) * channels, span_z), BF16),
            pltpu.VMEM(dense_middle.shape, BF16),
            pltpu.SemaphoreType.DMA,
        ],
        "main",
        n_any=1,
    )(own, before, after, right, left, kernel, pick, wz, wxy, pre, dense_first, dense_last, dense_middle)
    value = value.transpose(1, 0, 2).reshape(outputs, sects, bricks, capacity)
    value = swap_blocks(value, "sect", 1)
    value = swap_blocks(value, "brick", 2)
    return value.transpose(0, 2, 1, 3).reshape(outputs, slots)


def solution(mesh):
    in_specs = (
        P(None, ("case", "brick"), ("sect", "slab"), None),
        P(),
        P(None, ("case", "brick", "sect", "slab")),
        P(("case", "brick", "sect", "slab"), None),
        P(("case", "brick", "sect", "slab"), None),
        P(),
        P(),
        P(),
    )
    out_specs = P(None, ("case", "brick", "sect", "slab"))
    return jax.shard_map(
        on_device, mesh=mesh, in_specs=in_specs, out_specs=out_specs, check_vma=False
    )
```

```python
import jax
import jax.numpy as jnp
from jax import lax
from jax.experimental import pallas as pl
from jax.experimental.pallas import tpu as pltpu
from jax.sharding import PartitionSpec as P

F32 = jnp.float32
BF16 = jnp.bfloat16
HALO = 2


def hat(offset):
    return jnp.maximum(0.0, 1.0 - jnp.abs(offset))


def gelu(value):
    return jax.nn.gelu(value, approximate=True)


def iota(shape, axis):
    return lax.broadcasted_iota(jnp.int32, shape, axis)


def call(body, outs, scratch, name, mib, n_smem=0):
    def run(*args):
        spaces = [pltpu.SMEM] * n_smem + [pltpu.VMEM] * (len(args) - n_smem)
        return pl.pallas_call(
            body,
            out_shape=outs,
            in_specs=[pl.BlockSpec(memory_space=s) for s in spaces],
            out_specs=jax.tree.map(lambda _: pl.BlockSpec(memory_space=pltpu.VMEM), outs),
            scratch_shapes=scratch,
            name=name,
            compiler_params=pltpu.CompilerParams(vmem_limit_bytes=mib << 20),
        )(*args)

    return run


def columns_body(g_ref, own_ref, up_ref, down_ref):
    span_x = g_ref.shape[1]
    for x in range(span_x):
        layer = jnp.swapaxes(g_ref[:, x].astype(F32), 0, 1).astype(BF16)
        own_ref[x] = layer
        if x < HALO:
            down_ref[x] = layer
        if x >= span_x - HALO:
            up_ref[x - (span_x - HALO)] = layer


def edges_body(own_ref, before_ref, after_ref, _, right_ref, left_ref):
    span_x, span_y = own_ref.shape[:2]
    for ref, base, span in (
        (before_ref, 0, HALO),
        (own_ref, HALO, span_x),
        (after_ref, HALO + span_x, HALO),
    ):
        right_ref[base : base + span] = ref[:, span_y - HALO :]
        left_ref[base : base + span] = ref[:, :HALO]


def make_points_body(span_x, span_y, bricks, sects, capacity):
    def body(
        flags_ref, place_ref, dest_ref, attr_ref, first_ref, conv_ref,
        pick_ref, wz_ref, wxy_ref, pre_ref, kernel_ref,
    ):
        count = place_ref.shape[1]
        span_z = wz_ref.shape[0]
        slots = pick_ref.shape[0]
        half = slots // 2
        local_x = place_ref[0:1, :] * span_x
        local_y = place_ref[1:2, :] * span_y
        local_z = place_ref[2:3, :] * span_z
        cell_z = iota((span_z, count), 0).astype(F32) + 0.5
        wz_ref[...] = hat(local_z - cell_z).astype(BF16)
        weight_y = []
        for y in range(span_y + 2):
            w = hat(local_y - (y - 0.5))
            if y == 0:
                w = w * flags_ref[2].astype(F32)
            if y == span_y + 1:
                w = w * flags_ref[3].astype(F32)
            weight_y.append(w)
        for x in range(span_x + 2):
            w = hat(local_x - (x - 0.5))
            if x == 0:
                w = w * flags_ref[0].astype(F32)
            if x == span_x + 1:
                w = w * flags_ref[1].astype(F32)
            for y in range(span_y + 2):
                row = x * (span_y + 2) + y
                wxy_ref[row : row + 1, :] = w * weight_y[y]
        row = dest_ref[...].astype(F32)
        earlier, later = iota((count, count), 0), iota((count, count), 1)
        diagonal = jnp.where(earlier == later, jnp.broadcast_to(row, (count, count)), 0.0)
        along = jnp.sum(diagonal, axis=1, keepdims=True)
        same = jnp.where((along == row) & (earlier < later), 1.0, 0.0)
        arrival = jnp.sum(same, axis=0, keepdims=True).astype(jnp.int32)
        target = row.astype(jnp.int32)
        brick, sect = target // sects, target % sects
        slot = (sect * bricks + brick) * capacity + arrival
        pick = jnp.where(iota((slots, count), 0) == slot, 1.0, 0.0).astype(BF16)
        pick_ref[...] = pick
        attr = lax.dot_general(
            pick, attr_ref[...], (((1,), (1,)), ((), ())), preferred_element_type=F32
        ).astype(BF16)
        channels = first_ref.shape[1] - attr.shape[1]
        for s in range(2):
            pre_ref[s * half : (s + 1) * half] = jnp.dot(
                attr[s * half : (s + 1) * half], first_ref[s, channels:], preferred_element_type=F32
            )
        for a in range(3):
            for b in range(3):
                for e in range(3):
                    tile = conv_ref[a, b, e].astype(F32).T.astype(BF16)
                    lanes = (a * 3 + e) * channels
                    kernel_ref[b * channels : (b + 1) * channels, lanes : lanes + channels] = tile

    return body


def main_body(
    own_ref, before_ref, after_ref, right_ref, left_ref, kernel_ref,
    pick_ref, wz_ref, wxy_ref, pre_ref, first_ref, last_ref, middle_ref,
    value_ref, shifted, latent,
):
    span_x, span_y, channels, span_z = own_ref.shape
    wide_x, wide_y = span_x + 2 * HALO, span_y + 2 * HALO
    out_x, out_y = span_x + 2, span_y + 2
    lane = iota((channels, span_z), 1)

    def column(x, y):
        if y < HALO:
            return left_ref[x, y]
        if y >= HALO + span_y:
            return right_ref[x, y - HALO - span_y]
        if x < HALO:
            return before_ref[x, y - HALO]
        if x >= HALO + span_x:
            return after_ref[x - HALO - span_x, y - HALO]
        return own_ref[x - HALO, y - HALO]

    def put(x):
        for y in range(wide_y):
            tile = column(x, y)
            wide = tile.astype(F32)
            lower = jnp.where(lane == 0, 0.0, pltpu.roll(wide, 1, 1)).astype(BF16)
            upper = jnp.where(lane == span_z - 1, 0.0, pltpu.roll(wide, span_z - 1, 1)).astype(BF16)
            for e, piece in enumerate((lower, tile, upper)):
                base = (x * 3 + e) * channels
                shifted[base : base + channels, y * span_z : (y + 1) * span_z] = piece

    put(0)
    put(1)
    total = jnp.zeros((channels, wz_ref.shape[1]), F32)
    for x in range(out_x):
        put(x + 2)
        rows = shifted[x * 3 * channels : (x + 3) * 3 * channels, :]
        part = jnp.dot(kernel_ref[...], rows, preferred_element_type=F32)
        for y in range(out_y):
            response = sum(
                part[b * channels : (b + 1) * channels, (y + b) * span_z : (y + b + 1) * span_z]
                for b in range(3)
            )
            centre = column(x + 1, y + 1).astype(F32)
            latent[y * channels : (y + 1) * channels, :] = (centre + gelu(response)).astype(BF16)
        sampled = jnp.dot(latent[...], wz_ref[...], preferred_element_type=F32)
        for y in range(out_y):
            row = x * out_y + y
            total += sampled[y * channels : (y + 1) * channels] * wxy_ref[row : row + 1, :]
    feature = lax.dot_general(
        pick_ref[...], total.astype(BF16), (((1,), (1,)), ((), ())), preferred_element_type=F32
    ).astype(BF16)
    half = feature.shape[0] // 2
    for s in range(2):
        span = slice(s * half, (s + 1) * half)
        act = gelu(
            jnp.dot(feature[span], first_ref[s, :channels], preferred_element_type=F32)
            + pre_ref[span]
        ).astype(BF16)
        for i in range(middle_ref.shape[1]):
            act = gelu(jnp.dot(act, middle_ref[s, i], preferred_element_type=F32)).astype(BF16)
        value_ref[s] = lax.dot_general(
            last_ref[s], act, (((1,), (1,)), ((), ())), preferred_element_type=F32
        )


def shift(array, axes, step):
    size = lax.axis_size(axes)
    pairs = [(i, i + step) for i in range(size) if 0 <= i + step < size]
    return lax.ppermute(array, axes, pairs)


def swap_blocks(blocks, axis, dim):
    size = blocks.shape[dim]
    me = lax.axis_index(axis)
    lead, tail = blocks.shape[:dim], blocks.shape[dim + 1 :]
    step = size // 2
    while step:
        bit = (me // step) % 2
        split = blocks.reshape(lead + (size // (2 * step), 2, step) + tail)
        at = dim + 1
        sent = lax.dynamic_index_in_dim(split, 1 - bit, at, False)
        kept = lax.dynamic_index_in_dim(split, bit, at, False)
        got = lax.ppermute(sent, axis, [(i, i ^ step) for i in range(size)])
        split = jnp.stack(
            [jnp.where(bit == 0, kept, got), jnp.where(bit == 0, got, kept)], axis=at
        )
        blocks = split.reshape(lead + (size,) + tail)
        step //= 2
    return blocks


def on_device(
    geometry,
    conv_kernels,
    point_place,
    point_attr,
    destination,
    dense_first,
    dense_middle,
    dense_last,
):
    channels, span_x, span_y, span_z = geometry.shape
    count = point_place.shape[1]
    hidden = dense_first.shape[2]
    bricks, sects = lax.axis_size("brick"), lax.axis_size("sect")
    capacity = 5 * count // (4 * bricks * sects)
    slots = bricks * sects * capacity
    outputs = dense_last.shape[1]
    lines = ("sect", "slab")
    brick, line = lax.axis_index("brick"), lax.axis_index(lines)
    flags = jnp.stack(
        [brick > 0, brick < bricks - 1, line > 0, line < lax.axis_size(lines) - 1]
    ).astype(jnp.int32)

    def block(*shape):
        return jax.ShapeDtypeStruct(shape, BF16)

    own, up, down = call(
        columns_body,
        [
            block(span_x, span_y, channels, span_z),
            block(HALO, span_y, channels, span_z),
            block(HALO, span_y, channels, span_z),
        ],
        [],
        "columns",
        8,
    )(geometry)
    before = shift(up, "brick", 1)
    after = shift(down, "brick", -1)
    pick, wz, wxy, pre, kernel = call(
        make_points_body(span_x, span_y, bricks, sects, capacity),
        [
            block(slots, count),
            block(span_z, count),
            jax.ShapeDtypeStruct(((span_x + 2) * (span_y + 2), count), F32),
            jax.ShapeDtypeStruct((slots, hidden), F32),
            block(3 * channels, 9 * channels),
        ],
        [],
        "points",
        12,
        n_smem=1,
    )(flags, point_place, destination.reshape(1, count), point_attr.T, dense_first, conv_kernels[0])
    to_right, to_left = call(
        edges_body, [block(span_x + 2 * HALO, HALO, channels, span_z)] * 2, [], "edges", 8
    )(own, before, after, wxy)
    left = shift(to_right, lines, 1)
    right = shift(to_left, lines, -1)
    wide = (span_x + 2 * HALO) * 3 * channels
    value = call(
        main_body,
        jax.ShapeDtypeStruct((2, outputs, slots // 2), F32),
        [
            pltpu.VMEM((wide, (span_y + 2 * HALO) * span_z), BF16),
            pltpu.VMEM(((span_y + 2) * channels, span_z), BF16),
        ],
        "main",
        28,
    )(own, before, after, right, left, kernel, pick, wz, wxy, pre, dense_first, dense_last, dense_middle)
    value = value.transpose(1, 0, 2).reshape(outputs, sects, bricks, capacity)
    value = swap_blocks(value, "sect", 1)
    value = swap_blocks(value, "brick", 2)
    return value.transpose(0, 2, 1, 3).reshape(outputs, slots)


def solution(mesh):
    in_specs = (
        P(None, ("case", "brick"), ("sect", "slab"), None),
        P(),
        P(None, ("case", "brick", "sect", "slab")),
        P(("case", "brick", "sect", "slab"), None),
        P(("case", "brick", "sect", "slab"), None),
        P(),
        P(),
        P(),
    )
    out_specs = P(None, ("case", "brick", "sect", "slab"))
    return jax.shard_map(
        on_device, mesh=mesh, in_specs=in_specs, out_specs=out_specs, check_vma=False
    )
```

```python
import jax
import jax.numpy as jnp
from jax import lax
from jax.experimental import pallas as pl
from jax.experimental.pallas import tpu as pltpu
from jax.sharding import PartitionSpec as P

F32 = jnp.float32
BF16 = jnp.bfloat16
HALO = 2


def hat(offset):
    return jnp.maximum(0.0, 1.0 - jnp.abs(offset))


def gelu(value):
    return jax.nn.gelu(value, approximate=True)


def iota(shape, axis):
    return lax.broadcasted_iota(jnp.int32, shape, axis)


def call(body, outs, scratch, name, mib, n_hbm=0):
    def run(*args):
        spaces = [pltpu.VMEM] * (len(args) - n_hbm) + [pltpu.HBM] * n_hbm
        args = [pltpu.with_memory_space_constraint(a, s) if s == pltpu.HBM else a for a, s in zip(args, spaces)]
        return pl.pallas_call(
            body,
            out_shape=outs,
            in_specs=[pl.BlockSpec(memory_space=s) for s in spaces],
            out_specs=jax.tree.map(lambda _: pl.BlockSpec(memory_space=pltpu.VMEM), outs),
            scratch_shapes=scratch,
            name=name,
            compiler_params=pltpu.CompilerParams(vmem_limit_bytes=mib << 20),
        )(*args)

    return run


def columns_body(g_ref, own_ref, up_ref, down_ref):
    span_x = g_ref.shape[1]
    for x in range(span_x):
        layer = jnp.swapaxes(g_ref[:, x].astype(F32), 0, 1).astype(BF16)
        own_ref[x] = layer
        if x < HALO:
            down_ref[x] = layer
        if x >= span_x - HALO:
            up_ref[x - (span_x - HALO)] = layer


def edges_body(own_ref, before_ref, after_ref, _, partner_ref, cross_ref):
    span_x, span_y = own_ref.shape[:2]
    facing = ((partner_ref, cross_ref), (cross_ref, partner_ref))
    for slab, (right_ref, left_ref) in enumerate(facing):

        @pl.when(lax.axis_index("slab") == slab)
        def _(right_ref=right_ref, left_ref=left_ref):
            for ref, base, span in (
                (before_ref, 0, HALO),
                (own_ref, HALO, span_x),
                (after_ref, HALO + span_x, HALO),
            ):
                right_ref[base : base + span] = ref[:, span_y - HALO :]
                left_ref[base : base + span] = ref[:, :HALO]


def make_points_body(span_x, span_y, bricks, sects, capacity):
    def body(
        place_ref, dest_ref, attr_ref, first_ref, conv_ref,
        pick_ref, wz_ref, wxy_ref, pre_ref, kernel_ref,
    ):
        count = place_ref.shape[1]
        span_z = wz_ref.shape[0]
        slots = pick_ref.shape[0]
        brick, line = lax.axis_index("brick"), lax.axis_index(("sect", "slab"))
        last_brick, last_line = lax.axis_size("brick") - 1, lax.axis_size(("sect", "slab")) - 1
        half = slots // 2
        local_x = place_ref[0:1, :] * span_x
        local_y = place_ref[1:2, :] * span_y
        local_z = place_ref[2:3, :] * span_z
        cell_z = iota((span_z, count), 0).astype(F32) + 0.5
        wz_ref[...] = hat(local_z - cell_z).astype(BF16)
        weight_y = []
        for y in range(span_y + 2):
            w = hat(local_y - (y - 0.5))
            if y == 0:
                w = jnp.where(line > 0, w, 0.0)
            if y == span_y + 1:
                w = jnp.where(line < last_line, w, 0.0)
            weight_y.append(w)
        for x in range(span_x + 2):
            w = hat(local_x - (x - 0.5))
            if x == 0:
                w = jnp.where(brick > 0, w, 0.0)
            if x == span_x + 1:
                w = jnp.where(brick < last_brick, w, 0.0)
            for y in range(span_y + 2):
                row = x * (span_y + 2) + y
                wxy_ref[row : row + 1, :] = w * weight_y[y]
        row = dest_ref[...].astype(F32)
        earlier, later = iota((count, count), 0), iota((count, count), 1)
        diagonal = jnp.where(earlier == later, jnp.broadcast_to(row, (count, count)), 0.0)
        along = jnp.sum(diagonal, axis=1, keepdims=True)
        same = jnp.where((along == row) & (earlier < later), 1.0, 0.0)
        arrival = jnp.sum(same, axis=0, keepdims=True).astype(jnp.int32)
        target = row.astype(jnp.int32)
        slot = ((target % sects) * bricks + target // sects) * capacity + arrival
        pick = jnp.where(iota((slots, count), 0) == slot, 1.0, 0.0).astype(BF16)
        pick_ref[...] = pick
        attr = lax.dot_general(
            pick, attr_ref[...], (((1,), (1,)), ((), ())), preferred_element_type=F32
        ).astype(BF16)
        channels = first_ref.shape[1] - attr.shape[1]
        for s in range(2):
            pre_ref[s * half : (s + 1) * half] = jnp.dot(
                attr[s * half : (s + 1) * half], first_ref[s, channels:], preferred_element_type=F32
            )
        for a in range(3):
            for b in range(3):
                for e in range(3):
                    tile = conv_ref[a, b, e].astype(F32).T.astype(BF16)
                    lanes = (a * 3 + e) * channels
                    kernel_ref[b * channels : (b + 1) * channels, lanes : lanes + channels] = tile

    return body


def shifted_tiles(tile):
    span_z = tile.shape[1]
    lane = iota(tile.shape, 1)
    wide = tile.astype(F32)
    lower = jnp.where(lane == 0, 0.0, pltpu.roll(wide, 1, 1)).astype(BF16)
    upper = jnp.where(lane == span_z - 1, 0.0, pltpu.roll(wide, span_z - 1, 1)).astype(BF16)
    return lower, tile, upper


def latent_tile(part, centre, y):
    channels, span_z = centre.shape
    response = sum(
        part[b * channels : (b + 1) * channels, (y + b) * span_z : (y + b + 1) * span_z]
        for b in range(3)
    )
    return (centre.astype(F32) + gelu(response)).astype(BF16)


def layer_of(own_ref, before_ref, after_ref, x):
    span_x = own_ref.shape[0]
    if x < HALO:
        return before_ref, x
    if x >= HALO + span_x:
        return after_ref, x - HALO - span_x
    return own_ref, x - HALO


def inner_body(
    own_ref, before_ref, after_ref, kernel_ref, wz_ref, wxy_ref, total_ref, shifted, latent
):
    span_x, span_y, channels, span_z = own_ref.shape

    def put(x):
        ref, at = layer_of(own_ref, before_ref, after_ref, x)
        for y in range(span_y):
            for e, piece in enumerate(shifted_tiles(ref[at, y])):
                base = (x * 3 + e) * channels
                shifted[base : base + channels, y * span_z : (y + 1) * span_z] = piece

    put(0)
    put(1)
    total = jnp.zeros(total_ref.shape, F32)
    for x in range(span_x + 2):
        put(x + 2)
        rows = shifted[x * 3 * channels : (x + 3) * 3 * channels, :]
        part = jnp.dot(kernel_ref[...], rows, preferred_element_type=F32)
        ref, at = layer_of(own_ref, before_ref, after_ref, x + 1)
        for y in range(span_y - 2):
            latent[y * channels : (y + 1) * channels, :] = latent_tile(part, ref[at, y + 1], y)
        sampled = jnp.dot(latent[...], wz_ref[...], preferred_element_type=F32)
        for y in range(span_y - 2):
            row = x * (span_y + 2) + y + 2
            total += sampled[y * channels : (y + 1) * channels] * wxy_ref[row : row + 1, :]
    total_ref[...] = total


def outer_body(
    own_ref, before_ref, after_ref, partner_ref, cross_ref, kernel_ref, total_ref,
    pick_ref, wz_ref, wxy_ref, pre_ref, last_ref, first_hbm, middle_hbm,
    value_ref, shifted, latent, first_ref, middle_ref, sems,
):
    span_x, span_y, channels, span_z = own_ref.shape
    copies = [
        pltpu.make_async_copy(first_hbm, first_ref, sems.at[0]),
        pltpu.make_async_copy(middle_hbm, middle_ref, sems.at[1]),
    ]
    for copy in copies:
        copy.start()
    slab = lax.axis_index("slab")
    group = 3 * channels

    def put(x):
        base = x * group
        ref, at = layer_of(own_ref, before_ref, after_ref, x)
        for side in range(2):
            for j in range(2):
                tile = ref[at, j if side == 0 else span_y - HALO + j]
                for e, piece in enumerate(shifted_tiles(tile)):
                    rows = slice(base + e * channels, base + (e + 1) * channels)
                    shifted[side, j + (HALO if side == 0 else 0), rows, :] = piece
        for ref, side in ((cross_ref, slab), (partner_ref, 1 - slab)):
            for j in range(2):
                for e, piece in enumerate(shifted_tiles(ref[x, j])):
                    rows = slice(base + e * channels, base + (e + 1) * channels)
                    shifted[side, j + HALO * side, rows, :] = piece

    put(0)
    put(1)
    total = total_ref[...]
    for x in range(span_x + 2):
        put(x + 2)
        rows = slice(x * group, (x + 3) * group)
        middle = slice((x + 1) * group + channels, (x + 1) * group + 2 * channels)
        for side in range(2):
            wide = jnp.concatenate([shifted[side, c, rows, :] for c in range(4)], axis=1)
            part = jnp.dot(kernel_ref[...], wide, preferred_element_type=F32)
            for y in range(2):
                at = (side * 2 + y) * channels
                centre = shifted[side, y + 1, middle, :]
                latent[at : at + channels, :] = latent_tile(part, centre, y)
        sampled = jnp.dot(latent[...], wz_ref[...], preferred_element_type=F32)
        for side in range(2):
            for y in range(2):
                at = (side * 2 + y) * channels
                row = x * (span_y + 2) + side * span_y + y
                total += sampled[at : at + channels] * wxy_ref[row : row + 1, :]
    feature = lax.dot_general(
        pick_ref[...], total.astype(BF16), (((1,), (1,)), ((), ())), preferred_element_type=F32
    ).astype(BF16)
    for copy in copies:
        copy.wait()
    half = feature.shape[0] // 2
    for s in range(2):
        span = slice(s * half, (s + 1) * half)
        act = gelu(
            jnp.dot(feature[span], first_ref[s, :channels], preferred_element_type=F32)
            + pre_ref[span]
        ).astype(BF16)
        for i in range(middle_ref.shape[1]):
            act = gelu(jnp.dot(act, middle_ref[s, i], preferred_element_type=F32)).astype(BF16)
        value_ref[s] = lax.dot_general(
            last_ref[s], act, (((1,), (1,)), ((), ())), preferred_element_type=F32
        )


def shift(array, axes, step):
    size = lax.axis_size(axes)
    pairs = [(i, i + step) for i in range(size) if 0 <= i + step < size]
    return lax.ppermute(array, axes, pairs)


def swap_blocks(blocks, axis, dim):
    size = blocks.shape[dim]
    me = lax.axis_index(axis)
    lead, tail = blocks.shape[:dim], blocks.shape[dim + 1 :]
    step = size // 2
    while step:
        bit = (me // step) % 2
        split = blocks.reshape(lead + (size // (2 * step), 2, step) + tail)
        at = dim + 1
        sent = lax.dynamic_index_in_dim(split, 1 - bit, at, False)
        kept = lax.dynamic_index_in_dim(split, bit, at, False)
        got = lax.ppermute(sent, axis, [(i, i ^ step) for i in range(size)])
        split = jnp.stack(
            [jnp.where(bit == 0, kept, got), jnp.where(bit == 0, got, kept)], axis=at
        )
        blocks = split.reshape(lead + (size,) + tail)
        step //= 2
    return blocks


def on_device(
    geometry,
    conv_kernels,
    point_place,
    point_attr,
    destination,
    dense_first,
    dense_middle,
    dense_last,
):
    channels, span_x, span_y, span_z = geometry.shape
    count = point_place.shape[1]
    hidden = dense_first.shape[2]
    bricks, sects = lax.axis_size("brick"), lax.axis_size("sect")
    capacity = 5 * count // (4 * bricks * sects)
    slots = bricks * sects * capacity
    outputs = dense_last.shape[1]
    lines = ("sect", "slab")
    width = lax.axis_size(lines)

    def block(*shape):
        return jax.ShapeDtypeStruct(shape, BF16)

    own, up, down = call(
        columns_body,
        [
            block(span_x, span_y, channels, span_z),
            block(HALO, span_y, channels, span_z),
            block(HALO, span_y, channels, span_z),
        ],
        [],
        "columns",
        8,
    )(geometry)
    before = shift(up, "brick", 1)
    after = shift(down, "brick", -1)
    pick, wz, wxy, pre, kernel = call(
        make_points_body(span_x, span_y, bricks, sects, capacity),
        [
            block(slots, count),
            block(span_z, count),
            jax.ShapeDtypeStruct(((span_x + 2) * (span_y + 2), count), F32),
            jax.ShapeDtypeStruct((slots, hidden), F32),
            block(3 * channels, 9 * channels),
        ],
        [],
        "points",
        12,
    )(point_place, destination.reshape(1, count), point_attr.T, dense_first, conv_kernels[0])
    edge = block(span_x + 2 * HALO, HALO, channels, span_z)
    to_partner, to_cross = call(edges_body, [edge] * 2, [], "edges", 4)(
        own, before, after, wxy
    )
    partner = lax.ppermute(to_partner, lines, [(i, i ^ 1) for i in range(width)])
    inward = [(i, i + 1) for i in range(1, width - 1, 2)]
    cross = lax.ppermute(to_cross, lines, inward + [(j, i) for i, j in inward])
    rows = (span_x + 2 * HALO) * 3 * channels
    total = call(
        inner_body,
        jax.ShapeDtypeStruct((channels, count), F32),
        [
            pltpu.VMEM((rows, span_y * span_z), BF16),
            pltpu.VMEM(((span_y - 2) * channels, span_z), BF16),
        ],
        "inner",
        10,
    )(own, before, after, kernel, wz, wxy)
    value = call(
        outer_body,
        jax.ShapeDtypeStruct((2, outputs, slots // 2), F32),
        [
            pltpu.VMEM((2, 4, rows, span_z), BF16),
            pltpu.VMEM((4 * channels, span_z), BF16),
            pltpu.VMEM(dense_first.shape, BF16),
            pltpu.VMEM(dense_middle.shape, BF16),
            pltpu.SemaphoreType.DMA((2,)),
        ],
        "outer",
        16,
        n_hbm=2,
    )(own, before, after, partner, cross, kernel, total, pick, wz, wxy, pre, dense_last,
      dense_first, dense_middle)
    value = value.transpose(1, 0, 2).reshape(outputs, sects, bricks, capacity)
    value = swap_blocks(value, "sect", 1)
    value = swap_blocks(value, "brick", 2)
    return value.transpose(0, 2, 1, 3).reshape(outputs, slots)


def solution(mesh):
    in_specs = (
        P(None, ("case", "brick"), ("sect", "slab"), None),
        P(),
        P(None, ("case", "brick", "sect", "slab")),
        P(("case", "brick", "sect", "slab"), None),
        P(("case", "brick", "sect", "slab"), None),
        P(),
        P(),
        P(),
    )
    out_specs = P(None, ("case", "brick", "sect", "slab"))
    return jax.shard_map(
        on_device, mesh=mesh, in_specs=in_specs, out_specs=out_specs, check_vma=False
    )
```

```python
import jax
import jax.numpy as jnp
from jax import lax
from jax.experimental import pallas as pl
from jax.experimental.pallas import tpu as pltpu
from jax.sharding import PartitionSpec as P


F32 = jnp.float32
BF16 = jnp.bfloat16
HALO = 2


def hat(offset):
    return jnp.maximum(0.0, 1.0 - jnp.abs(offset))


def gelu(value):
    half = 0.5 * value
    slope = 0.7978845608028654
    return half + half * jnp.tanh(value * (slope + (slope * 0.044715) * (value * value)))


def iota(shape, axis):
    return lax.broadcasted_iota(jnp.int32, shape, axis)


def call(body, outs, scratch, mib, n_hbm=0):
    def run(*args):
        spaces = [pltpu.VMEM] * (len(args) - n_hbm) + [pltpu.HBM] * n_hbm
        args = [pltpu.with_memory_space_constraint(a, s) if s == pltpu.HBM else a for a, s in zip(args, spaces)]
        return pl.pallas_call(
            body,
            out_shape=outs,
            in_specs=[pl.BlockSpec(memory_space=s) for s in spaces],
            out_specs=jax.tree.map(lambda _: pl.BlockSpec(memory_space=pltpu.VMEM), outs),
            scratch_shapes=scratch,
            compiler_params=pltpu.CompilerParams(vmem_limit_bytes=mib << 20),
        )(*args)

    return run


def columns_body(g_ref, own_ref, up_ref, down_ref, cross_ref):
    span_x, span_y = g_ref.shape[1:3]
    slab = lax.axis_index("slab")
    for x in range(span_x):
        layer = jnp.swapaxes(g_ref[:, x].astype(F32), 0, 1).astype(BF16)
        own_ref[x] = layer
        if x < HALO:
            down_ref[x] = layer
        if x >= span_x - HALO:
            up_ref[x - (span_x - HALO)] = layer
    for side in range(2):

        @pl.when(slab == side)
        def _(side=side):
            cross_ref[...] = own_ref[:, span_y - HALO :] if side else own_ref[:, :HALO]


def edges_body(own_ref, before_ref, after_ref, _, partner_ref, cross_ref):
    span_x, span_y = own_ref.shape[:2]
    for slab in range(2):

        @pl.when(lax.axis_index("slab") == slab)
        def _(slab=slab):
            near, far = slice(0, HALO), slice(span_y - HALO, span_y)
            facing, outward = (near, far) if slab else (far, near)
            partner_ref[:HALO] = before_ref[:, facing]
            partner_ref[HALO : HALO + span_x] = own_ref[:, facing]
            partner_ref[HALO + span_x :] = after_ref[:, facing]
            cross_ref[:HALO] = before_ref[:, outward]
            cross_ref[HALO:] = after_ref[:, outward]


def make_points_body(span_x, span_y, bricks, sects, capacity):
    def body(
        place_ref, dest_ref, attr_ref, first_ref, conv_ref, middle_hbm,
        pick_ref, wz_ref, wxy_ref, pre_ref, kernel_ref, middle_ref, sem,
    ):
        fetch = pltpu.make_async_copy(middle_hbm, middle_ref, sem)
        fetch.start()
        count = place_ref.shape[1]
        span_z = wz_ref.shape[0]
        slots = pick_ref.shape[0]
        brick, line = lax.axis_index("brick"), lax.axis_index(("sect", "slab"))
        last_brick, last_line = lax.axis_size("brick") - 1, lax.axis_size(("sect", "slab")) - 1
        half = slots // 2
        local_x = place_ref[0:1, :] * span_x
        local_y = place_ref[1:2, :] * span_y
        local_z = place_ref[2:3, :] * span_z
        cell_z = iota((span_z, count), 0).astype(F32) + 0.5
        wz_ref[...] = hat(local_z - cell_z).astype(BF16)
        weight_y = []
        for y in range(span_y + 2):
            w = hat(local_y - (y - 0.5))
            if y == 0:
                w = jnp.where(line > 0, w, 0.0)
            if y == span_y + 1:
                w = jnp.where(line < last_line, w, 0.0)
            weight_y.append(w)
        for x in range(span_x + 2):
            w = hat(local_x - (x - 0.5))
            if x == 0:
                w = jnp.where(brick > 0, w, 0.0)
            if x == span_x + 1:
                w = jnp.where(brick < last_brick, w, 0.0)
            for y in range(span_y + 2):
                row = x * (span_y + 2) + y
                wxy_ref[row : row + 1, :] = w * weight_y[y]
        row = dest_ref[...].astype(F32)
        earlier, later = iota((count, count), 0), iota((count, count), 1)
        diagonal = jnp.where(earlier == later, jnp.broadcast_to(row, (count, count)), 0.0)
        along = jnp.sum(diagonal, axis=1, keepdims=True)
        same = jnp.where((along == row) & (earlier < later), 1.0, 0.0)
        arrival = jnp.sum(same, axis=0, keepdims=True).astype(jnp.int32)
        target = row.astype(jnp.int32)
        slot = ((target % sects) * bricks + target // sects) * capacity + arrival
        pick = jnp.where(iota((slots, count), 0) == slot, 1.0, 0.0).astype(BF16)
        pick_ref[...] = pick
        attr = lax.dot_general(
            pick, attr_ref[...], (((1,), (1,)), ((), ())), preferred_element_type=F32
        ).astype(BF16)
        channels = first_ref.shape[1] - attr.shape[1]
        for s in range(2):
            pre_ref[s] = jnp.dot(
                attr[s * half : (s + 1) * half], first_ref[s, channels:], preferred_element_type=F32
            )
        group = 9 * channels
        kernel_ref[:channels, 3 * group :] = jnp.zeros((channels, group), BF16)
        kernel_ref[channels:, :group] = jnp.zeros((channels, group), BF16)
        for a in range(3):
            for b in range(3):
                for e in range(3):
                    tile = conv_ref[a, b, e].astype(F32).T.astype(BF16)
                    for j in range(2):
                        lanes = (j + b) * group + (a * 3 + e) * channels
                        kernel_ref[j * channels : (j + 1) * channels, lanes : lanes + channels] = tile
        fetch.wait()

    return body


def shifted_tiles(tile):
    span_z = tile.shape[1]
    lane = iota(tile.shape, 1)
    wide = tile.astype(F32)
    lower = jnp.where(lane == 0, 0.0, pltpu.roll(wide, 1, 1)).astype(BF16)
    upper = jnp.where(lane == span_z - 1, 0.0, pltpu.roll(wide, span_z - 1, 1)).astype(BF16)
    return lower, tile, upper


def layer_of(own_ref, before_ref, after_ref, x):
    span_x = own_ref.shape[0]
    if x < HALO:
        return before_ref, x
    if x >= HALO + span_x:
        return after_ref, x - HALO - span_x
    return own_ref, x - HALO


def inner_body(
    own_ref, before_ref, after_ref, kernel_ref, wz_ref, wxy_ref, total_ref, shifted, latent
):
    span_x, span_y, channels, span_z = own_ref.shape
    group, pairs, step = 3 * channels, (span_y - 2) // 2, 2

    def put(x):
        ref, at = layer_of(own_ref, before_ref, after_ref, x)
        for y in range(span_y):
            for e, piece in enumerate(shifted_tiles(ref[at, y])):
                base = x * group + e * channels
                shifted[base : base + channels, y * span_z : (y + 1) * span_z] = piece

    def lanes(y):
        return slice(y * span_z, (y + 1) * span_z)

    put(0)
    put(1)
    total = jnp.zeros(total_ref.shape, F32)
    for x in range(0, span_x + 2, step):
        layers = range(x, x + step)
        for k in layers:
            put(k + 2)
        wide = jnp.concatenate(
            [
                jnp.concatenate(
                    [shifted[k * group : (k + 3) * group, lanes(2 * p + c)] for k in layers for p in range(pairs)],
                    axis=1,
                )
                for c in range(4)
            ],
            axis=0,
        )
        part = jnp.dot(kernel_ref[...], wide, preferred_element_type=F32)
        for k in layers:
            ref, at = layer_of(own_ref, before_ref, after_ref, k + 1)
            for y in range(2 * pairs):
                response = part[
                    (y % 2) * channels : (y % 2 + 1) * channels, lanes((k - x) * pairs + y // 2)
                ]
                base = ((k - x) * 2 * pairs + y) * channels
                latent[base : base + channels, :] = (
                    ref[at, y + 1].astype(F32) + gelu(response)
                ).astype(BF16)
        sampled = jnp.dot(latent[...], wz_ref[...], preferred_element_type=F32)
        for k in layers:
            for y in range(2 * pairs):
                row = k * (span_y + 2) + y + 2
                base = ((k - x) * 2 * pairs + y) * channels
                total += sampled[base : base + channels] * wxy_ref[row : row + 1, :]
    total_ref[...] = total


def outer_body(
    own_ref, before_ref, after_ref, partner_ref, cross_ref, corner_ref, kernel_ref, total_ref,
    pick_ref, wz_ref, wxy_ref, pre_ref, last_ref, first_ref, middle_ref,
    value_ref, feature_ref, shifted, latent,
):
    span_x, span_y, channels, span_z = own_ref.shape
    group = 3 * channels
    left_chip = lax.axis_index("slab") == 0

    def put(x):
        ref, at = layer_of(own_ref, before_ref, after_ref, x)
        far, near = layer_of(cross_ref, corner_ref, corner_ref.at[HALO:], x)
        for j in range(2):
            cross, partner = far[near, j].astype(F32), partner_ref[x, j].astype(F32)
            left = jnp.where(left_chip, cross, partner).astype(BF16)
            right = jnp.where(left_chip, partner, cross).astype(BF16)
            for side, column, tile in (
                (0, j, left),
                (0, j + HALO, ref[at, j]),
                (1, j, ref[at, span_y - HALO + j]),
                (1, j + HALO, right),
            ):
                for e, piece in enumerate(shifted_tiles(tile)):
                    rows = slice(x * group + e * channels, x * group + (e + 1) * channels)
                    shifted[column, rows, side * span_z : (side + 1) * span_z] = piece

    put(0)
    put(1)
    total = total_ref[...]
    for x in range(span_x + 2):
        put(x + 2)
        wide = jnp.concatenate([shifted[c, x * group : (x + 3) * group, :] for c in range(4)], axis=0)
        part = jnp.dot(kernel_ref[...], wide, preferred_element_type=F32)
        middle = slice((x + 1) * group + channels, (x + 1) * group + 2 * channels)
        for y in range(2):
            response = part[y * channels : (y + 1) * channels]
            tiles = (shifted[y + 1, middle, :].astype(F32) + gelu(response)).astype(BF16)
            for side in range(2):
                base = (side * 2 + y) * channels
                latent[base : base + channels, :] = tiles[:, side * span_z : (side + 1) * span_z]
        sampled = jnp.dot(latent[...], wz_ref[...], preferred_element_type=F32)
        for side in range(2):
            for y in range(2):
                base = (side * 2 + y) * channels
                row = x * (span_y + 2) + side * span_y + y
                total += sampled[base : base + channels] * wxy_ref[row : row + 1, :]
    feature = lax.dot_general(
        pick_ref[...], total.astype(BF16), (((1,), (1,)), ((), ())), preferred_element_type=F32
    ).astype(BF16)
    half = feature.shape[0] // 2
    for s in range(2):
        feature_ref[s] = feature[s * half : (s + 1) * half]
    network(1 - own_section(), feature_ref, pre_ref, first_ref, middle_ref, last_ref, value_ref)


def own_section():
    return lax.axis_index("sect") // (lax.axis_size("sect") // 2)


def network(s, feature_ref, pre_ref, first_ref, middle_ref, last_ref, value_ref):
    channels = feature_ref.shape[2]
    act = gelu(
        jnp.dot(feature_ref[s], first_ref[s, :channels], preferred_element_type=F32) + pre_ref[s]
    ).astype(BF16)
    for i in range(middle_ref.shape[1]):
        act = gelu(jnp.dot(act, middle_ref[s, i], preferred_element_type=F32)).astype(BF16)
    value_ref[...] = lax.dot_general(
        last_ref[s], act, (((1,), (1,)), ((), ())), preferred_element_type=F32
    )


def own_body(*refs):
    network(own_section(), *refs)


def shift(array, axes, step):
    size = lax.axis_size(axes)
    pairs = [(i, i + step) for i in range(size) if 0 <= i + step < size]
    return lax.ppermute(array, axes, pairs)


def by_source(kept, got, bit, dim):
    first = jnp.where(bit == 0, kept, got)
    return jnp.stack([first, jnp.where(bit == 0, got, kept)], axis=dim)


def trade(blocks, axis, step, dim):
    bit = (lax.axis_index(axis) // step) % 2
    sent = lax.dynamic_index_in_dim(blocks, 1 - bit, dim, False)
    kept = lax.dynamic_index_in_dim(blocks, bit, dim, False)
    return by_source(kept, swap(sent, axis, step), bit, dim)


def swap(array, axis, step):
    return lax.ppermute(array, axis, [(i, i ^ step) for i in range(lax.axis_size(axis))])


def on_device(
    geometry,
    conv_kernels,
    point_place,
    point_attr,
    destination,
    dense_first,
    dense_middle,
    dense_last,
):
    channels, span_x, span_y, span_z = geometry.shape
    count = point_place.shape[1]
    hidden = dense_first.shape[2]
    bricks, sects = lax.axis_size("brick"), lax.axis_size("sect")
    capacity = 5 * count // (4 * bricks * sects)
    slots = bricks * sects * capacity
    outputs = dense_last.shape[1]
    lines = ("sect", "slab")
    width = lax.axis_size(lines)

    def block(*shape):
        return jax.ShapeDtypeStruct(shape, BF16)

    own, up, down, facing = call(
        columns_body,
        [
            block(span_x, span_y, channels, span_z),
            block(HALO, span_y, channels, span_z),
            block(HALO, span_y, channels, span_z),
            block(span_x, HALO, channels, span_z),
        ],
        [],
        8,
    )(geometry)
    inward = [(i, i + 1) for i in range(1, width - 1, 2)]
    inward = inward + [(j, i) for i, j in inward]
    before = shift(up, "brick", 1)
    after = shift(down, "brick", -1)
    cross = lax.ppermute(facing, lines, inward)
    pick, wz, wxy, pre, kernel, middle = call(
        make_points_body(span_x, span_y, bricks, sects, capacity),
        [
            block(slots, count),
            block(span_z, count),
            jax.ShapeDtypeStruct(((span_x + 2) * (span_y + 2), count), F32),
            jax.ShapeDtypeStruct((2, slots // 2, hidden), F32),
            block(2 * channels, 36 * channels),
            block(*dense_middle.shape),
        ],
        [pltpu.SemaphoreType.DMA],
        16,
        n_hbm=1,
    )(point_place, destination.reshape(1, count), point_attr.T, dense_first, conv_kernels[0], dense_middle)
    to_partner, to_cross = call(
        edges_body,
        [
            block(span_x + 2 * HALO, HALO, channels, span_z),
            block(2 * HALO, HALO, channels, span_z),
        ],
        [],
        4,
    )(own, before, after, wxy)
    partner = lax.ppermute(to_partner, lines, [(i, i ^ 1) for i in range(width)])
    corner = lax.ppermute(to_cross, lines, inward)
    rows = (span_x + 2 * HALO) * 3 * channels
    total = call(
        inner_body,
        jax.ShapeDtypeStruct((channels, count), F32),
        [
            pltpu.VMEM((rows, span_y * span_z), BF16),
            pltpu.VMEM((2 * (span_y - 2) * channels, span_z), BF16),
        ],
        10,
    )(own, before, after, kernel, wz, wxy)
    value = jax.ShapeDtypeStruct((outputs, slots // 2), F32)
    sent, feature = call(
        outer_body,
        [value, block(2, slots // 2, channels)],
        [
            pltpu.VMEM((4, rows, 2 * span_z), BF16),
            pltpu.VMEM((4 * channels, span_z), BF16),
        ],
        12,
    )(own, before, after, partner, cross, corner, kernel, total, pick, wz, wxy, pre, dense_last,
      dense_first, middle)
    got = swap(sent, "sect", sects // 2)
    kept = call(own_body, value, [], 8)(feature, pre, dense_first, middle, dense_last)
    value = by_source(kept, got, own_section(), 1)
    bits = [("sect", 1 << i) for i in reversed(range(sects.bit_length() - 2))]
    bits += [("brick", 1 << i) for i in reversed(range(bricks.bit_length() - 1))]
    value = value.reshape((outputs, 2) + (2,) * len(bits) + (capacity,))
    for i, (axis, step) in enumerate(bits):
        value = trade(value, axis, step, i + 2)
    value = value.reshape(outputs, sects, bricks, capacity)
    return value.transpose(0, 2, 1, 3).reshape(outputs, slots)


def solution(mesh):
    in_specs = (
        P(None, ("case", "brick"), ("sect", "slab"), None),
        P(),
        P(None, ("case", "brick", "sect", "slab")),
        P(("case", "brick", "sect", "slab"), None),
        P(("case", "brick", "sect", "slab"), None),
        P(),
        P(),
        P(),
    )
    out_specs = P(None, ("case", "brick", "sect", "slab"))
    return jax.shard_map(on_device, mesh=mesh, in_specs=in_specs, out_specs=out_specs, check_vma=False)
```

```python
import jax
import jax.numpy as jnp
from jax import lax
from jax.experimental import pallas as pl
from jax.experimental.pallas import tpu as pltpu
from jax.sharding import PartitionSpec as P


F32 = jnp.float32
BF16 = jnp.bfloat16
HALO = 2


def hat(offset):
    return jnp.maximum(0.0, 1.0 - jnp.abs(offset))


def gelu(value):
    half = 0.5 * value
    slope = 0.7978845608028654
    return half + half * jnp.tanh(value * (slope + (slope * 0.044715) * (value * value)))


def iota(shape, axis):
    return lax.broadcasted_iota(jnp.int32, shape, axis)


def call(body, outs, scratch, mib, n_hbm=0):
    def run(*args):
        spaces = [pltpu.VMEM] * (len(args) - n_hbm) + [pltpu.HBM] * n_hbm
        args = [pltpu.with_memory_space_constraint(a, s) if s == pltpu.HBM else a for a, s in zip(args, spaces)]
        return pl.pallas_call(
            body,
            out_shape=outs,
            in_specs=[pl.BlockSpec(memory_space=s) for s in spaces],
            out_specs=jax.tree.map(lambda _: pl.BlockSpec(memory_space=pltpu.VMEM), outs),
            scratch_shapes=scratch,
            compiler_params=pltpu.CompilerParams(vmem_limit_bytes=mib << 20),
        )(*args)

    return run


def columns_body(g_ref, own_ref, even_ref, odd_ref, cross_ref):
    span_x, span_y = g_ref.shape[1:3]
    parity, slab = lax.axis_index("brick") % 2, lax.axis_index("slab")
    for x in range(span_x):
        own_ref[x] = jnp.swapaxes(g_ref[:, x].astype(F32), 0, 1).astype(BF16)
    for side in range(2):

        @pl.when(parity == side)
        def _(up=(even_ref, odd_ref)[side], down=(odd_ref, even_ref)[side]):
            up[...] = own_ref[span_x - HALO :]
            down[...] = own_ref[:HALO]

        @pl.when(slab == side)
        def _(side=side):
            cross_ref[...] = own_ref[:, span_y - HALO :] if side else own_ref[:, :HALO]


def edges_body(own_ref, even_ref, odd_ref, _, before_ref, after_ref, partner_ref, cross_ref):
    span_x, span_y = own_ref.shape[:2]
    for side in range(2):

        @pl.when(lax.axis_index("brick") % 2 == side)
        def _(before=(odd_ref, even_ref)[side], after=(even_ref, odd_ref)[side]):
            before_ref[...] = before[...]
            after_ref[...] = after[...]

    for slab in range(2):

        @pl.when(lax.axis_index("slab") == slab)
        def _(slab=slab):
            near, far = slice(0, HALO), slice(span_y - HALO, span_y)
            facing, outward = (near, far) if slab else (far, near)
            partner_ref[:HALO] = before_ref[:, facing]
            partner_ref[HALO : HALO + span_x] = own_ref[:, facing]
            partner_ref[HALO + span_x :] = after_ref[:, facing]
            cross_ref[:HALO] = before_ref[:, outward]
            cross_ref[HALO:] = after_ref[:, outward]


def make_points_body(span_x, span_y, bricks, sects, capacity):
    def body(
        place_hbm, dest_hbm, conv_hbm, attr_hbm, first_hbm, middle_hbm, last_hbm,
        pick_ref, wz_ref, wxy_ref, kernel_ref, attr_ref, first_ref, middle_ref, last_ref,
        place_ref, dest_ref, conv_ref, sems,
    ):
        sources = (place_hbm, dest_hbm, conv_hbm, attr_hbm, first_hbm, middle_hbm, last_hbm)
        targets = (place_ref, dest_ref, conv_ref, attr_ref, first_ref, middle_ref, last_ref)
        copies = [
            pltpu.make_async_copy(source, target, sems.at[i])
            for i, (source, target) in enumerate(zip(sources, targets))
        ]
        for copy in copies:
            copy.start()
        copies[0].wait()
        count = place_ref.shape[1]
        span_z = wz_ref.shape[0]
        slots = pick_ref.shape[0]
        brick, line = lax.axis_index("brick"), lax.axis_index(("sect", "slab"))
        last_brick, last_line = lax.axis_size("brick") - 1, lax.axis_size(("sect", "slab")) - 1
        local_x = place_ref[0:1, :] * span_x
        local_y = place_ref[1:2, :] * span_y
        local_z = place_ref[2:3, :] * span_z
        cell_z = iota((span_z, count), 0).astype(F32) + 0.5
        wz_ref[...] = hat(local_z - cell_z).astype(BF16)
        weight_y = []
        for y in range(span_y + 2):
            w = hat(local_y - (y - 0.5))
            if y == 0:
                w = jnp.where(line > 0, w, 0.0)
            if y == span_y + 1:
                w = jnp.where(line < last_line, w, 0.0)
            weight_y.append(w)
        for x in range(span_x + 2):
            w = hat(local_x - (x - 0.5))
            if x == 0:
                w = jnp.where(brick > 0, w, 0.0)
            if x == span_x + 1:
                w = jnp.where(brick < last_brick, w, 0.0)
            for y in range(span_y + 2):
                row = x * (span_y + 2) + y
                wxy_ref[row : row + 1, :] = w * weight_y[y]
        copies[1].wait()
        row = dest_ref[...].astype(F32)
        earlier, later = iota((count, count), 0), iota((count, count), 1)
        diagonal = jnp.where(earlier == later, jnp.broadcast_to(row, (count, count)), 0.0)
        along = jnp.sum(diagonal, axis=1, keepdims=True)
        same = jnp.where((along == row) & (earlier < later), 1.0, 0.0)
        arrival = jnp.sum(same, axis=0, keepdims=True).astype(jnp.int32)
        target = row.astype(jnp.int32)
        slot = ((target % sects) * bricks + target // sects) * capacity + arrival
        pick = jnp.where(iota((slots, count), 0) == slot, 1.0, 0.0).astype(BF16)
        pick_ref[...] = pick
        copies[2].wait()
        channels = conv_ref.shape[-1]
        group = 9 * channels
        kernel_ref[:channels, 3 * group :] = jnp.zeros((channels, group), BF16)
        kernel_ref[channels:, :group] = jnp.zeros((channels, group), BF16)
        for a in range(3):
            for b in range(3):
                for e in range(3):
                    tile = conv_ref[a, b, e].astype(F32).T.astype(BF16)
                    for j in range(2):
                        lanes = (j + b) * group + (a * 3 + e) * channels
                        kernel_ref[j * channels : (j + 1) * channels, lanes : lanes + channels] = tile
        for copy in copies[3:]:
            copy.wait()

    return body


def shifted_tiles(tile):
    span_z = tile.shape[1]
    lane = iota(tile.shape, 1)
    wide = tile.astype(F32)
    lower = jnp.where(lane == 0, 0.0, pltpu.roll(wide, 1, 1)).astype(BF16)
    upper = jnp.where(lane == span_z - 1, 0.0, pltpu.roll(wide, span_z - 1, 1)).astype(BF16)
    return lower, tile, upper


def layer_of(own_ref, before_ref, after_ref, x):
    span_x = own_ref.shape[0]
    if x < HALO:
        return before_ref, x
    if x >= HALO + span_x:
        return after_ref, x - HALO - span_x
    return own_ref, x - HALO


def inner_body(
    own_ref, before_ref, after_ref, kernel_ref, wz_ref, wxy_ref, total_ref, shifted, latent
):
    span_x, span_y, channels, span_z = own_ref.shape
    group, pairs, step = 3 * channels, (span_y - 2) // 2, 2

    def put(x):
        ref, at = layer_of(own_ref, before_ref, after_ref, x)
        for y in range(span_y):
            for e, piece in enumerate(shifted_tiles(ref[at, y])):
                base = x * group + e * channels
                shifted[base : base + channels, y * span_z : (y + 1) * span_z] = piece

    def lanes(y):
        return slice(y * span_z, (y + 1) * span_z)

    put(0)
    put(1)
    total = jnp.zeros(total_ref.shape, F32)
    for x in range(0, span_x + 2, step):
        layers = range(x, x + step)
        for k in layers:
            put(k + 2)
        wide = jnp.concatenate(
            [
                jnp.concatenate(
                    [shifted[k * group : (k + 3) * group, lanes(2 * p + c)] for k in layers for p in range(pairs)],
                    axis=1,
                )
                for c in range(4)
            ],
            axis=0,
        )
        part = jnp.dot(kernel_ref[...], wide, preferred_element_type=F32)
        for k in layers:
            ref, at = layer_of(own_ref, before_ref, after_ref, k + 1)
            for y in range(2 * pairs):
                response = part[
                    (y % 2) * channels : (y % 2 + 1) * channels, lanes((k - x) * pairs + y // 2)
                ]
                base = ((k - x) * 2 * pairs + y) * channels
                latent[base : base + channels, :] = (
                    ref[at, y + 1].astype(F32) + gelu(response)
                ).astype(BF16)
        sampled = jnp.dot(latent[...], wz_ref[...], preferred_element_type=F32)
        for k in layers:
            for y in range(2 * pairs):
                row = k * (span_y + 2) + y + 2
                base = ((k - x) * 2 * pairs + y) * channels
                total += sampled[base : base + channels] * wxy_ref[row : row + 1, :]
    total_ref[...] = total


def outer_body(
    own_ref, before_ref, after_ref, partner_ref, cross_ref, corner_ref, kernel_ref, total_ref,
    pick_ref, wz_ref, wxy_ref, attr_ref, first_ref, middle_ref, last_ref,
    value_ref, row_ref, shifted, latent,
):
    span_x, span_y, channels, span_z = own_ref.shape
    group = 3 * channels
    left_chip = lax.axis_index("slab") == 0

    def put(x):
        ref, at = layer_of(own_ref, before_ref, after_ref, x)
        far, near = layer_of(cross_ref, corner_ref, corner_ref.at[HALO:], x)
        for j in range(2):
            cross, partner = far[near, j].astype(F32), partner_ref[x, j].astype(F32)
            left = jnp.where(left_chip, cross, partner).astype(BF16)
            right = jnp.where(left_chip, partner, cross).astype(BF16)
            for side, column, tile in (
                (0, j, left),
                (0, j + HALO, ref[at, j]),
                (1, j, ref[at, span_y - HALO + j]),
                (1, j + HALO, right),
            ):
                for e, piece in enumerate(shifted_tiles(tile)):
                    rows = slice(x * group + e * channels, x * group + (e + 1) * channels)
                    shifted[column, rows, side * span_z : (side + 1) * span_z] = piece

    put(0)
    put(1)
    total = total_ref[...]
    for x in range(span_x + 2):
        put(x + 2)
        wide = jnp.concatenate([shifted[c, x * group : (x + 3) * group, :] for c in range(4)], axis=0)
        part = jnp.dot(kernel_ref[...], wide, preferred_element_type=F32)
        middle = slice((x + 1) * group + channels, (x + 1) * group + 2 * channels)
        for y in range(2):
            response = part[y * channels : (y + 1) * channels]
            tiles = (shifted[y + 1, middle, :].astype(F32) + gelu(response)).astype(BF16)
            for side in range(2):
                base = (side * 2 + y) * channels
                latent[base : base + channels, :] = tiles[:, side * span_z : (side + 1) * span_z]
        sampled = jnp.dot(latent[...], wz_ref[...], preferred_element_type=F32)
        for side in range(2):
            for y in range(2):
                base = (side * 2 + y) * channels
                row = x * (span_y + 2) + side * span_y + y
                total += sampled[base : base + channels] * wxy_ref[row : row + 1, :]
    table = jnp.concatenate([total.astype(BF16), attr_ref[...]], axis=0)
    row = lax.dot_general(
        pick_ref[...], table, (((1,), (1,)), ((), ())), preferred_element_type=F32
    ).astype(BF16)
    half = row.shape[0] // 2
    for s in range(2):
        row_ref[s] = row[s * half : (s + 1) * half]
    network(1 - own_section(), row_ref, first_ref, middle_ref, last_ref, value_ref)


def own_section():
    return lax.axis_index("sect") // (lax.axis_size("sect") // 2)


def own_place():
    return (
        lax.axis_index("sect") % (lax.axis_size("sect") // 2) * lax.axis_size("brick")
        + lax.axis_index("brick")
    )


def network(s, row_ref, first_ref, middle_ref, last_ref, value_ref):
    act = gelu(jnp.dot(row_ref[s], first_ref[s], preferred_element_type=F32)).astype(BF16)
    for i in range(middle_ref.shape[1]):
        act = gelu(jnp.dot(act, middle_ref[s, i], preferred_element_type=F32)).astype(BF16)
    value = lax.dot_general(
        last_ref[s], act, (((1,), (1,)), ((), ())), preferred_element_type=F32
    )
    blocks, _, capacity = value_ref.shape
    place = own_place()
    for q in range(blocks):
        value_ref[q ^ place] = value[:, q * capacity : (q + 1) * capacity]


def own_body(*refs):
    network(own_section(), *refs)


def make_deal_body(sent, kept):
    def body(kept_ref, got_ref, sent_out, kept_out):
        for out, blocks in ((sent_out, sent), (kept_out, kept)):
            for i, (which, at) in enumerate(blocks):
                out[i] = (kept_ref, got_ref)[which][at]

    return body


def make_collect_body(order, bricks, sects):
    def body(kept_ref, got_ref, out_ref, blocks):
        for r, (which, at) in enumerate(order):
            blocks[r] = (kept_ref, got_ref)[which][at]
        capacity = kept_ref.shape[2]
        me = own_section() * (bricks * sects // 2) + own_place()
        for brick in range(bricks):
            for sect in range(sects):
                lane = (brick * sects + sect) * capacity
                out_ref[:, lane : lane + capacity] = blocks[(sect * bricks + brick) ^ me]

    return body


def swap(array, axis, step):
    return lax.ppermute(array, axis, [(i, i ^ step) for i in range(lax.axis_size(axis))])


def swap_pairs(array, axis, start):
    pairs = [(i, i + 1) for i in range(start, lax.axis_size(axis) - 1, 2)]
    return lax.ppermute(array, axis, pairs + [(j, i) for i, j in pairs])


def on_device(
    geometry,
    conv_kernels,
    point_place,
    point_attr,
    destination,
    dense_first,
    dense_middle,
    dense_last,
):
    channels, span_x, span_y, span_z = geometry.shape
    count = point_place.shape[1]
    bricks, sects = lax.axis_size("brick"), lax.axis_size("sect")
    capacity = 5 * count // (4 * bricks * sects)
    slots = bricks * sects * capacity
    outputs = dense_last.shape[1]
    lines = ("sect", "slab")

    def block(*shape):
        return jax.ShapeDtypeStruct(shape, BF16)

    own, even, odd, facing = call(
        columns_body,
        [
            block(span_x, span_y, channels, span_z),
            block(HALO, span_y, channels, span_z),
            block(HALO, span_y, channels, span_z),
            block(span_x, HALO, channels, span_z),
        ],
        [],
        8,
    )(geometry)
    even = swap_pairs(even, "brick", 0)
    odd = swap_pairs(odd, "brick", 1)
    cross = swap_pairs(facing, lines, 1)
    pick, wz, wxy, kernel, attr, first, middle, last = call(
        make_points_body(span_x, span_y, bricks, sects, capacity),
        [
            block(slots, count),
            block(span_z, count),
            jax.ShapeDtypeStruct(((span_x + 2) * (span_y + 2), count), F32),
            block(2 * channels, 36 * channels),
            block(point_attr.shape[1], count),
            block(*dense_first.shape),
            block(*dense_middle.shape),
            block(*dense_last.shape),
        ],
        [
            pltpu.VMEM(point_place.shape, F32),
            pltpu.VMEM((1, count), jnp.int32),
            pltpu.VMEM(conv_kernels.shape[1:], BF16),
            pltpu.SemaphoreType.DMA((7,)),
        ],
        12,
        n_hbm=7,
    )(point_place, destination.reshape(1, count), conv_kernels[0], point_attr.T, dense_first,
      dense_middle, dense_last)
    before, after, to_partner, to_cross = call(
        edges_body,
        [
            block(HALO, span_y, channels, span_z),
            block(HALO, span_y, channels, span_z),
            block(span_x + 2 * HALO, HALO, channels, span_z),
            block(2 * HALO, HALO, channels, span_z),
        ],
        [],
        4,
    )(own, even, odd, wxy)
    partner = swap(to_partner, "slab", 1)
    corner = swap_pairs(to_cross, lines, 1)
    rows = (span_x + 2 * HALO) * 3 * channels
    total = call(
        inner_body,
        jax.ShapeDtypeStruct((channels, count), F32),
        [
            pltpu.VMEM((rows, span_y * span_z), BF16),
            pltpu.VMEM((2 * (span_y - 2) * channels, span_z), BF16),
        ],
        10,
    )(own, before, after, kernel, wz, wxy)
    blocks = bricks * sects // 2

    def values(number):
        return jax.ShapeDtypeStruct((number, outputs, capacity), F32)

    sent, table = call(
        outer_body,
        [values(blocks), block(2, slots // 2, point_attr.shape[1] + channels)],
        [
            pltpu.VMEM((4, rows, 2 * span_z), BF16),
            pltpu.VMEM((4 * channels, span_z), BF16),
        ],
        12,
    )(own, before, after, partner, cross, corner, kernel, total, pick, wz, wxy, attr, first, middle,
      last)
    got = swap(sent, "sect", sects // 2)
    kept = call(own_body, values(blocks), [], 8)(table, first, middle, last)
    labels = [list(range(blocks)), [blocks + q for q in range(blocks)]]
    step = blocks // 2
    while step:
        found = [(label, w, i) for w in range(2) for i, label in enumerate(labels[w])]
        leaving = [f for f in found if f[0] & step]
        staying = [f for f in found if not f[0] & step]
        sent, kept = call(
            make_deal_body([f[1:] for f in leaving], [f[1:] for f in staying]), [values(blocks)] * 2, [], 2
        )(kept, got)
        axis, distance = ("brick", step) if step < bricks else ("sect", step // bricks)
        got = swap(sent, axis, distance)
        labels = [[f[0] for f in staying], [f[0] for f in leaving]]
        step //= 2
    order = {label: (w, i) for w in range(2) for i, label in enumerate(labels[w])}
    return call(
        make_collect_body([order[r] for r in range(2 * blocks)], bricks, sects),
        jax.ShapeDtypeStruct((outputs, slots), F32),
        [pltpu.VMEM((2 * blocks, outputs, capacity), F32)],
        2,
    )(kept, got)


def solution(mesh):
    in_specs = (
        P(None, ("case", "brick"), ("sect", "slab"), None),
        P(),
        P(None, ("case", "brick", "sect", "slab")),
        P(("case", "brick", "sect", "slab"), None),
        P(("case", "brick", "sect", "slab"), None),
        P(),
        P(),
        P(),
    )
    out_specs = P(None, ("case", "brick", "sect", "slab"))
    return jax.shard_map(on_device, mesh=mesh, in_specs=in_specs, out_specs=out_specs, check_vma=False)
```

```python
import jax
import jax.numpy as jnp
import numpy as np
from jax import lax
from jax.experimental import pallas as pl
from jax.experimental.pallas import tpu as pltpu
from jax.sharding import PartitionSpec as P


F32 = jnp.float32
BF16 = jnp.bfloat16
HALO = 2


def hat(offset):
    return jnp.maximum(0.0, 1.0 - jnp.abs(offset))


def gelu(value):
    half = 0.5 * value
    slope = 0.7978845608028654
    return half + half * jnp.tanh(value * (slope + (slope * 0.044715) * (value * value)))


def iota(shape, axis):
    return lax.broadcasted_iota(jnp.int32, shape, axis)


def call(body, outs, scratch, mib, n_hbm=0):
    def run(*args):
        spaces = [pltpu.VMEM] * (len(args) - n_hbm) + [pltpu.HBM] * n_hbm
        args = [pltpu.with_memory_space_constraint(a, s) if s == pltpu.HBM else a for a, s in zip(args, spaces)]
        return pl.pallas_call(
            body,
            out_shape=outs,
            in_specs=[pl.BlockSpec(memory_space=s) for s in spaces],
            out_specs=jax.tree.map(lambda _: pl.BlockSpec(memory_space=pltpu.VMEM), outs),
            scratch_shapes=scratch,
            compiler_params=pltpu.CompilerParams(vmem_limit_bytes=mib << 20),
        )(*args)

    return run


def columns_body(g_ref, own_ref, even_ref, odd_ref, cross_ref):
    span_x, span_y = g_ref.shape[1:3]
    parity, slab = lax.axis_index("brick") % 2, lax.axis_index("slab")
    for x in range(span_x):
        own_ref[x] = jnp.swapaxes(g_ref[:, x].astype(F32), 0, 1).astype(BF16)
    for side in range(2):

        @pl.when(parity == side)
        def _(up=(even_ref, odd_ref)[side], down=(odd_ref, even_ref)[side]):
            up[...] = own_ref[span_x - HALO :]
            down[...] = own_ref[:HALO]

        @pl.when(slab == side)
        def _(side=side):
            cross_ref[...] = own_ref[:, span_y - HALO :] if side else own_ref[:, :HALO]


def edges_body(own_ref, even_ref, odd_ref, _, before_ref, after_ref, partner_ref, cross_ref):
    span_x, span_y = own_ref.shape[:2]
    for side in range(2):

        @pl.when(lax.axis_index("brick") % 2 == side)
        def _(before=(odd_ref, even_ref)[side], after=(even_ref, odd_ref)[side]):
            brick = lax.axis_index("brick")
            outside = jnp.zeros(before_ref.shape, F32)
            inside = before[...].astype(F32)
            before_ref[...] = jnp.where(brick > 0, inside, outside).astype(BF16)
            inside = after[...].astype(F32)
            after_ref[...] = jnp.where(brick < lax.axis_size("brick") - 1, inside, outside).astype(BF16)

    for slab in range(2):

        @pl.when(lax.axis_index("slab") == slab)
        def _(slab=slab):
            near, far = slice(0, HALO), slice(span_y - HALO, span_y)
            facing, outward = (near, far) if slab else (far, near)
            partner_ref[:HALO] = before_ref[:, facing]
            partner_ref[HALO : HALO + span_x] = own_ref[:, facing]
            partner_ref[HALO + span_x :] = after_ref[:, facing]
            cross_ref[:HALO] = before_ref[:, outward]
            cross_ref[HALO:] = after_ref[:, outward]


def make_points_body(span_x, span_y, bricks, sects, capacity):
    def body(
        place_hbm, dest_hbm, conv_hbm, attr_hbm, first_hbm, middle_hbm, last_hbm,
        pick_ref, wz_ref, wxy_ref, kernel_ref, attr_ref, first_ref, middle_ref, last_ref,
        place_ref, dest_ref, conv_ref, sems,
    ):
        sources = (place_hbm, dest_hbm, conv_hbm, attr_hbm, first_hbm, middle_hbm, last_hbm)
        targets = (place_ref, dest_ref, conv_ref, attr_ref, first_ref, middle_ref, last_ref)
        copies = [
            pltpu.make_async_copy(source, target, sems.at[i])
            for i, (source, target) in enumerate(zip(sources, targets))
        ]
        for copy in copies:
            copy.start()
        copies[0].wait()
        count = place_ref.shape[1]
        span_z = wz_ref.shape[0]
        slots = pick_ref.shape[0]
        brick, line = lax.axis_index("brick"), lax.axis_index(("sect", "slab"))
        last_brick, last_line = lax.axis_size("brick") - 1, lax.axis_size(("sect", "slab")) - 1
        local_x = place_ref[0:1, :] * span_x
        local_y = place_ref[1:2, :] * span_y
        local_z = place_ref[2:3, :] * span_z
        cell_z = iota((span_z, count), 0).astype(F32) + 0.5
        wz_ref[...] = hat(local_z - cell_z).astype(BF16)
        weight_y = []
        for y in range(span_y + 2):
            w = hat(local_y - (y - 0.5))
            if y == 0:
                w = jnp.where(line > 0, w, 0.0)
            if y == span_y + 1:
                w = jnp.where(line < last_line, w, 0.0)
            weight_y.append(w)
        for x in range(span_x + 2):
            w = hat(local_x - (x - 0.5))
            if x == 0:
                w = jnp.where(brick > 0, w, 0.0)
            if x == span_x + 1:
                w = jnp.where(brick < last_brick, w, 0.0)
            for y in range(span_y + 2):
                row = x * (span_y + 2) + y
                wxy_ref[row : row + 1, :] = w * weight_y[y]
        copies[1].wait()
        row = dest_ref[...].astype(F32)
        earlier, later = iota((count, count), 0), iota((count, count), 1)
        diagonal = jnp.where(earlier == later, jnp.broadcast_to(row, (count, count)), 0.0)
        along = jnp.sum(diagonal, axis=1, keepdims=True)
        same = jnp.where((along == row) & (earlier < later), 1.0, 0.0)
        arrival = jnp.sum(same, axis=0, keepdims=True).astype(jnp.int32)
        target = row.astype(jnp.int32)
        slot = ((target % sects) * bricks + target // sects) * capacity + arrival
        pick = jnp.where(iota((slots, count), 0) == slot, 1.0, 0.0).astype(BF16)
        pick_ref[...] = pick
        copies[2].wait()
        channels = conv_ref.shape[-1]
        group = 9 * channels
        kernel_ref[:channels, 3 * group :] = jnp.zeros((channels, group), BF16)
        kernel_ref[channels:, :group] = jnp.zeros((channels, group), BF16)
        for a in range(3):
            for b in range(3):
                for e in range(3):
                    tile = conv_ref[a, b, e].astype(F32).T.astype(BF16)
                    for j in range(2):
                        lanes = (j + b) * group + (a * 3 + e) * channels
                        kernel_ref[j * channels : (j + 1) * channels, lanes : lanes + channels] = tile
        for copy in copies[3:]:
            copy.wait()

    return body


def shifted_tiles(tile):
    span_z = tile.shape[1]
    lane = iota(tile.shape, 1)
    wide = tile.astype(F32)
    lower = jnp.where(lane == 0, 0.0, pltpu.roll(wide, 1, 1)).astype(BF16)
    upper = jnp.where(lane == span_z - 1, 0.0, pltpu.roll(wide, span_z - 1, 1)).astype(BF16)
    return lower, tile, upper


def layer_of(own_ref, before_ref, after_ref, x):
    span_x = own_ref.shape[0]
    if x < HALO:
        return before_ref, x
    if x >= HALO + span_x:
        return after_ref, x - HALO - span_x
    return own_ref, x - HALO


def inner_body(
    own_ref, before_ref, after_ref, kernel_ref, wz_ref, wxy_ref, total_ref, shifted, latent
):
    span_x, span_y, channels, span_z = own_ref.shape
    group, pairs, step = 3 * channels, (span_y - 2) // 2, 2

    def put(x):
        ref, at = layer_of(own_ref, before_ref, after_ref, x)
        for y in range(span_y):
            for e, piece in enumerate(shifted_tiles(ref[at, y])):
                base = x * group + e * channels
                shifted[base : base + channels, y * span_z : (y + 1) * span_z] = piece

    def lanes(y):
        return slice(y * span_z, (y + 1) * span_z)

    put(0)
    put(1)
    total = jnp.zeros(total_ref.shape, F32)
    for x in range(0, span_x + 2, step):
        layers = range(x, x + step)
        for k in layers:
            put(k + 2)
        wide = jnp.concatenate(
            [
                jnp.concatenate(
                    [shifted[k * group : (k + 3) * group, lanes(2 * p + c)] for k in layers for p in range(pairs)],
                    axis=1,
                )
                for c in range(4)
            ],
            axis=0,
        )
        part = jnp.dot(kernel_ref[...], wide, preferred_element_type=F32)
        for k in layers:
            ref, at = layer_of(own_ref, before_ref, after_ref, k + 1)
            for y in range(2 * pairs):
                response = part[
                    (y % 2) * channels : (y % 2 + 1) * channels, lanes((k - x) * pairs + y // 2)
                ]
                base = ((k - x) * 2 * pairs + y) * channels
                latent[base : base + channels, :] = (
                    ref[at, y + 1].astype(F32) + gelu(response)
                ).astype(BF16)
        sampled = jnp.dot(latent[...], wz_ref[...], preferred_element_type=F32)
        for k in layers:
            for y in range(2 * pairs):
                row = k * (span_y + 2) + y + 2
                base = ((k - x) * 2 * pairs + y) * channels
                total += sampled[base : base + channels] * wxy_ref[row : row + 1, :]
    total_ref[...] = total


def outer_body(
    own_ref, before_ref, after_ref, partner_ref, cross_ref, corner_ref, kernel_ref, total_ref,
    pick_ref, wz_ref, wxy_ref, attr_ref, first_ref, middle_ref, last_ref,
    value_ref, row_ref, shifted, latent,
):
    span_x, span_y, channels, span_z = own_ref.shape
    group = 3 * channels
    left_chip = lax.axis_index("slab") == 0
    line = lax.axis_index(("sect", "slab"))
    inside = (line > 0) & (line < lax.axis_size(("sect", "slab")) - 1)

    def put(x):
        ref, at = layer_of(own_ref, before_ref, after_ref, x)
        far, near = layer_of(cross_ref, corner_ref, corner_ref.at[HALO:], x)
        for j in range(2):
            cross, partner = far[near, j].astype(F32), partner_ref[x, j].astype(F32)
            cross = jnp.where(inside, cross, 0.0)
            left = jnp.where(left_chip, cross, partner).astype(BF16)
            right = jnp.where(left_chip, partner, cross).astype(BF16)
            for side, column, tile in (
                (0, j, left),
                (0, j + HALO, ref[at, j]),
                (1, j, ref[at, span_y - HALO + j]),
                (1, j + HALO, right),
            ):
                for e, piece in enumerate(shifted_tiles(tile)):
                    rows = slice(x * group + e * channels, x * group + (e + 1) * channels)
                    shifted[column, rows, side * span_z : (side + 1) * span_z] = piece

    put(0)
    put(1)
    total = total_ref[...]
    for x in range(span_x + 2):
        put(x + 2)
        wide = jnp.concatenate([shifted[c, x * group : (x + 3) * group, :] for c in range(4)], axis=0)
        part = jnp.dot(kernel_ref[...], wide, preferred_element_type=F32)
        middle = slice((x + 1) * group + channels, (x + 1) * group + 2 * channels)
        for y in range(2):
            response = part[y * channels : (y + 1) * channels]
            tiles = (shifted[y + 1, middle, :].astype(F32) + gelu(response)).astype(BF16)
            for side in range(2):
                base = (side * 2 + y) * channels
                latent[base : base + channels, :] = tiles[:, side * span_z : (side + 1) * span_z]
        sampled = jnp.dot(latent[...], wz_ref[...], preferred_element_type=F32)
        for side in range(2):
            for y in range(2):
                base = (side * 2 + y) * channels
                row = x * (span_y + 2) + side * span_y + y
                total += sampled[base : base + channels] * wxy_ref[row : row + 1, :]
    table = jnp.concatenate([total.astype(BF16), attr_ref[...]], axis=0)
    row = lax.dot_general(
        pick_ref[...], table, (((1,), (1,)), ((), ())), preferred_element_type=F32
    ).astype(BF16)
    half = row.shape[0] // 2
    for s in range(2):
        row_ref[s] = row[s * half : (s + 1) * half]
    network(1 - own_section(), row_ref, first_ref, middle_ref, last_ref, value_ref)


def own_section():
    return lax.axis_index("sect") // (lax.axis_size("sect") // 2)


def own_place():
    return (
        lax.axis_index("sect") % (lax.axis_size("sect") // 2) * lax.axis_size("brick")
        + lax.axis_index("brick")
    )


def network(s, row_ref, first_ref, middle_ref, last_ref, value_ref):
    act = gelu(jnp.dot(row_ref[s], first_ref[s], preferred_element_type=F32)).astype(BF16)
    for i in range(middle_ref.shape[1]):
        act = gelu(jnp.dot(act, middle_ref[s, i], preferred_element_type=F32)).astype(BF16)
    value = lax.dot_general(
        last_ref[s], act, (((1,), (1,)), ((), ())), preferred_element_type=F32
    )
    blocks, _, capacity = value_ref.shape
    place = own_place()
    for q in range(blocks):
        value_ref[q ^ place] = value[:, q * capacity : (q + 1) * capacity]


def own_body(*refs):
    network(own_section(), *refs)


def make_deal_body(sent, kept):
    def body(kept_ref, got_ref, sent_out, kept_out):
        for out, blocks in ((sent_out, sent), (kept_out, kept)):
            for i, (which, at) in enumerate(blocks):
                out[i] = (kept_ref, got_ref)[which][at]

    return body


def make_collect_body(order, bricks, sects):
    def body(kept_ref, got_ref, out_ref, blocks):
        for r, (which, at) in enumerate(order):
            blocks[r] = (kept_ref, got_ref)[which][at]
        capacity = kept_ref.shape[2]
        me = own_section() * (bricks * sects // 2) + own_place()
        for brick in range(bricks):
            for sect in range(sects):
                lane = (brick * sects + sect) * capacity
                out_ref[:, lane : lane + capacity] = blocks[(sect * bricks + brick) ^ me]

    return body


def swap(array, axis, step):
    return lax.ppermute(array, axis, [(i, i ^ step) for i in range(lax.axis_size(axis))])


def swap_pairs(array, axes, start, fill):
    everything = ("case", "brick", "sect", "slab")
    sizes = [lax.axis_size(a) for a in everything]
    pairs = []
    for i, at in enumerate(np.ndindex(*sizes)):
        at = dict(zip(everything, at))
        place, size = 0, 1
        for a in axes:
            place, size = place * lax.axis_size(a) + at[a], size * lax.axis_size(a)
        other = place + 1 if (place - start) % 2 == 0 else place - 1
        if 0 <= other < size:
            for a in reversed(axes):
                other, at[a] = divmod(other, lax.axis_size(a))
        else:
            at[fill] ^= 1
        pairs.append((i, int(np.ravel_multi_index([at[a] for a in everything], sizes))))
    return lax.ppermute(array, everything, pairs)


def on_device(
    geometry,
    conv_kernels,
    point_place,
    point_attr,
    destination,
    dense_first,
    dense_middle,
    dense_last,
):
    channels, span_x, span_y, span_z = geometry.shape
    count = point_place.shape[1]
    bricks, sects = lax.axis_size("brick"), lax.axis_size("sect")
    capacity = 5 * count // (4 * bricks * sects)
    slots = bricks * sects * capacity
    outputs = dense_last.shape[1]
    lines = ("sect", "slab")

    def block(*shape):
        return jax.ShapeDtypeStruct(shape, BF16)

    own, even, odd, facing = call(
        columns_body,
        [
            block(span_x, span_y, channels, span_z),
            block(HALO, span_y, channels, span_z),
            block(HALO, span_y, channels, span_z),
            block(span_x, HALO, channels, span_z),
        ],
        [],
        8,
    )(geometry)
    even = swap_pairs(even, ("brick",), 0, "slab")
    odd = swap_pairs(odd, ("brick",), 1, "slab")
    cross = swap_pairs(facing, lines, 1, "case")
    pick, wz, wxy, kernel, attr, first, middle, last = call(
        make_points_body(span_x, span_y, bricks, sects, capacity),
        [
            block(slots, count),
            block(span_z, count),
            jax.ShapeDtypeStruct(((span_x + 2) * (span_y + 2), count), F32),
            block(2 * channels, 36 * channels),
            block(point_attr.shape[1], count),
            block(*dense_first.shape),
            block(*dense_middle.shape),
            block(*dense_last.shape),
        ],
        [
            pltpu.VMEM(point_place.shape, F32),
            pltpu.VMEM((1, count), jnp.int32),
            pltpu.VMEM(conv_kernels.shape[1:], BF16),
            pltpu.SemaphoreType.DMA((7,)),
        ],
        12,
        n_hbm=7,
    )(point_place, destination.reshape(1, count), conv_kernels[0], point_attr.T, dense_first,
      dense_middle, dense_last)
    before, after, to_partner, to_cross = call(
        edges_body,
        [
            block(HALO, span_y, channels, span_z),
            block(HALO, span_y, channels, span_z),
            block(span_x + 2 * HALO, HALO, channels, span_z),
            block(2 * HALO, HALO, channels, span_z),
        ],
        [],
        4,
    )(own, even, odd, wxy)
    partner = swap(to_partner, "slab", 1)
    corner = swap_pairs(to_cross, lines, 1, "case")
    rows = (span_x + 2 * HALO) * 3 * channels
    total = call(
        inner_body,
        jax.ShapeDtypeStruct((channels, count), F32),
        [
            pltpu.VMEM((rows, span_y * span_z), BF16),
            pltpu.VMEM((2 * (span_y - 2) * channels, span_z), BF16),
        ],
        10,
    )(own, before, after, kernel, wz, wxy)
    blocks = bricks * sects // 2

    def values(number):
        return jax.ShapeDtypeStruct((number, outputs, capacity), F32)

    sent, table = call(
        outer_body,
        [values(blocks), block(2, slots // 2, point_attr.shape[1] + channels)],
        [
            pltpu.VMEM((4, rows, 2 * span_z), BF16),
            pltpu.VMEM((4 * channels, span_z), BF16),
        ],
        12,
    )(own, before, after, partner, cross, corner, kernel, total, pick, wz, wxy, attr, first, middle,
      last)
    got = swap(sent, "sect", sects // 2)
    kept = call(own_body, values(blocks), [], 8)(table, first, middle, last)
    labels = [list(range(blocks)), [blocks + q for q in range(blocks)]]
    step = blocks // 2
    while step:
        found = [(label, w, i) for w in range(2) for i, label in enumerate(labels[w])]
        leaving = [f for f in found if f[0] & step]
        staying = [f for f in found if not f[0] & step]
        sent, kept = call(
            make_deal_body([f[1:] for f in leaving], [f[1:] for f in staying]), [values(blocks)] * 2, [], 2
        )(kept, got)
        axis, distance = ("brick", step) if step < bricks else ("sect", step // bricks)
        got = swap(sent, axis, distance)
        labels = [[f[0] for f in staying], [f[0] for f in leaving]]
        step //= 2
    order = {label: (w, i) for w in range(2) for i, label in enumerate(labels[w])}
    return call(
        make_collect_body([order[r] for r in range(2 * blocks)], bricks, sects),
        jax.ShapeDtypeStruct((outputs, slots), F32),
        [pltpu.VMEM((2 * blocks, outputs, capacity), F32)],
        2,
    )(kept, got)


def solution(mesh):
    in_specs = (
        P(None, ("case", "brick"), ("sect", "slab"), None),
        P(),
        P(None, ("case", "brick", "sect", "slab")),
        P(("case", "brick", "sect", "slab"), None),
        P(("case", "brick", "sect", "slab"), None),
        P(),
        P(),
        P(),
    )
    out_specs = P(None, ("case", "brick", "sect", "slab"))
    return jax.shard_map(on_device, mesh=mesh, in_specs=in_specs, out_specs=out_specs, check_vma=False)
```

```python
import jax
import jax.numpy as jnp
import numpy as np
from jax import lax
from jax.experimental import pallas as pl
from jax.experimental.pallas import tpu as pltpu
from jax.sharding import PartitionSpec as P


F32 = jnp.float32
BF16 = jnp.bfloat16
HALO = 2


def hat(offset):
    return jnp.maximum(0.0, 1.0 - jnp.abs(offset))


def gelu(value):
    half = 0.5 * value
    slope = 0.7978845608028654
    return half + half * jnp.tanh(value * (slope + (slope * 0.044715) * (value * value)))


def iota(shape, axis):
    return lax.broadcasted_iota(jnp.int32, shape, axis)


def call(body, outs, scratch, mib, n_hbm=0):
    def run(*args):
        spaces = [pltpu.VMEM] * (len(args) - n_hbm) + [pltpu.HBM] * n_hbm
        args = [pltpu.with_memory_space_constraint(a, s) if s == pltpu.HBM else a for a, s in zip(args, spaces)]
        return pl.pallas_call(
            body,
            out_shape=outs,
            in_specs=[pl.BlockSpec(memory_space=s) for s in spaces],
            out_specs=jax.tree.map(lambda _: pl.BlockSpec(memory_space=pltpu.VMEM), outs),
            scratch_shapes=scratch,
            compiler_params=pltpu.CompilerParams(vmem_limit_bytes=mib << 20),
        )(*args)

    return run


def columns_body(g_ref, own_ref, even_ref, odd_ref, cross_ref):
    span_x, span_y = g_ref.shape[1:3]
    parity, slab = lax.axis_index("brick") % 2, lax.axis_index("slab")
    for x in range(span_x):
        own_ref[x] = jnp.swapaxes(g_ref[:, x].astype(F32), 0, 1).astype(BF16)
    for side in range(2):

        @pl.when(parity == side)
        def _(up=(even_ref, odd_ref)[side], down=(odd_ref, even_ref)[side]):
            up[...] = own_ref[span_x - HALO :]
            down[...] = own_ref[:HALO]

        @pl.when(slab == side)
        def _(side=side):
            cross_ref[...] = own_ref[:, span_y - HALO :] if side else own_ref[:, :HALO]


def edges_body(own_ref, even_ref, odd_ref, _, before_ref, after_ref, partner_ref, cross_ref):
    span_x, span_y = own_ref.shape[:2]
    for side in range(2):

        @pl.when(lax.axis_index("brick") % 2 == side)
        def _(before=(odd_ref, even_ref)[side], after=(even_ref, odd_ref)[side]):
            brick = lax.axis_index("brick")
            outside = jnp.zeros(before_ref.shape, F32)
            inside = before[...].astype(F32)
            before_ref[...] = jnp.where(brick > 0, inside, outside).astype(BF16)
            inside = after[...].astype(F32)
            after_ref[...] = jnp.where(brick < lax.axis_size("brick") - 1, inside, outside).astype(BF16)

    for slab in range(2):

        @pl.when(lax.axis_index("slab") == slab)
        def _(slab=slab):
            near, far = slice(0, HALO), slice(span_y - HALO, span_y)
            facing, outward = (near, far) if slab else (far, near)
            partner_ref[:HALO] = before_ref[:, facing]
            partner_ref[HALO : HALO + span_x] = own_ref[:, facing]
            partner_ref[HALO + span_x :] = after_ref[:, facing]
            cross_ref[:HALO] = before_ref[:, outward]
            cross_ref[HALO:] = after_ref[:, outward]


def make_points_body(span_x, span_y, bricks, sects, capacity):
    def body(
        place_hbm, dest_hbm, conv_hbm, attr_hbm, first_hbm, middle_hbm, last_hbm,
        pick_ref, wz_ref, wxy_ref, kernel_ref, attr_ref, first_ref, middle_ref, last_ref,
        place_ref, dest_ref, conv_ref, sems,
    ):
        sources = (place_hbm, dest_hbm, conv_hbm, attr_hbm, first_hbm, middle_hbm, last_hbm)
        targets = (place_ref, dest_ref, conv_ref, attr_ref, first_ref, middle_ref, last_ref)
        copies = [
            pltpu.make_async_copy(source, target, sems.at[i])
            for i, (source, target) in enumerate(zip(sources, targets))
        ]
        for copy in copies:
            copy.start()
        copies[0].wait()
        count = place_ref.shape[1]
        span_z = wz_ref.shape[0]
        slots = pick_ref.shape[0]
        brick, line = lax.axis_index("brick"), lax.axis_index(("sect", "slab"))
        last_brick, last_line = lax.axis_size("brick") - 1, lax.axis_size(("sect", "slab")) - 1
        local_x = place_ref[0:1, :] * span_x
        local_y = place_ref[1:2, :] * span_y
        local_z = place_ref[2:3, :] * span_z
        cell_z = iota((span_z, count), 0).astype(F32) + 0.5
        wz_ref[...] = hat(local_z - cell_z).astype(BF16)
        weight_y = []
        for y in range(span_y + 2):
            w = hat(local_y - (y - 0.5))
            if y == 0:
                w = jnp.where(line > 0, w, 0.0)
            if y == span_y + 1:
                w = jnp.where(line < last_line, w, 0.0)
            weight_y.append(w)
        for x in range(span_x + 2):
            w = hat(local_x - (x - 0.5))
            if x == 0:
                w = jnp.where(brick > 0, w, 0.0)
            if x == span_x + 1:
                w = jnp.where(brick < last_brick, w, 0.0)
            for y in range(span_y + 2):
                row = x * (span_y + 2) + y
                wxy_ref[row : row + 1, :] = w * weight_y[y]
        copies[1].wait()
        row = dest_ref[...].astype(F32)
        earlier, later = iota((count, count), 0), iota((count, count), 1)
        diagonal = jnp.where(earlier == later, jnp.broadcast_to(row, (count, count)), 0.0)
        along = jnp.sum(diagonal, axis=1, keepdims=True)
        same = jnp.where((along == row) & (earlier < later), 1.0, 0.0)
        arrival = jnp.sum(same, axis=0, keepdims=True).astype(jnp.int32)
        target = row.astype(jnp.int32)
        slot = ((target % sects) * bricks + target // sects) * capacity + arrival
        pick = jnp.where(iota((slots, count), 0) == slot, 1.0, 0.0).astype(BF16)
        pick_ref[...] = pick
        copies[2].wait()
        channels = conv_ref.shape[-1]
        group = 9 * channels
        kernel_ref[:channels, 3 * group :] = jnp.zeros((channels, group), BF16)
        kernel_ref[channels:, :group] = jnp.zeros((channels, group), BF16)
        for a in range(3):
            for b in range(3):
                for e in range(3):
                    tile = conv_ref[a, b, e].astype(F32).T.astype(BF16)
                    for j in range(2):
                        lanes = (j + b) * group + (a * 3 + e) * channels
                        kernel_ref[j * channels : (j + 1) * channels, lanes : lanes + channels] = tile
        for copy in copies[3:]:
            copy.wait()

    return body


def taps(tile, inside=True):
    span_z = tile.shape[1]
    lane = iota((1, span_z), 1)
    below, here, above = (
        jnp.where(keep & inside, 1.0, 0.0).astype(BF16)
        for keep in (lane > 0, lane >= 0, lane < span_z - 1)
    )
    pieces = (pltpu.roll(tile, 1, 1) * below, tile * here, pltpu.roll(tile, span_z - 1, 1) * above)
    return jnp.concatenate(pieces, axis=0)


def share(total, units, tap, weight, kernel_ref, wz_ref, wxy_ref):
    channels, span_z = total.shape[0], wz_ref.shape[0]
    for first in range(0, len(units), 4):
        pair = units[first : first + 4]
        wide = jnp.concatenate(
            [
                jnp.concatenate([tap(x + a, y + c) for x, y in pair], axis=1)
                for c in range(4)
                for a in range(3)
            ],
            axis=0,
        )
        part = jnp.dot(kernel_ref[...], wide, preferred_element_type=F32)
        tiles, weights = [], []
        for j in range(2):
            centre = jnp.concatenate(
                [tap(x + 1, y + j + 1)[channels : 2 * channels] for x, y in pair], axis=1
            )
            response = part[j * channels : (j + 1) * channels]
            latent = (centre.astype(F32) + gelu(response)).astype(BF16)
            for u, (x, y) in enumerate(pair):
                tiles.append(latent[:, u * span_z : (u + 1) * span_z])
                weights.append(weight(x, y + j))
        sampled = jnp.dot(
            jnp.concatenate(tiles, axis=0), wz_ref[...], preferred_element_type=F32
        )
        for k, w in enumerate(weights):
            total += sampled[k * channels : (k + 1) * channels] * wxy_ref[pl.ds(w, 1), :]
    return total


def inner_units(layers, span_y):
    return [(x, y) for x in layers for y in range(HALO, span_y, 2)]


def block_body(own_ref, kernel_ref, wz_ref, wxy_ref, taps_ref, total_ref):
    span_x, span_y = own_ref.shape[:2]
    for x in range(span_x):
        for y in range(span_y):
            taps_ref[x, y] = taps(own_ref[x, y])
    total_ref[...] = share(
        jnp.zeros(total_ref.shape, F32),
        inner_units(range(HALO, span_x), span_y),
        lambda x, y: taps_ref[x - HALO, y - HALO],
        lambda x, y: x * (span_y + 2) + y,
        kernel_ref, wz_ref, wxy_ref,
    )


def tap_of(own_ref, halo_ref, x):
    span_x = own_ref.shape[0]
    if HALO <= x < HALO + span_x:
        return own_ref.at[x - HALO]
    return halo_ref.at[x if x < HALO else x - span_x]


def inner_body(
    own_ref, before_ref, after_ref, kernel_ref, wz_ref, wxy_ref, start_ref, halo_ref, total_ref
):
    span_x, span_y = own_ref.shape[:2]
    for x in range(HALO):
        for y in range(span_y):
            halo_ref[x, y] = taps(before_ref[x, y])
            halo_ref[HALO + x, y] = taps(after_ref[x, y])
    total_ref[...] = share(
        start_ref[...],
        inner_units([*range(HALO), *range(span_x, span_x + 2)], span_y),
        lambda x, y: tap_of(own_ref, halo_ref, x)[y - HALO],
        lambda x, y: x * (span_y + 2) + y,
        kernel_ref, wz_ref, wxy_ref,
    )


def side_share(total, on_left, inside, halo_tile, own_ref, halo_ref, side_ref, kernel_ref, wz_ref, wxy_ref):
    span_x, span_y = own_ref.shape[:2]
    near = jnp.where(on_left, 0, span_y - HALO)
    for x in range(side_ref.shape[0]):
        layer = tap_of(own_ref, halo_ref, x)
        for j in range(HALO):
            side_ref[x, jnp.where(on_left, HALO, 0) + j] = layer[near + j]
            side_ref[x, jnp.where(on_left, 0, HALO) + j] = taps(halo_tile(x, j), inside)
    base = jnp.where(on_left, 0, span_y)
    return share(
        total,
        [(x, 0) for x in range(span_x + 2)],
        lambda x, y: side_ref[x, y],
        lambda x, y: x * (span_y + 2) + base + y,
        kernel_ref, wz_ref, wxy_ref,
    )


def partner_body(
    own_ref, halo_ref, partner_ref, kernel_ref, wz_ref, wxy_ref, start_ref, total_ref, side_ref
):
    total_ref[...] = side_share(
        start_ref[...], lax.axis_index("slab") == 1, True, lambda x, j: partner_ref[x, j],
        own_ref, halo_ref, side_ref, kernel_ref, wz_ref, wxy_ref,
    )


def outer_body(
    own_ref, halo_ref, cross_ref, corner_ref, kernel_ref, wz_ref, wxy_ref, start_ref,
    pick_ref, attr_ref, first_ref, middle_ref, last_ref,
    value_ref, row_ref, side_ref,
):
    line = lax.axis_index(("sect", "slab"))
    total = side_share(
        start_ref[...],
        lax.axis_index("slab") == 0,
        (line > 0) & (line < lax.axis_size(("sect", "slab")) - 1),
        lambda x, j: tap_of(cross_ref, corner_ref, x)[j],
        own_ref, halo_ref, side_ref, kernel_ref, wz_ref, wxy_ref,
    )
    table = jnp.concatenate([total.astype(BF16), attr_ref[...]], axis=0)
    row = lax.dot_general(
        pick_ref[...], table, (((1,), (1,)), ((), ())), preferred_element_type=F32
    ).astype(BF16)
    half = row.shape[0] // 2
    for s in range(2):
        row_ref[s] = row[s * half : (s + 1) * half]
    network(1 - own_section(), row_ref, first_ref, middle_ref, last_ref, value_ref)


def own_section():
    return lax.axis_index("sect") // (lax.axis_size("sect") // 2)


def own_place():
    return (
        lax.axis_index("sect") % (lax.axis_size("sect") // 2) * lax.axis_size("brick")
        + lax.axis_index("brick")
    )


def network(s, row_ref, first_ref, middle_ref, last_ref, value_ref):
    act = gelu(jnp.dot(row_ref[s], first_ref[s], preferred_element_type=F32)).astype(BF16)
    for i in range(middle_ref.shape[1]):
        act = gelu(jnp.dot(act, middle_ref[s, i], preferred_element_type=F32)).astype(BF16)
    value = lax.dot_general(
        last_ref[s], act, (((1,), (1,)), ((), ())), preferred_element_type=F32
    )
    blocks, _, capacity = value_ref.shape
    place = own_place()
    for q in range(blocks):
        value_ref[q ^ place] = value[:, q * capacity : (q + 1) * capacity]


def own_body(*refs):
    network(own_section(), *refs)


def make_deal_body(sent, kept):
    def body(kept_ref, got_ref, sent_out, kept_out):
        for out, blocks in ((sent_out, sent), (kept_out, kept)):
            for i, (which, at) in enumerate(blocks):
                out[i] = (kept_ref, got_ref)[which][at]

    return body


def make_collect_body(order, bricks, sects):
    def body(kept_ref, got_ref, out_ref, blocks):
        for r, (which, at) in enumerate(order):
            blocks[r] = (kept_ref, got_ref)[which][at]
        capacity = kept_ref.shape[2]
        me = own_section() * (bricks * sects // 2) + own_place()
        for brick in range(bricks):
            for sect in range(sects):
                lane = (brick * sects + sect) * capacity
                out_ref[:, lane : lane + capacity] = blocks[(sect * bricks + brick) ^ me]

    return body


def swap(array, axis, step):
    return lax.ppermute(array, axis, [(i, i ^ step) for i in range(lax.axis_size(axis))])


def swap_pairs(array, axes, start, fill):
    everything = ("case", "brick", "sect", "slab")
    sizes = [lax.axis_size(a) for a in everything]
    pairs = []
    for i, at in enumerate(np.ndindex(*sizes)):
        at = dict(zip(everything, at))
        place, size = 0, 1
        for a in axes:
            place, size = place * lax.axis_size(a) + at[a], size * lax.axis_size(a)
        other = place + 1 if (place - start) % 2 == 0 else place - 1
        if 0 <= other < size:
            for a in reversed(axes):
                other, at[a] = divmod(other, lax.axis_size(a))
        else:
            at[fill] ^= 1
        pairs.append((i, int(np.ravel_multi_index([at[a] for a in everything], sizes))))
    return lax.ppermute(array, everything, pairs)


def on_device(
    geometry,
    conv_kernels,
    point_place,
    point_attr,
    destination,
    dense_first,
    dense_middle,
    dense_last,
):
    channels, span_x, span_y, span_z = geometry.shape
    count = point_place.shape[1]
    bricks, sects = lax.axis_size("brick"), lax.axis_size("sect")
    capacity = 5 * count // (4 * bricks * sects)
    slots = bricks * sects * capacity
    outputs = dense_last.shape[1]
    lines = ("sect", "slab")

    def block(*shape):
        return jax.ShapeDtypeStruct(shape, BF16)

    own, even, odd, facing = call(
        columns_body,
        [
            block(span_x, span_y, channels, span_z),
            block(HALO, span_y, channels, span_z),
            block(HALO, span_y, channels, span_z),
            block(span_x, HALO, channels, span_z),
        ],
        [],
        8,
    )(geometry)
    even = swap_pairs(even, ("brick",), 0, "slab")
    odd = swap_pairs(odd, ("brick",), 1, "slab")
    cross = swap_pairs(facing, lines, 1, "case")
    pick, wz, wxy, kernel, attr, first, middle, last = call(
        make_points_body(span_x, span_y, bricks, sects, capacity),
        [
            block(slots, count),
            block(span_z, count),
            jax.ShapeDtypeStruct(((span_x + 2) * (span_y + 2), count), F32),
            block(2 * channels, 36 * channels),
            block(point_attr.shape[1], count),
            block(*dense_first.shape),
            block(*dense_middle.shape),
            block(*dense_last.shape),
        ],
        [
            pltpu.VMEM(point_place.shape, F32),
            pltpu.VMEM((1, count), jnp.int32),
            pltpu.VMEM(conv_kernels.shape[1:], BF16),
            pltpu.SemaphoreType.DMA((7,)),
        ],
        12,
        n_hbm=7,
    )(point_place, destination.reshape(1, count), conv_kernels[0], point_attr.T, dense_first,
      dense_middle, dense_last)
    features = jax.ShapeDtypeStruct((channels, count), F32)
    own_taps, total = call(
        block_body, [block(span_x, span_y, 3 * channels, span_z), features], [], 8
    )(own, kernel, wz, wxy)
    before, after, to_partner, to_cross = call(
        edges_body,
        [
            block(HALO, span_y, channels, span_z),
            block(HALO, span_y, channels, span_z),
            block(span_x + 2 * HALO, HALO, channels, span_z),
            block(2 * HALO, HALO, channels, span_z),
        ],
        [],
        4,
    )(own, even, odd, total)
    partner = swap(to_partner, "slab", 1)
    corner = swap_pairs(to_cross, lines, 1, "case")
    halo_taps, total = call(
        inner_body, [block(2 * HALO, span_y, 3 * channels, span_z), features], [], 8
    )(own_taps, before, after, kernel, wz, wxy, total)
    side = pltpu.VMEM((span_x + 2 * HALO, 2 * HALO, 3 * channels, span_z), BF16)
    total = call(partner_body, features, [side], 8)(
        own_taps, halo_taps, partner, kernel, wz, wxy, total
    )
    blocks = bricks * sects // 2

    def values(number):
        return jax.ShapeDtypeStruct((number, outputs, capacity), F32)

    sent, table = call(
        outer_body, [values(blocks), block(2, slots // 2, point_attr.shape[1] + channels)], [side], 8
    )(own_taps, halo_taps, cross, corner, kernel, wz, wxy, total, pick, attr, first, middle, last)
    got = swap(sent, "sect", sects // 2)
    kept = call(own_body, values(blocks), [], 8)(table, first, middle, last)
    labels = [list(range(blocks)), [blocks + q for q in range(blocks)]]
    step = blocks // 2
    while step:
        found = [(label, w, i) for w in range(2) for i, label in enumerate(labels[w])]
        leaving = [f for f in found if f[0] & step]
        staying = [f for f in found if not f[0] & step]
        sent, kept = call(
            make_deal_body([f[1:] for f in leaving], [f[1:] for f in staying]), [values(blocks)] * 2, [], 2
        )(kept, got)
        axis, distance = ("brick", step) if step < bricks else ("sect", step // bricks)
        got = swap(sent, axis, distance)
        labels = [[f[0] for f in staying], [f[0] for f in leaving]]
        step //= 2
    order = {label: (w, i) for w in range(2) for i, label in enumerate(labels[w])}
    return call(
        make_collect_body([order[r] for r in range(2 * blocks)], bricks, sects),
        jax.ShapeDtypeStruct((outputs, slots), F32),
        [pltpu.VMEM((2 * blocks, outputs, capacity), F32)],
        2,
    )(kept, got)


def solution(mesh):
    in_specs = (
        P(None, ("case", "brick"), ("sect", "slab"), None),
        P(),
        P(None, ("case", "brick", "sect", "slab")),
        P(("case", "brick", "sect", "slab"), None),
        P(("case", "brick", "sect", "slab"), None),
        P(),
        P(),
        P(),
    )
    out_specs = P(None, ("case", "brick", "sect", "slab"))
    return jax.shard_map(on_device, mesh=mesh, in_specs=in_specs, out_specs=out_specs, check_vma=False)
```

```python
import jax
import jax.numpy as jnp
import numpy as np
from jax import lax
from jax.experimental import pallas as pl
from jax.experimental.pallas import tpu as pltpu
from jax.sharding import PartitionSpec as P


F32 = jnp.float32
BF16 = jnp.bfloat16
HALO = 2


def hat(offset):
    return jnp.maximum(0.0, 1.0 - jnp.abs(offset))


def gelu(value):
    half = 0.5 * value
    slope = 0.7978845608028654
    return half + half * jnp.tanh(value * (slope + (slope * 0.044715) * (value * value)))


def iota(shape, axis):
    return lax.broadcasted_iota(jnp.int32, shape, axis)


def call(body, outs, scratch, mib, n_hbm=0):
    def run(*args):
        spaces = [pltpu.VMEM] * (len(args) - n_hbm) + [pltpu.HBM] * n_hbm
        args = [pltpu.with_memory_space_constraint(a, s) if s == pltpu.HBM else a for a, s in zip(args, spaces)]
        return pl.pallas_call(
            body,
            out_shape=outs,
            in_specs=[pl.BlockSpec(memory_space=s) for s in spaces],
            out_specs=jax.tree.map(lambda _: pl.BlockSpec(memory_space=pltpu.VMEM), outs),
            scratch_shapes=scratch,
            compiler_params=pltpu.CompilerParams(vmem_limit_bytes=mib << 20),
        )(*args)

    return run


def columns_body(g_ref, own_ref, even_ref, odd_ref, cross_ref):
    span_x, span_y = g_ref.shape[1:3]
    parity, slab = lax.axis_index("brick") % 2, lax.axis_index("slab")
    for x in range(span_x):
        own_ref[x] = jnp.swapaxes(g_ref[:, x].astype(F32), 0, 1).astype(BF16)
    for side in range(2):

        @pl.when(parity == side)
        def _(up=(even_ref, odd_ref)[side], down=(odd_ref, even_ref)[side]):
            up[...] = own_ref[span_x - HALO :]
            down[...] = own_ref[:HALO]

        @pl.when(slab == side)
        def _(side=side):
            cross_ref[...] = own_ref[:, span_y - HALO :] if side else own_ref[:, :HALO]


def edges_body(own_ref, even_ref, odd_ref, _, before_ref, after_ref, partner_ref, cross_ref):
    span_x, span_y = own_ref.shape[:2]
    for side in range(2):

        @pl.when(lax.axis_index("brick") % 2 == side)
        def _(before=(odd_ref, even_ref)[side], after=(even_ref, odd_ref)[side]):
            brick = lax.axis_index("brick")
            outside = jnp.zeros(before_ref.shape, F32)
            inside = before[...].astype(F32)
            before_ref[...] = jnp.where(brick > 0, inside, outside).astype(BF16)
            inside = after[...].astype(F32)
            after_ref[...] = jnp.where(brick < lax.axis_size("brick") - 1, inside, outside).astype(BF16)

    for slab in range(2):

        @pl.when(lax.axis_index("slab") == slab)
        def _(slab=slab):
            near, far = slice(0, HALO), slice(span_y - HALO, span_y)
            facing, outward = (near, far) if slab else (far, near)
            partner_ref[:HALO] = before_ref[:, facing]
            partner_ref[HALO : HALO + span_x] = own_ref[:, facing]
            partner_ref[HALO + span_x :] = after_ref[:, facing]
            cross_ref[:HALO] = before_ref[:, outward]
            cross_ref[HALO:] = after_ref[:, outward]


def make_points_body(span_x, span_y, bricks, sects, capacity):
    def body(
        place_hbm, dest_hbm, conv_hbm, attr_hbm, first_hbm, middle_hbm, last_hbm,
        pick_ref, wz_ref, wxy_ref, kernel_ref, attr_ref, first_ref, middle_ref, last_ref,
        place_ref, dest_ref, conv_ref, sems,
    ):
        sources = (place_hbm, dest_hbm, conv_hbm, attr_hbm, first_hbm, middle_hbm, last_hbm)
        targets = (place_ref, dest_ref, conv_ref, attr_ref, first_ref, middle_ref, last_ref)
        copies = [
            pltpu.make_async_copy(source, target, sems.at[i])
            for i, (source, target) in enumerate(zip(sources, targets))
        ]
        for copy in copies:
            copy.start()
        copies[0].wait()
        count = place_ref.shape[1]
        span_z = wz_ref.shape[0]
        slots = pick_ref.shape[0]
        brick, line = lax.axis_index("brick"), lax.axis_index(("sect", "slab"))
        last_brick, last_line = lax.axis_size("brick") - 1, lax.axis_size(("sect", "slab")) - 1
        local_x = place_ref[0:1, :] * span_x
        local_y = place_ref[1:2, :] * span_y
        local_z = place_ref[2:3, :] * span_z
        cell_z = iota((span_z, count), 0).astype(F32) + 0.5
        wz_ref[...] = hat(local_z - cell_z).astype(BF16)
        weight_y = []
        for y in range(span_y + 2):
            w = hat(local_y - (y - 0.5))
            if y == 0:
                w = jnp.where(line > 0, w, 0.0)
            if y == span_y + 1:
                w = jnp.where(line < last_line, w, 0.0)
            weight_y.append(w)
        for x in range(span_x + 2):
            w = hat(local_x - (x - 0.5))
            if x == 0:
                w = jnp.where(brick > 0, w, 0.0)
            if x == span_x + 1:
                w = jnp.where(brick < last_brick, w, 0.0)
            for y in range(span_y + 2):
                row = x * (span_y + 2) + y
                wxy_ref[row : row + 1, :] = w * weight_y[y]
        copies[1].wait()
        row = dest_ref[...].astype(F32)
        earlier, later = iota((count, count), 0), iota((count, count), 1)
        diagonal = jnp.where(earlier == later, jnp.broadcast_to(row, (count, count)), 0.0)
        along = jnp.sum(diagonal, axis=1, keepdims=True)
        same = jnp.where((along == row) & (earlier < later), 1.0, 0.0)
        arrival = jnp.sum(same, axis=0, keepdims=True).astype(jnp.int32)
        target = row.astype(jnp.int32)
        slot = ((target % sects) * bricks + target // sects) * capacity + arrival
        pick = jnp.where(iota((slots, count), 0) == slot, 1.0, 0.0).astype(BF16)
        pick_ref[...] = pick
        copies[2].wait()
        channels = conv_ref.shape[-1]
        group = 9 * channels
        kernel_ref[:channels, 3 * group :] = jnp.zeros((channels, group), BF16)
        kernel_ref[channels:, :group] = jnp.zeros((channels, group), BF16)
        for a in range(3):
            for b in range(3):
                for e in range(3):
                    tile = conv_ref[a, b, e].astype(F32).T.astype(BF16)
                    for j in range(2):
                        lanes = (j + b) * group + (a * 3 + e) * channels
                        kernel_ref[j * channels : (j + 1) * channels, lanes : lanes + channels] = tile
        for copy in copies[3:]:
            copy.wait()

    return body


def taps(tile, inside=True):
    span_z = tile.shape[1]
    lane = iota((1, span_z), 1)
    below, here, above = (
        jnp.where(keep & inside, 1.0, 0.0).astype(BF16)
        for keep in (lane > 0, lane >= 0, lane < span_z - 1)
    )
    pieces = (pltpu.roll(tile, 1, 1) * below, tile * here, pltpu.roll(tile, span_z - 1, 1) * above)
    return jnp.concatenate(pieces, axis=0)


def share(total, units, kernel_ref, wz_ref, wxy_ref):
    channels, span_z = total.shape[0], wz_ref.shape[0]
    for first in range(0, len(units), 4):
        group = units[first : first + 4]
        wide = jnp.concatenate(
            [
                jnp.concatenate([tap(x + a, c) for tap, _, x in group], axis=1)
                for c in range(4)
                for a in range(3)
            ],
            axis=0,
        )
        part = jnp.dot(kernel_ref[...], wide, preferred_element_type=F32)
        tiles, weights = [], []
        for j in range(2):
            centre = jnp.concatenate(
                [tap(x + 1, j + 1)[channels : 2 * channels] for tap, _, x in group], axis=1
            )
            response = part[j * channels : (j + 1) * channels]
            latent = (centre.astype(F32) + gelu(response)).astype(BF16)
            for u, (_, row, x) in enumerate(group):
                tiles.append(latent[:, u * span_z : (u + 1) * span_z])
                weights.append(wxy_ref[pl.ds(row(x) + j, 1), :])
        sampled = jnp.dot(
            jnp.concatenate(tiles, axis=0), wz_ref[...], preferred_element_type=F32
        )
        for k, w in enumerate(weights):
            total += sampled[k * channels : (k + 1) * channels] * w
    return total


def inner_units(layers, span_y, layer_taps):
    return [
        (
            lambda x, c, y=y: layer_taps(x)[y - HALO + c],
            lambda x, y=y: x * (span_y + 2) + y,
            x,
        )
        for x in layers
        for y in range(HALO, span_y, 2)
    ]


def block_body(own_ref, kernel_ref, wz_ref, wxy_ref, taps_ref, total_ref):
    span_x, span_y = own_ref.shape[:2]
    for x in range(span_x):
        for y in range(span_y):
            taps_ref[x, y] = taps(own_ref[x, y])
    units = inner_units(range(HALO, span_x), span_y, lambda x: taps_ref.at[x - HALO])
    total = jnp.zeros(total_ref.shape, F32)
    total_ref[...] = share(total, units, kernel_ref, wz_ref, wxy_ref)


def layer_of(own_ref, halo_ref, x):
    span_x = own_ref.shape[0]
    if HALO <= x < HALO + span_x:
        return own_ref.at[x - HALO]
    return halo_ref.at[x if x < HALO else x - span_x]


def inner_body(
    own_ref, before_ref, after_ref, kernel_ref, wz_ref, wxy_ref, start_ref, halo_ref, total_ref
):
    span_x, span_y = own_ref.shape[:2]
    for x in range(HALO):
        for y in range(span_y):
            halo_ref[x, y] = taps(before_ref[x, y])
            halo_ref[HALO + x, y] = taps(after_ref[x, y])
    layers = [*range(HALO), *range(span_x, span_x + 2)]
    units = inner_units(layers, span_y, lambda x: layer_of(own_ref, halo_ref, x))
    total_ref[...] = share(start_ref[...], units, kernel_ref, wz_ref, wxy_ref)


def side_units(on_left, inside, layers, halo_tile, own_ref, halo_ref, side_ref):
    _, span_y = own_ref.shape[:2]
    near = jnp.where(on_left, 0, span_y - HALO)
    for x in sorted({x + a for x in layers for a in range(3)}):
        for j in range(HALO):
            side_ref[x, jnp.where(on_left, HALO, 0) + j] = layer_of(own_ref, halo_ref, x)[near + j]
            side_ref[x, jnp.where(on_left, 0, HALO) + j] = taps(halo_tile(x)[j], inside)
    base = jnp.where(on_left, 0, span_y)
    return [(lambda x, c: side_ref[x, c], lambda x: x * (span_y + 2) + base, x) for x in layers]


def cross_units(layers, cross_ref, corner_ref, own_ref, halo_ref, side_ref):
    line = lax.axis_index(("sect", "slab"))
    inside = (line > 0) & (line < lax.axis_size(("sect", "slab")) - 1)
    return side_units(
        lax.axis_index("slab") == 0, inside, layers, lambda x: layer_of(cross_ref, corner_ref, x),
        own_ref, halo_ref, side_ref,
    )


def beside_body(
    own_ref, halo_ref, partner_ref, cross_ref, kernel_ref, wz_ref, wxy_ref, start_ref,
    total_ref, partner_side, cross_side,
):
    span_x = own_ref.shape[0]
    units = side_units(
        lax.axis_index("slab") == 1, True, range(span_x + 2), lambda x: partner_ref.at[x],
        own_ref, halo_ref, partner_side,
    )
    units += cross_units(range(HALO, span_x), cross_ref, None, own_ref, halo_ref, cross_side)
    total_ref[...] = share(start_ref[...], units, kernel_ref, wz_ref, wxy_ref)


def outer_body(
    own_ref, halo_ref, cross_ref, corner_ref, kernel_ref, wz_ref, wxy_ref, start_ref,
    pick_ref, attr_ref, first_ref, middle_ref, last_ref,
    value_ref, row_ref, cross_side,
):
    span_x = own_ref.shape[0]
    layers = [*range(HALO), *range(span_x, span_x + 2)]
    units = cross_units(layers, cross_ref, corner_ref, own_ref, halo_ref, cross_side)
    total = share(start_ref[...], units, kernel_ref, wz_ref, wxy_ref)
    table = jnp.concatenate([total.astype(BF16), attr_ref[...]], axis=0)
    row = lax.dot_general(
        pick_ref[...], table, (((1,), (1,)), ((), ())), preferred_element_type=F32
    ).astype(BF16)
    half = row.shape[0] // 2
    for s in range(2):
        row_ref[s] = row[s * half : (s + 1) * half]
    network(1 - own_section(), row_ref, first_ref, middle_ref, last_ref, value_ref)


def own_section():
    return lax.axis_index("sect") // (lax.axis_size("sect") // 2)


def own_place():
    return (
        lax.axis_index("sect") % (lax.axis_size("sect") // 2) * lax.axis_size("brick")
        + lax.axis_index("brick")
    )


def network(s, row_ref, first_ref, middle_ref, last_ref, value_ref):
    act = gelu(jnp.dot(row_ref[s], first_ref[s], preferred_element_type=F32)).astype(BF16)
    for i in range(middle_ref.shape[1]):
        act = gelu(jnp.dot(act, middle_ref[s, i], preferred_element_type=F32)).astype(BF16)
    value = lax.dot_general(
        last_ref[s], act, (((1,), (1,)), ((), ())), preferred_element_type=F32
    )
    blocks, _, capacity = value_ref.shape
    place = own_place()
    for q in range(blocks):
        value_ref[q ^ place] = value[:, q * capacity : (q + 1) * capacity]


def own_body(*refs):
    network(own_section(), *refs)


def make_deal_body(sent, kept):
    def body(kept_ref, got_ref, sent_out, kept_out):
        for out, blocks in ((sent_out, sent), (kept_out, kept)):
            for i, (which, at) in enumerate(blocks):
                out[i] = (kept_ref, got_ref)[which][at]

    return body


def make_collect_body(order, bricks, sects):
    def body(kept_ref, got_ref, out_ref, blocks):
        for r, (which, at) in enumerate(order):
            blocks[r] = (kept_ref, got_ref)[which][at]
        capacity = kept_ref.shape[2]
        me = own_section() * (bricks * sects // 2) + own_place()
        for brick in range(bricks):
            for sect in range(sects):
                lane = (brick * sects + sect) * capacity
                out_ref[:, lane : lane + capacity] = blocks[(sect * bricks + brick) ^ me]

    return body


def swap(array, axis, step):
    return lax.ppermute(array, axis, [(i, i ^ step) for i in range(lax.axis_size(axis))])


def swap_pairs(array, axes, start, fill):
    everything = ("case", "brick", "sect", "slab")
    sizes = [lax.axis_size(a) for a in everything]
    pairs = []
    for i, at in enumerate(np.ndindex(*sizes)):
        at = dict(zip(everything, at))
        place, size = 0, 1
        for a in axes:
            place, size = place * lax.axis_size(a) + at[a], size * lax.axis_size(a)
        other = place + 1 if (place - start) % 2 == 0 else place - 1
        if 0 <= other < size:
            for a in reversed(axes):
                other, at[a] = divmod(other, lax.axis_size(a))
        else:
            at[fill] ^= 1
        pairs.append((i, int(np.ravel_multi_index([at[a] for a in everything], sizes))))
    return lax.ppermute(array, everything, pairs)


def on_device(
    geometry,
    conv_kernels,
    point_place,
    point_attr,
    destination,
    dense_first,
    dense_middle,
    dense_last,
):
    channels, span_x, span_y, span_z = geometry.shape
    count = point_place.shape[1]
    bricks, sects = lax.axis_size("brick"), lax.axis_size("sect")
    capacity = 5 * count // (4 * bricks * sects)
    slots = bricks * sects * capacity
    outputs = dense_last.shape[1]
    lines = ("sect", "slab")

    def block(*shape):
        return jax.ShapeDtypeStruct(shape, BF16)

    own, even, odd, facing = call(
        columns_body,
        [
            block(span_x, span_y, channels, span_z),
            block(HALO, span_y, channels, span_z),
            block(HALO, span_y, channels, span_z),
            block(span_x, HALO, channels, span_z),
        ],
        [],
        8,
    )(geometry)
    even = swap_pairs(even, ("brick",), 0, "slab")
    odd = swap_pairs(odd, ("brick",), 1, "slab")
    cross = swap_pairs(facing, lines, 1, "case")
    pick, wz, wxy, kernel, attr, first, middle, last = call(
        make_points_body(span_x, span_y, bricks, sects, capacity),
        [
            block(slots, count),
            block(span_z, count),
            jax.ShapeDtypeStruct(((span_x + 2) * (span_y + 2), count), F32),
            block(2 * channels, 36 * channels),
            block(point_attr.shape[1], count),
            block(*dense_first.shape),
            block(*dense_middle.shape),
            block(*dense_last.shape),
        ],
        [
            pltpu.VMEM(point_place.shape, F32),
            pltpu.VMEM((1, count), jnp.int32),
            pltpu.VMEM(conv_kernels.shape[1:], BF16),
            pltpu.SemaphoreType.DMA((7,)),
        ],
        12,
        n_hbm=7,
    )(point_place, destination.reshape(1, count), conv_kernels[0], point_attr.T, dense_first,
      dense_middle, dense_last)
    features = jax.ShapeDtypeStruct((channels, count), F32)
    own_taps, total = call(
        block_body, [block(span_x, span_y, 3 * channels, span_z), features], [], 8
    )(own, kernel, wz, wxy)
    before, after, to_partner, to_cross = call(
        edges_body,
        [
            block(HALO, span_y, channels, span_z),
            block(HALO, span_y, channels, span_z),
            block(span_x + 2 * HALO, HALO, channels, span_z),
            block(2 * HALO, HALO, channels, span_z),
        ],
        [],
        4,
    )(own, even, odd, total)
    partner = swap(to_partner, "slab", 1)
    corner = swap_pairs(to_cross, lines, 1, "case")
    halo_taps, total = call(
        inner_body, [block(2 * HALO, span_y, 3 * channels, span_z), features], [], 8
    )(own_taps, before, after, kernel, wz, wxy, total)
    side = pltpu.VMEM((span_x + 2 * HALO, 2 * HALO, 3 * channels, span_z), BF16)
    total = call(beside_body, features, [side, side], 10)(own_taps, halo_taps, partner, cross, kernel, wz, wxy, total)
    blocks = bricks * sects // 2

    def values(number):
        return jax.ShapeDtypeStruct((number, outputs, capacity), F32)

    sent, table = call(
        outer_body, [values(blocks), block(2, slots // 2, point_attr.shape[1] + channels)], [side], 8
    )(own_taps, halo_taps, cross, corner, kernel, wz, wxy, total, pick, attr, first, middle, last)
    got = swap(sent, "sect", sects // 2)
    kept = call(own_body, values(blocks), [], 8)(table, first, middle, last)
    labels = [list(range(blocks)), [blocks + q for q in range(blocks)]]
    step = blocks // 2
    while step:
        found = [(label, w, i) for w in range(2) for i, label in enumerate(labels[w])]
        leaving = [f for f in found if f[0] & step]
        staying = [f for f in found if not f[0] & step]
        sent, kept = call(
            make_deal_body([f[1:] for f in leaving], [f[1:] for f in staying]), [values(blocks)] * 2, [], 2
        )(kept, got)
        axis, distance = ("brick", step) if step < bricks else ("sect", step // bricks)
        got = swap(sent, axis, distance)
        labels = [[f[0] for f in staying], [f[0] for f in leaving]]
        step //= 2
    order = {label: (w, i) for w in range(2) for i, label in enumerate(labels[w])}
    return call(
        make_collect_body([order[r] for r in range(2 * blocks)], bricks, sects),
        jax.ShapeDtypeStruct((outputs, slots), F32),
        [pltpu.VMEM((2 * blocks, outputs, capacity), F32)],
        2,
    )(kept, got)


def solution(mesh):
    in_specs = (
        P(None, ("case", "brick"), ("sect", "slab"), None),
        P(),
        P(None, ("case", "brick", "sect", "slab")),
        P(("case", "brick", "sect", "slab"), None),
        P(("case", "brick", "sect", "slab"), None),
        P(),
        P(),
        P(),
    )
    out_specs = P(None, ("case", "brick", "sect", "slab"))
    return jax.shard_map(on_device, mesh=mesh, in_specs=in_specs, out_specs=out_specs, check_vma=False)
```

```python
import jax
import jax.numpy as jnp
import numpy as np
from jax import lax
from jax.experimental import pallas as pl
from jax.experimental.pallas import tpu as pltpu
from jax.sharding import PartitionSpec as P


F32 = jnp.float32
BF16 = jnp.bfloat16
HALO = 2


def hat(offset):
    return jnp.maximum(0.0, 1.0 - jnp.abs(offset))


def gelu(value):
    half = 0.5 * value
    slope = 0.7978845608028654
    return half + half * jnp.tanh(value * (slope + (slope * 0.044715) * (value * value)))


def iota(shape, axis):
    return lax.broadcasted_iota(jnp.int32, shape, axis)


def call(body, outs, scratch, mib, n_hbm=0):
    def run(*args):
        spaces = [pltpu.VMEM] * (len(args) - n_hbm) + [pltpu.HBM] * n_hbm
        args = [pltpu.with_memory_space_constraint(a, s) if s == pltpu.HBM else a for a, s in zip(args, spaces)]
        return pl.pallas_call(
            body,
            out_shape=outs,
            in_specs=[pl.BlockSpec(memory_space=s) for s in spaces],
            out_specs=jax.tree.map(lambda _: pl.BlockSpec(memory_space=pltpu.VMEM), outs),
            scratch_shapes=scratch,
            compiler_params=pltpu.CompilerParams(vmem_limit_bytes=mib << 20),
        )(*args)

    return run


def columns_body(g_ref, own_ref, even_ref, odd_ref, cross_ref):
    span_x, span_y = g_ref.shape[1:3]
    parity, slab = lax.axis_index("brick") % 2, lax.axis_index("slab")
    for x in range(span_x):
        own_ref[x] = jnp.swapaxes(g_ref[:, x], 0, 1)
    for side in range(2):

        @pl.when(parity == side)
        def _(up=(even_ref, odd_ref)[side], down=(odd_ref, even_ref)[side]):
            up[...] = own_ref[span_x - HALO :]
            down[...] = own_ref[:HALO]

        @pl.when(slab == side)
        def _(side=side):
            cross_ref[...] = own_ref[:, span_y - HALO :] if side else own_ref[:, :HALO]


def edges_body(own_ref, even_ref, odd_ref, _, before_ref, after_ref, partner_ref, cross_ref):
    span_x, span_y = own_ref.shape[:2]
    for side in range(2):

        @pl.when(lax.axis_index("brick") % 2 == side)
        def _(before=(odd_ref, even_ref)[side], after=(even_ref, odd_ref)[side]):
            brick, last = lax.axis_index("brick"), lax.axis_size("brick") - 1
            for ref, source, inside in (
                (before_ref, before, brick > 0),
                (after_ref, after, brick < last),
            ):
                keep = jnp.where(inside, jnp.ones((1, 1, 1, source.shape[3]), F32), 0.0).astype(BF16)
                ref[...] = source[...] * keep

    for slab in range(2):

        @pl.when(lax.axis_index("slab") == slab)
        def _(slab=slab):
            near, far = slice(0, HALO), slice(span_y - HALO, span_y)
            facing, outward = (near, far) if slab else (far, near)
            partner_ref[:HALO] = before_ref[:, facing]
            partner_ref[HALO : HALO + span_x] = own_ref[:, facing]
            partner_ref[HALO + span_x :] = after_ref[:, facing]
            cross_ref[:HALO] = before_ref[:, outward]
            cross_ref[HALO:] = after_ref[:, outward]


def make_points_body(span_x, span_y, bricks, sects, capacity):
    def body(
        place_hbm, dest_hbm, conv_hbm, attr_hbm, first_hbm, middle_hbm, last_hbm,
        pick_ref, wz_ref, wxy_ref, kernel_ref, attr_ref, first_ref, middle_ref, last_ref,
        place_ref, dest_ref, conv_ref, sems,
    ):
        sources = (place_hbm, dest_hbm, conv_hbm, attr_hbm, first_hbm, middle_hbm, last_hbm)
        targets = (place_ref, dest_ref, conv_ref, attr_ref, first_ref, middle_ref, last_ref)
        copies = [
            pltpu.make_async_copy(source, target, sems.at[i])
            for i, (source, target) in enumerate(zip(sources, targets))
        ]
        for copy in copies:
            copy.start()
        copies[0].wait()
        count = place_ref.shape[1]
        span_z = wz_ref.shape[0]
        slots = pick_ref.shape[0]
        brick, line = lax.axis_index("brick"), lax.axis_index(("sect", "slab"))
        last_brick, last_line = lax.axis_size("brick") - 1, lax.axis_size(("sect", "slab")) - 1
        local_x = place_ref[0:1, :] * span_x
        local_y = place_ref[1:2, :] * span_y
        local_z = place_ref[2:3, :] * span_z
        cell_z = iota((span_z, count), 0).astype(F32) + 0.5
        wz_ref[...] = hat(local_z - cell_z).astype(BF16)
        weight_y = []
        for y in range(span_y + 2):
            w = hat(local_y - (y - 0.5))
            if y == 0:
                w = jnp.where(line > 0, w, 0.0)
            if y == span_y + 1:
                w = jnp.where(line < last_line, w, 0.0)
            weight_y.append(w)
        for x in range(span_x + 2):
            w = hat(local_x - (x - 0.5))
            if x == 0:
                w = jnp.where(brick > 0, w, 0.0)
            if x == span_x + 1:
                w = jnp.where(brick < last_brick, w, 0.0)
            for y in range(span_y + 2):
                row = x * (span_y + 2) + y
                wxy_ref[row : row + 1, :] = w * weight_y[y]
        copies[1].wait()
        row = dest_ref[...].astype(F32)
        earlier, later = iota((count, count), 0), iota((count, count), 1)
        diagonal = jnp.where(earlier == later, jnp.broadcast_to(row, (count, count)), 0.0)
        along = jnp.sum(diagonal, axis=1, keepdims=True)
        same = jnp.where((along == row) & (earlier < later), 1.0, 0.0)
        arrival = jnp.sum(same, axis=0, keepdims=True).astype(jnp.int32)
        target = row.astype(jnp.int32)
        slot = ((target % sects) * bricks + target // sects) * capacity + arrival
        pick = jnp.where(iota((slots, count), 0) == slot, 1.0, 0.0).astype(BF16)
        pick_ref[...] = pick
        copies[2].wait()
        channels = conv_ref.shape[-1]
        group = 9 * channels
        kernel_ref[:channels, 3 * group :] = jnp.zeros((channels, group), BF16)
        kernel_ref[channels:, :group] = jnp.zeros((channels, group), BF16)
        for a in range(3):
            for b in range(3):
                for e in range(3):
                    tile = conv_ref[a, b, e].astype(F32).T.astype(BF16)
                    for j in range(2):
                        lanes = (j + b) * group + (a * 3 + e) * channels
                        kernel_ref[j * channels : (j + 1) * channels, lanes : lanes + channels] = tile
        for copy in copies[3:]:
            copy.wait()

    return body


def taps(tile, inside=True):
    span_z = tile.shape[1]
    lane = iota((1, span_z), 1)
    below, here, above = (
        jnp.where(keep & inside, 1.0, 0.0).astype(BF16)
        for keep in (lane > 0, lane >= 0, lane < span_z - 1)
    )
    pieces = (pltpu.roll(tile, 1, 1) * below, tile * here, pltpu.roll(tile, span_z - 1, 1) * above)
    return jnp.concatenate(pieces, axis=0)


def share(total, units, kernel_ref, wz_ref, wxy_ref):
    channels, span_z = total.shape[0], wz_ref.shape[0]
    for first in range(0, len(units), 4):
        group = units[first : first + 4]
        wide = jnp.concatenate(
            [
                jnp.concatenate([tap(x + a, c) for tap, _, x in group], axis=1)
                for c in range(4)
                for a in range(3)
            ],
            axis=0,
        )
        part = jnp.dot(kernel_ref[...], wide, preferred_element_type=F32)
        tiles, weights = [], []
        for j in range(2):
            centre = jnp.concatenate(
                [tap(x + 1, j + 1)[channels : 2 * channels] for tap, _, x in group], axis=1
            )
            response = part[j * channels : (j + 1) * channels]
            latent = (centre.astype(F32) + gelu(response)).astype(BF16)
            for u, (_, row, x) in enumerate(group):
                tiles.append(latent[:, u * span_z : (u + 1) * span_z])
                weights.append(wxy_ref[pl.ds(row(x) + j, 1), :])
        sampled = jnp.dot(
            jnp.concatenate(tiles, axis=0), wz_ref[...], preferred_element_type=F32
        )
        for k, w in enumerate(weights):
            total += sampled[k * channels : (k + 1) * channels] * w
    return total


def inner_units(layers, span_y, layer_taps):
    return [
        (
            lambda x, c, y=y: layer_taps(x)[y - HALO + c],
            lambda x, y=y: x * (span_y + 2) + y,
            x,
        )
        for x in layers
        for y in range(HALO, span_y, 2)
    ]


def block_body(own_ref, kernel_ref, wz_ref, wxy_ref, taps_ref, total_ref):
    span_x, span_y = own_ref.shape[:2]
    for x in range(span_x):
        for y in range(span_y):
            taps_ref[x, y] = taps(own_ref[x, y])
    units = inner_units(range(HALO, span_x), span_y, lambda x: taps_ref.at[x - HALO])
    total = jnp.zeros(total_ref.shape, F32)
    total_ref[...] = share(total, units, kernel_ref, wz_ref, wxy_ref)


def layer_of(own_ref, halo_ref, x):
    span_x = own_ref.shape[0]
    if HALO <= x < HALO + span_x:
        return own_ref.at[x - HALO]
    return halo_ref.at[x if x < HALO else x - span_x]


def inner_body(
    own_ref, before_ref, after_ref, kernel_ref, wz_ref, wxy_ref, start_ref, halo_ref, total_ref
):
    span_x, span_y = own_ref.shape[:2]
    for x in range(HALO):
        for y in range(span_y):
            halo_ref[x, y] = taps(before_ref[x, y])
            halo_ref[HALO + x, y] = taps(after_ref[x, y])
    layers = [*range(HALO), *range(span_x, span_x + 2)]
    units = inner_units(layers, span_y, lambda x: layer_of(own_ref, halo_ref, x))
    total_ref[...] = share(start_ref[...], units, kernel_ref, wz_ref, wxy_ref)


def side_units(on_left, inside, layers, halo_tile, own_ref, halo_ref, side_ref):
    _, span_y = own_ref.shape[:2]
    near = jnp.where(on_left, 0, span_y - HALO)
    for x in sorted({x + a for x in layers for a in range(3)}):
        for j in range(HALO):
            side_ref[x, jnp.where(on_left, HALO, 0) + j] = layer_of(own_ref, halo_ref, x)[near + j]
            side_ref[x, jnp.where(on_left, 0, HALO) + j] = taps(halo_tile(x)[j], inside)
    base = jnp.where(on_left, 0, span_y)
    return [(lambda x, c: side_ref[x, c], lambda x: x * (span_y + 2) + base, x) for x in layers]


def cross_units(layers, cross_ref, corner_ref, own_ref, halo_ref, side_ref):
    line = lax.axis_index(("sect", "slab"))
    inside = (line > 0) & (line < lax.axis_size(("sect", "slab")) - 1)
    return side_units(
        lax.axis_index("slab") == 0, inside, layers, lambda x: layer_of(cross_ref, corner_ref, x),
        own_ref, halo_ref, side_ref,
    )


def beside_body(
    own_ref, halo_ref, partner_ref, cross_ref, kernel_ref, wz_ref, wxy_ref, start_ref,
    total_ref, partner_side, cross_side,
):
    span_x = own_ref.shape[0]
    units = side_units(
        lax.axis_index("slab") == 1, True, range(span_x + 2), lambda x: partner_ref.at[x],
        own_ref, halo_ref, partner_side,
    )
    units += cross_units(range(HALO, span_x), cross_ref, None, own_ref, halo_ref, cross_side)
    total_ref[...] = share(start_ref[...], units, kernel_ref, wz_ref, wxy_ref)


def outer_body(
    own_ref, halo_ref, cross_ref, corner_ref, kernel_ref, wz_ref, wxy_ref, start_ref,
    pick_ref, attr_ref, first_ref, middle_ref, last_ref,
    value_ref, row_ref, cross_side,
):
    span_x = own_ref.shape[0]
    layers = [*range(HALO), *range(span_x, span_x + 2)]
    units = cross_units(layers, cross_ref, corner_ref, own_ref, halo_ref, cross_side)
    total = share(start_ref[...], units, kernel_ref, wz_ref, wxy_ref)
    table = jnp.concatenate([total.astype(BF16), attr_ref[...]], axis=0)
    row = lax.dot_general(
        pick_ref[...], table, (((1,), (1,)), ((), ())), preferred_element_type=F32
    ).astype(BF16)
    half = row.shape[0] // 2
    for s in range(2):
        row_ref[s] = row[s * half : (s + 1) * half]
    network(1 - own_section(), row_ref, first_ref, middle_ref, last_ref, value_ref)


def own_section():
    return lax.axis_index("sect") // (lax.axis_size("sect") // 2)


def own_place():
    return (
        lax.axis_index("sect") % (lax.axis_size("sect") // 2) * lax.axis_size("brick")
        + lax.axis_index("brick")
    )


def network(s, row_ref, first_ref, middle_ref, last_ref, value_ref):
    act = gelu(jnp.dot(row_ref[s], first_ref[s], preferred_element_type=F32)).astype(BF16)
    for i in range(middle_ref.shape[1]):
        act = gelu(jnp.dot(act, middle_ref[s, i], preferred_element_type=F32)).astype(BF16)
    value = lax.dot_general(
        last_ref[s], act, (((1,), (1,)), ((), ())), preferred_element_type=F32
    )
    blocks, _, capacity = value_ref.shape
    place = own_place()
    for q in range(blocks):
        value_ref[q ^ place] = value[:, q * capacity : (q + 1) * capacity]


def own_body(*refs):
    network(own_section(), *refs)


def make_deal_body(sent, kept):
    def body(kept_ref, got_ref, sent_out, kept_out):
        for out, blocks in ((sent_out, sent), (kept_out, kept)):
            for i, (which, at) in enumerate(blocks):
                out[i] = (kept_ref, got_ref)[which][at]

    return body


def make_collect_body(order, bricks, sects):
    def body(kept_ref, got_ref, out_ref, blocks):
        for r, (which, at) in enumerate(order):
            blocks[r] = (kept_ref, got_ref)[which][at]
        capacity = kept_ref.shape[2]
        me = own_section() * (bricks * sects // 2) + own_place()
        for brick in range(bricks):
            for sect in range(sects):
                lane = (brick * sects + sect) * capacity
                out_ref[:, lane : lane + capacity] = blocks[(sect * bricks + brick) ^ me]

    return body


def swap(array, axis, step):
    return lax.ppermute(array, axis, [(i, i ^ step) for i in range(lax.axis_size(axis))])


def swap_pairs(array, axes, start, fill):
    everything = ("case", "brick", "sect", "slab")
    sizes = [lax.axis_size(a) for a in everything]
    pairs = []
    for i, at in enumerate(np.ndindex(*sizes)):
        at = dict(zip(everything, at))
        place, size = 0, 1
        for a in axes:
            place, size = place * lax.axis_size(a) + at[a], size * lax.axis_size(a)
        other = place + 1 if (place - start) % 2 == 0 else place - 1
        if 0 <= other < size:
            for a in reversed(axes):
                other, at[a] = divmod(other, lax.axis_size(a))
        else:
            at[fill] ^= 1
        pairs.append((i, int(np.ravel_multi_index([at[a] for a in everything], sizes))))
    return lax.ppermute(array, everything, pairs)


def on_device(
    geometry,
    conv_kernels,
    point_place,
    point_attr,
    destination,
    dense_first,
    dense_middle,
    dense_last,
):
    channels, span_x, span_y, span_z = geometry.shape
    count = point_place.shape[1]
    bricks, sects = lax.axis_size("brick"), lax.axis_size("sect")
    capacity = 5 * count // (4 * bricks * sects)
    slots = bricks * sects * capacity
    outputs = dense_last.shape[1]
    lines = ("sect", "slab")

    def block(*shape):
        return jax.ShapeDtypeStruct(shape, BF16)

    own, even, odd, facing = call(
        columns_body,
        [
            block(span_x, span_y, channels, span_z),
            block(HALO, span_y, channels, span_z),
            block(HALO, span_y, channels, span_z),
            block(span_x, HALO, channels, span_z),
        ],
        [],
        8,
    )(geometry)
    even = swap_pairs(even, ("brick",), 0, "slab")
    odd = swap_pairs(odd, ("brick",), 1, "slab")
    cross = swap_pairs(facing, lines, 1, "case")
    pick, wz, wxy, kernel, attr, first, middle, last = call(
        make_points_body(span_x, span_y, bricks, sects, capacity),
        [
            block(slots, count),
            block(span_z, count),
            jax.ShapeDtypeStruct(((span_x + 2) * (span_y + 2), count), F32),
            block(2 * channels, 36 * channels),
            block(point_attr.shape[1], count),
            block(*dense_first.shape),
            block(*dense_middle.shape),
            block(*dense_last.shape),
        ],
        [
            pltpu.VMEM(point_place.shape, F32),
            pltpu.VMEM((1, count), jnp.int32),
            pltpu.VMEM(conv_kernels.shape[1:], BF16),
            pltpu.SemaphoreType.DMA((7,)),
        ],
        12,
        n_hbm=7,
    )(point_place, destination.reshape(1, count), conv_kernels[0], point_attr.T, dense_first,
      dense_middle, dense_last)
    features = jax.ShapeDtypeStruct((channels, count), F32)
    own_taps, total = call(
        block_body, [block(span_x, span_y, 3 * channels, span_z), features], [], 8
    )(own, kernel, wz, wxy)
    before, after, to_partner, to_cross = call(
        edges_body,
        [
            block(HALO, span_y, channels, span_z),
            block(HALO, span_y, channels, span_z),
            block(span_x + 2 * HALO, HALO, channels, span_z),
            block(2 * HALO, HALO, channels, span_z),
        ],
        [],
        4,
    )(own, even, odd, total)
    partner = swap(to_partner, "slab", 1)
    corner = swap_pairs(to_cross, lines, 1, "case")
    halo_taps, total = call(
        inner_body, [block(2 * HALO, span_y, 3 * channels, span_z), features], [], 8
    )(own_taps, before, after, kernel, wz, wxy, total)
    side = pltpu.VMEM((span_x + 2 * HALO, 2 * HALO, 3 * channels, span_z), BF16)
    total = call(beside_body, features, [side, side], 10)(own_taps, halo_taps, partner, cross, kernel, wz, wxy, total)
    blocks = bricks * sects // 2

    def values(number):
        return jax.ShapeDtypeStruct((number, outputs, capacity), F32)

    sent, table = call(
        outer_body, [values(blocks), block(2, slots // 2, point_attr.shape[1] + channels)], [side], 8
    )(own_taps, halo_taps, cross, corner, kernel, wz, wxy, total, pick, attr, first, middle, last)
    got = swap(sent, "sect", sects // 2)
    kept = call(own_body, values(blocks), [], 8)(table, first, middle, last)
    labels = [list(range(blocks)), [blocks + q for q in range(blocks)]]
    step = blocks // 2
    while step:
        found = [(label, w, i) for w in range(2) for i, label in enumerate(labels[w])]
        leaving = [f for f in found if f[0] & step]
        staying = [f for f in found if not f[0] & step]
        sent, kept = call(
            make_deal_body([f[1:] for f in leaving], [f[1:] for f in staying]), [values(blocks)] * 2, [], 2
        )(kept, got)
        axis, distance = ("brick", step) if step < bricks else ("sect", step // bricks)
        got = swap(sent, axis, distance)
        labels = [[f[0] for f in staying], [f[0] for f in leaving]]
        step //= 2
    order = {label: (w, i) for w in range(2) for i, label in enumerate(labels[w])}
    return call(
        make_collect_body([order[r] for r in range(2 * blocks)], bricks, sects),
        jax.ShapeDtypeStruct((outputs, slots), F32),
        [pltpu.VMEM((2 * blocks, outputs, capacity), F32)],
        2,
    )(kept, got)


def solution(mesh):
    in_specs = (
        P(None, ("case", "brick"), ("sect", "slab"), None),
        P(),
        P(None, ("case", "brick", "sect", "slab")),
        P(("case", "brick", "sect", "slab"), None),
        P(("case", "brick", "sect", "slab"), None),
        P(),
        P(),
        P(),
    )
    out_specs = P(None, ("case", "brick", "sect", "slab"))
    return jax.shard_map(on_device, mesh=mesh, in_specs=in_specs, out_specs=out_specs, check_vma=False)
```

```python
import jax
import jax.numpy as jnp
import numpy as np
from jax import lax
from jax.experimental import pallas as pl
from jax.experimental.pallas import tpu as pltpu
from jax.sharding import PartitionSpec as P


F32 = jnp.float32
BF16 = jnp.bfloat16
HALO = 2


def hat(offset):
    return jnp.maximum(0.0, 1.0 - jnp.abs(offset))


def gelu(value):
    half = 0.5 * value
    slope = 0.7978845608028654
    return half + half * jnp.tanh(value * (slope + (slope * 0.044715) * (value * value)))


def iota(shape, axis):
    return lax.broadcasted_iota(jnp.int32, shape, axis)


def call(body, outs, scratch, mib, n_hbm=0):
    def run(*args):
        spaces = [pltpu.VMEM] * (len(args) - n_hbm) + [pltpu.HBM] * n_hbm
        args = [pltpu.with_memory_space_constraint(a, s) if s == pltpu.HBM else a for a, s in zip(args, spaces)]
        return pl.pallas_call(
            body,
            out_shape=outs,
            in_specs=[pl.BlockSpec(memory_space=s) for s in spaces],
            out_specs=jax.tree.map(lambda _: pl.BlockSpec(memory_space=pltpu.VMEM), outs),
            scratch_shapes=scratch,
            compiler_params=pltpu.CompilerParams(vmem_limit_bytes=mib << 20),
        )(*args)

    return run


def columns_body(g_ref, own_ref, even_ref, odd_ref, cross_ref):
    span_x, span_y = g_ref.shape[1:3]
    parity, slab = lax.axis_index("brick") % 2, lax.axis_index("slab")
    for x in range(span_x):
        own_ref[x] = jnp.swapaxes(g_ref[:, x], 0, 1)
    for side in range(2):

        @pl.when(parity == side)
        def _(up=(even_ref, odd_ref)[side], down=(odd_ref, even_ref)[side]):
            up[...] = own_ref[span_x - HALO :]
            down[...] = own_ref[:HALO]

        @pl.when(slab == side)
        def _(side=side):
            cross_ref[...] = own_ref[:, span_y - HALO :] if side else own_ref[:, :HALO]


def edges_body(own_ref, even_ref, odd_ref, _, before_ref, after_ref, partner_ref, cross_ref):
    span_x, span_y = own_ref.shape[:2]
    for side in range(2):

        @pl.when(lax.axis_index("brick") % 2 == side)
        def _(before=(odd_ref, even_ref)[side], after=(even_ref, odd_ref)[side]):
            brick, last = lax.axis_index("brick"), lax.axis_size("brick") - 1
            for ref, source, inside in (
                (before_ref, before, brick > 0),
                (after_ref, after, brick < last),
            ):
                keep = jnp.where(inside, jnp.ones((1, 1, 1, source.shape[3]), F32), 0.0).astype(BF16)
                ref[...] = source[...] * keep

    for slab in range(2):

        @pl.when(lax.axis_index("slab") == slab)
        def _(slab=slab):
            near, far = slice(0, HALO), slice(span_y - HALO, span_y)
            facing, outward = (near, far) if slab else (far, near)
            partner_ref[:HALO] = before_ref[:, facing]
            partner_ref[HALO : HALO + span_x] = own_ref[:, facing]
            partner_ref[HALO + span_x :] = after_ref[:, facing]
            cross_ref[:HALO] = before_ref[:, outward]
            cross_ref[HALO:] = after_ref[:, outward]


def make_points_body(span_x, span_y, bricks, sects, capacity):
    def body(
        place_hbm, dest_hbm, conv_hbm, attr_hbm, first_hbm, middle_hbm, last_hbm,
        pick_ref, wz_ref, wxy_ref, kernel_ref, attr_ref, first_ref, middle_ref, last_ref,
        place_ref, dest_ref, conv_ref, sems,
    ):
        sources = (place_hbm, dest_hbm, conv_hbm, attr_hbm, first_hbm, middle_hbm, last_hbm)
        targets = (place_ref, dest_ref, conv_ref, attr_ref, first_ref, middle_ref, last_ref)
        copies = [
            pltpu.make_async_copy(source, target, sems.at[i])
            for i, (source, target) in enumerate(zip(sources, targets))
        ]
        for copy in copies:
            copy.start()
        copies[0].wait()
        count = place_ref.shape[1]
        span_z = wz_ref.shape[0]
        slots = pick_ref.shape[0]
        brick, line = lax.axis_index("brick"), lax.axis_index(("sect", "slab"))
        last_brick, last_line = lax.axis_size("brick") - 1, lax.axis_size(("sect", "slab")) - 1
        half = slots // 2
        local_x = place_ref[0:1, :] * span_x
        local_y = place_ref[1:2, :] * span_y
        local_z = place_ref[2:3, :] * span_z
        cell_z = iota((span_z, count), 0).astype(F32) + 0.5
        wz_ref[...] = hat(local_z - cell_z).astype(BF16)
        weight_y = []
        for y in range(span_y + 2):
            w = hat(local_y - (y - 0.5))
            if y == 0:
                w = jnp.where(line > 0, w, 0.0)
            if y == span_y + 1:
                w = jnp.where(line < last_line, w, 0.0)
            weight_y.append(w)
        for x in range(span_x + 2):
            w = hat(local_x - (x - 0.5))
            if x == 0:
                w = jnp.where(brick > 0, w, 0.0)
            if x == span_x + 1:
                w = jnp.where(brick < last_brick, w, 0.0)
            for y in range(span_y + 2):
                row = x * (span_y + 2) + y
                wxy_ref[row : row + 1, :] = w * weight_y[y]
        copies[1].wait()
        row = dest_ref[...].astype(F32)
        earlier, later = iota((count, count), 0), iota((count, count), 1)
        diagonal = jnp.where(earlier == later, jnp.broadcast_to(row, (count, count)), 0.0)
        along = jnp.sum(diagonal, axis=1, keepdims=True)
        same = jnp.where((along == row) & (earlier < later), 1.0, 0.0)
        arrival = jnp.sum(same, axis=0, keepdims=True).astype(jnp.int32)
        target = row.astype(jnp.int32)
        slot = ((target % sects) * bricks + target // sects) * capacity + arrival
        pick = jnp.where(iota((slots, count), 0) == slot, 1.0, 0.0).astype(BF16)
        pick_ref[...] = pick
        copies[2].wait()
        channels = conv_ref.shape[-1]
        group = 9 * channels
        kernel_ref[:channels, 3 * group :] = jnp.zeros((channels, group), BF16)
        kernel_ref[channels:, :group] = jnp.zeros((channels, group), BF16)
        for a in range(3):
            for b in range(3):
                for e in range(3):
                    tile = conv_ref[a, b, e].astype(F32).T.astype(BF16)
                    for j in range(2):
                        lanes = (j + b) * group + (a * 3 + e) * channels
                        kernel_ref[j * channels : (j + 1) * channels, lanes : lanes + channels] = tile
        for copy in copies[3:]:
            copy.wait()

    return body


def taps(tile, inside=True):
    span_z = tile.shape[1]
    lane = iota((1, span_z), 1)
    below, here, above = (
        jnp.where(keep & inside, 1.0, 0.0).astype(BF16)
        for keep in (lane > 0, lane >= 0, lane < span_z - 1)
    )
    pieces = (pltpu.roll(tile, 1, 1) * below, tile * here, pltpu.roll(tile, span_z - 1, 1) * above)
    return jnp.concatenate(pieces, axis=0)


def share(total, units, kernel_ref, wz_ref, wxy_ref):
    channels, span_z = total.shape[0], wz_ref.shape[0]
    for first in range(0, len(units), 4):
        group = units[first : first + 4]
        wide = jnp.concatenate(
            [
                jnp.concatenate([tap(x + a, c) for tap, _, x in group], axis=1)
                for c in range(4)
                for a in range(3)
            ],
            axis=0,
        )
        part = jnp.dot(kernel_ref[...], wide, preferred_element_type=F32)
        tiles, weights = [], []
        for j in range(2):
            centre = jnp.concatenate(
                [tap(x + 1, j + 1)[channels : 2 * channels] for tap, _, x in group], axis=1
            )
            response = part[j * channels : (j + 1) * channels]
            latent = (centre.astype(F32) + gelu(response)).astype(BF16)
            for u, (_, row, x) in enumerate(group):
                tiles.append(latent[:, u * span_z : (u + 1) * span_z])
                weights.append(wxy_ref[pl.ds(row(x) + j, 1), :])
        sampled = jnp.dot(
            jnp.concatenate(tiles, axis=0), wz_ref[...], preferred_element_type=F32
        )
        for k, w in enumerate(weights):
            total += sampled[k * channels : (k + 1) * channels] * w
    return total


def inner_units(layers, span_y, layer_taps):
    return [
        (
            lambda x, c, y=y: layer_taps(x)[y - HALO + c],
            lambda x, y=y: x * (span_y + 2) + y,
            x,
        )
        for x in layers
        for y in range(HALO, span_y, 2)
    ]


def block_body(own_ref, kernel_ref, wz_ref, wxy_ref, taps_ref, total_ref):
    span_x, span_y = own_ref.shape[:2]
    for x in range(span_x):
        for y in range(span_y):
            taps_ref[x, y] = taps(own_ref[x, y])
    units = inner_units(range(HALO, span_x), span_y, lambda x: taps_ref.at[x - HALO])
    total = jnp.zeros(total_ref.shape, F32)
    total_ref[...] = share(total, units, kernel_ref, wz_ref, wxy_ref)


def layer_of(own_ref, halo_ref, x):
    span_x = own_ref.shape[0]
    if HALO <= x < HALO + span_x:
        return own_ref.at[x - HALO]
    return halo_ref.at[x if x < HALO else x - span_x]


def inner_body(
    own_ref, before_ref, after_ref, kernel_ref, wz_ref, wxy_ref, start_ref, halo_ref, total_ref
):
    span_x, span_y = own_ref.shape[:2]
    for x in range(HALO):
        for y in range(span_y):
            halo_ref[x, y] = taps(before_ref[x, y])
            halo_ref[HALO + x, y] = taps(after_ref[x, y])
    layers = [*range(HALO), *range(span_x, span_x + 2)]
    units = inner_units(layers, span_y, lambda x: layer_of(own_ref, halo_ref, x))
    total_ref[...] = share(start_ref[...], units, kernel_ref, wz_ref, wxy_ref)


class Shifted:
    def __init__(self, ref, base):
        self.ref, self.base = ref, base

    def __getitem__(self, at):
        return self.ref[at[0] - self.base, at[1]]

    def __setitem__(self, at, value):
        self.ref[at[0] - self.base, at[1]] = value


def side_units(on_left, inside, layers, halo_tile, own_ref, halo_ref, side_ref, ready_ref=None):
    span_x, span_y = own_ref.shape[:2]
    near = jnp.where(on_left, 0, span_y - HALO)

    def ready(x):
        return ready_ref is not None and HALO <= x < HALO + span_x

    for x in sorted({x + a for x in layers for a in range(3)}):
        if ready(x):
            continue
        for j in range(HALO):
            side_ref[x, jnp.where(on_left, HALO, 0) + j] = layer_of(own_ref, halo_ref, x)[near + j]
            side_ref[x, jnp.where(on_left, 0, HALO) + j] = taps(halo_tile(x)[j], inside)
    base = jnp.where(on_left, 0, span_y)

    def tap(x, c):
        return ready_ref[x - HALO, c] if ready(x) else side_ref[x, c]

    return [(tap, lambda x: x * (span_y + 2) + base, x) for x in layers]


def cross_units(layers, cross_ref, corner_ref, own_ref, halo_ref, side_ref, ready_ref=None):
    line = lax.axis_index(("sect", "slab"))
    inside = (line > 0) & (line < lax.axis_size(("sect", "slab")) - 1)
    return side_units(
        lax.axis_index("slab") == 0, inside, layers, lambda x: layer_of(cross_ref, corner_ref, x),
        own_ref, halo_ref, side_ref, ready_ref,
    )


def beside_body(
    own_ref, halo_ref, partner_ref, cross_ref, kernel_ref, wz_ref, wxy_ref, start_ref,
    total_ref, ready_ref, partner_side,
):
    span_x = own_ref.shape[0]
    units = side_units(
        lax.axis_index("slab") == 1, True, range(span_x + 2), lambda x: partner_ref.at[x],
        own_ref, halo_ref, partner_side,
    )
    units += cross_units(range(HALO, span_x), cross_ref, None, own_ref, halo_ref, Shifted(ready_ref, HALO))
    total_ref[...] = share(start_ref[...], units, kernel_ref, wz_ref, wxy_ref)


def outer_body(
    own_ref, halo_ref, cross_ref, corner_ref, ready_ref, kernel_ref, wz_ref, wxy_ref, start_ref,
    pick_ref, attr_ref, first_ref, middle_ref, last_ref,
    value_ref, row_ref, cross_side,
):
    span_x = own_ref.shape[0]
    layers = [*range(HALO), *range(span_x, span_x + 2)]
    units = cross_units(layers, cross_ref, corner_ref, own_ref, halo_ref, cross_side, ready_ref)
    total = share(start_ref[...], units, kernel_ref, wz_ref, wxy_ref)
    table = jnp.concatenate([total.astype(BF16), attr_ref[...]], axis=0)
    row = lax.dot_general(
        pick_ref[...], table, (((1,), (1,)), ((), ())), preferred_element_type=F32
    ).astype(BF16)
    half = row.shape[0] // 2
    for s in range(2):
        row_ref[s] = row[s * half : (s + 1) * half]
    network(1 - own_section(), row_ref, first_ref, middle_ref, last_ref, value_ref)


def own_section():
    return lax.axis_index("sect") // (lax.axis_size("sect") // 2)


def own_place():
    return (
        lax.axis_index("sect") % (lax.axis_size("sect") // 2) * lax.axis_size("brick")
        + lax.axis_index("brick")
    )


def network(s, row_ref, first_ref, middle_ref, last_ref, value_ref):
    act = gelu(jnp.dot(row_ref[s], first_ref[s], preferred_element_type=F32)).astype(BF16)
    for i in range(middle_ref.shape[1]):
        act = gelu(jnp.dot(act, middle_ref[s, i], preferred_element_type=F32)).astype(BF16)
    value = lax.dot_general(
        last_ref[s], act, (((1,), (1,)), ((), ())), preferred_element_type=F32
    )
    blocks, _, capacity = value_ref.shape
    place = own_place()
    for q in range(blocks):
        value_ref[q ^ place] = value[:, q * capacity : (q + 1) * capacity]


def own_body(*refs):
    network(own_section(), *refs)


def make_deal_body(sent, kept):
    def body(kept_ref, got_ref, sent_out, kept_out):
        for out, blocks in ((sent_out, sent), (kept_out, kept)):
            for i, (which, at) in enumerate(blocks):
                out[i] = (kept_ref, got_ref)[which][at]

    return body


def make_collect_body(order, bricks, sects):
    def body(kept_ref, got_ref, out_ref, blocks):
        for r, (which, at) in enumerate(order):
            blocks[r] = (kept_ref, got_ref)[which][at]
        capacity = kept_ref.shape[2]
        me = own_section() * (bricks * sects // 2) + own_place()
        for brick in range(bricks):
            for sect in range(sects):
                lane = (brick * sects + sect) * capacity
                out_ref[:, lane : lane + capacity] = blocks[(sect * bricks + brick) ^ me]

    return body


def swap(array, axis, step):
    return lax.ppermute(array, axis, [(i, i ^ step) for i in range(lax.axis_size(axis))])


def swap_pairs(array, axes, start, fill):
    everything = ("case", "brick", "sect", "slab")
    sizes = [lax.axis_size(a) for a in everything]
    pairs = []
    for i, at in enumerate(np.ndindex(*sizes)):
        at = dict(zip(everything, at))
        place, size = 0, 1
        for a in axes:
            place, size = place * lax.axis_size(a) + at[a], size * lax.axis_size(a)
        other = place + 1 if (place - start) % 2 == 0 else place - 1
        if 0 <= other < size:
            for a in reversed(axes):
                other, at[a] = divmod(other, lax.axis_size(a))
        else:
            at[fill] ^= 1
        pairs.append((i, int(np.ravel_multi_index([at[a] for a in everything], sizes))))
    return lax.ppermute(array, everything, pairs)


def on_device(
    geometry,
    conv_kernels,
    point_place,
    point_attr,
    destination,
    dense_first,
    dense_middle,
    dense_last,
):
    channels, span_x, span_y, span_z = geometry.shape
    count = point_place.shape[1]
    bricks, sects = lax.axis_size("brick"), lax.axis_size("sect")
    capacity = 5 * count // (4 * bricks * sects)
    slots = bricks * sects * capacity
    outputs = dense_last.shape[1]
    lines = ("sect", "slab")

    def block(*shape):
        return jax.ShapeDtypeStruct(shape, BF16)

    own, even, odd, facing = call(
        columns_body,
        [
            block(span_x, span_y, channels, span_z),
            block(HALO, span_y, channels, span_z),
            block(HALO, span_y, channels, span_z),
            block(span_x, HALO, channels, span_z),
        ],
        [],
        8,
    )(geometry)
    even = swap_pairs(even, ("brick",), 0, "slab")
    odd = swap_pairs(odd, ("brick",), 1, "slab")
    cross = swap_pairs(facing, lines, 1, "case")
    pick, wz, wxy, kernel, attr, first, middle, last = call(
        make_points_body(span_x, span_y, bricks, sects, capacity),
        [
            block(slots, count),
            block(span_z, count),
            jax.ShapeDtypeStruct(((span_x + 2) * (span_y + 2), count), F32),
            block(2 * channels, 36 * channels),
            block(point_attr.shape[1], count),
            block(*dense_first.shape),
            block(*dense_middle.shape),
            block(*dense_last.shape),
        ],
        [
            pltpu.VMEM(point_place.shape, F32),
            pltpu.VMEM((1, count), jnp.int32),
            pltpu.VMEM(conv_kernels.shape[1:], BF16),
            pltpu.SemaphoreType.DMA((7,)),
        ],
        12,
        n_hbm=7,
    )(point_place, destination.reshape(1, count), conv_kernels[0], point_attr.T, dense_first,
      dense_middle, dense_last)
    features = jax.ShapeDtypeStruct((channels, count), F32)
    own_taps, total = call(
        block_body, [block(span_x, span_y, 3 * channels, span_z), features], [], 8
    )(own, kernel, wz, wxy)
    before, after, to_partner, to_cross = call(
        edges_body,
        [
            block(HALO, span_y, channels, span_z),
            block(HALO, span_y, channels, span_z),
            block(span_x + 2 * HALO, HALO, channels, span_z),
            block(2 * HALO, HALO, channels, span_z),
        ],
        [],
        4,
    )(own, even, odd, total)
    partner = swap(to_partner, "slab", 1)
    corner = swap_pairs(to_cross, lines, 1, "case")
    halo_taps, total = call(
        inner_body, [block(2 * HALO, span_y, 3 * channels, span_z), features], [], 8
    )(own_taps, before, after, kernel, wz, wxy, total)
    side = pltpu.VMEM((span_x + 2 * HALO, 2 * HALO, 3 * channels, span_z), BF16)
    ready = block(span_x, 2 * HALO, 3 * channels, span_z)
    total, ready = call(beside_body, [features, ready], [side], 10)(
        own_taps, halo_taps, partner, cross, kernel, wz, wxy, total
    )
    blocks = bricks * sects // 2

    def values(number):
        return jax.ShapeDtypeStruct((number, outputs, capacity), F32)

    sent, table = call(
        outer_body, [values(blocks), block(2, slots // 2, point_attr.shape[1] + channels)], [side], 8
    )(own_taps, halo_taps, cross, corner, ready, kernel, wz, wxy, total, pick, attr, first, middle, last)
    got = swap(sent, "sect", sects // 2)
    kept = call(own_body, values(blocks), [], 8)(table, first, middle, last)
    labels = [list(range(blocks)), [blocks + q for q in range(blocks)]]
    step = blocks // 2
    while step:
        found = [(label, w, i) for w in range(2) for i, label in enumerate(labels[w])]
        leaving = [f for f in found if f[0] & step]
        staying = [f for f in found if not f[0] & step]
        sent, kept = call(
            make_deal_body([f[1:] for f in leaving], [f[1:] for f in staying]), [values(blocks)] * 2, [], 2
        )(kept, got)
        axis, distance = ("brick", step) if step < bricks else ("sect", step // bricks)
        got = swap(sent, axis, distance)
        labels = [[f[0] for f in staying], [f[0] for f in leaving]]
        step //= 2
    order = {label: (w, i) for w in range(2) for i, label in enumerate(labels[w])}
    return call(
        make_collect_body([order[r] for r in range(2 * blocks)], bricks, sects),
        jax.ShapeDtypeStruct((outputs, slots), F32),
        [pltpu.VMEM((2 * blocks, outputs, capacity), F32)],
        2,
    )(kept, got)


def solution(mesh):
    in_specs = (
        P(None, ("case", "brick"), ("sect", "slab"), None),
        P(),
        P(None, ("case", "brick", "sect", "slab")),
        P(("case", "brick", "sect", "slab"), None),
        P(("case", "brick", "sect", "slab"), None),
        P(),
        P(),
        P(),
    )
    out_specs = P(None, ("case", "brick", "sect", "slab"))
    return jax.shard_map(on_device, mesh=mesh, in_specs=in_specs, out_specs=out_specs, check_vma=False)
```

```python
import jax
import jax.numpy as jnp
import numpy as np
from jax import lax
from jax.experimental import pallas as pl
from jax.experimental.pallas import tpu as pltpu
from jax.sharding import PartitionSpec as P


F32 = jnp.float32
BF16 = jnp.bfloat16
HALO = 2


def hat(offset):
    return jnp.maximum(0.0, 1.0 - jnp.abs(offset))


def gelu(value):
    half = 0.5 * value
    slope = 0.7978845608028654
    return half + half * jnp.tanh(value * (slope + (slope * 0.044715) * (value * value)))


def iota(shape, axis):
    return lax.broadcasted_iota(jnp.int32, shape, axis)


def call(body, outs, scratch, mib, n_hbm=0):
    def run(*args):
        spaces = [pltpu.VMEM] * (len(args) - n_hbm) + [pltpu.HBM] * n_hbm
        args = [pltpu.with_memory_space_constraint(a, s) if s == pltpu.HBM else a for a, s in zip(args, spaces)]
        return pl.pallas_call(
            body,
            out_shape=outs,
            in_specs=[pl.BlockSpec(memory_space=s) for s in spaces],
            out_specs=jax.tree.map(lambda _: pl.BlockSpec(memory_space=pltpu.VMEM), outs),
            scratch_shapes=scratch,
            compiler_params=pltpu.CompilerParams(vmem_limit_bytes=mib << 20),
        )(*args)

    return run


def columns_body(g_ref, own_ref, even_ref, odd_ref, cross_ref):
    span_x, span_y = g_ref.shape[1:3]
    parity, slab = lax.axis_index("brick") % 2, lax.axis_index("slab")
    for x in range(span_x):
        own_ref[x] = jnp.swapaxes(g_ref[:, x], 0, 1)
    for side in range(2):

        @pl.when(parity == side)
        def _(up=(even_ref, odd_ref)[side], down=(odd_ref, even_ref)[side]):
            up[...] = own_ref[span_x - HALO :]
            down[...] = own_ref[:HALO]

        @pl.when(slab == side)
        def _(side=side):
            cross_ref[...] = own_ref[:, span_y - HALO :] if side else own_ref[:, :HALO]


def edges_body(own_ref, even_ref, odd_ref, _, before_ref, after_ref, partner_ref, cross_ref):
    span_x, span_y = own_ref.shape[:2]
    for side in range(2):

        @pl.when(lax.axis_index("brick") % 2 == side)
        def _(before=(odd_ref, even_ref)[side], after=(even_ref, odd_ref)[side]):
            brick, last = lax.axis_index("brick"), lax.axis_size("brick") - 1
            for ref, source, inside in (
                (before_ref, before, brick > 0),
                (after_ref, after, brick < last),
            ):
                keep = jnp.where(inside, jnp.ones((1, 1, 1, source.shape[3]), F32), 0.0).astype(BF16)
                ref[...] = source[...] * keep

    for slab in range(2):

        @pl.when(lax.axis_index("slab") == slab)
        def _(slab=slab):
            near, far = slice(0, HALO), slice(span_y - HALO, span_y)
            facing, outward = (near, far) if slab else (far, near)
            partner_ref[:HALO] = before_ref[:, facing]
            partner_ref[HALO : HALO + span_x] = own_ref[:, facing]
            partner_ref[HALO + span_x :] = after_ref[:, facing]
            cross_ref[:HALO] = before_ref[:, outward]
            cross_ref[HALO:] = after_ref[:, outward]


def make_points_body(span_x, span_y, bricks, sects, capacity):
    def body(
        place_hbm, dest_hbm, conv_hbm, attr_hbm, first_hbm, middle_hbm, last_hbm,
        pick_ref, wz_ref, wxy_ref, kernel_ref, attr_ref, first_ref, middle_ref, last_ref,
        place_ref, dest_ref, conv_ref, sems,
    ):
        sources = (place_hbm, dest_hbm, conv_hbm, attr_hbm, first_hbm, middle_hbm, last_hbm)
        targets = (place_ref, dest_ref, conv_ref, attr_ref, first_ref, middle_ref, last_ref)
        copies = [
            pltpu.make_async_copy(source, target, sems.at[i])
            for i, (source, target) in enumerate(zip(sources, targets))
        ]
        for copy in copies:
            copy.start()
        copies[0].wait()
        count = place_ref.shape[1]
        span_z = wz_ref.shape[0]
        slots = 2 * pick_ref.shape[1]
        brick, line = lax.axis_index("brick"), lax.axis_index(("sect", "slab"))
        last_brick, last_line = lax.axis_size("brick") - 1, lax.axis_size(("sect", "slab")) - 1
        half = slots // 2
        local_x = place_ref[0:1, :] * span_x
        local_y = place_ref[1:2, :] * span_y
        local_z = place_ref[2:3, :] * span_z
        cell_z = iota((span_z, count), 0).astype(F32) + 0.5
        wz_ref[...] = hat(local_z - cell_z).astype(BF16)
        weight_y = []
        for y in range(span_y + 2):
            w = hat(local_y - (y - 0.5))
            if y == 0:
                w = jnp.where(line > 0, w, 0.0)
            if y == span_y + 1:
                w = jnp.where(line < last_line, w, 0.0)
            weight_y.append(w)
        for x in range(span_x + 2):
            w = hat(local_x - (x - 0.5))
            if x == 0:
                w = jnp.where(brick > 0, w, 0.0)
            if x == span_x + 1:
                w = jnp.where(brick < last_brick, w, 0.0)
            for y in range(span_y + 2):
                row = x * (span_y + 2) + y
                wxy_ref[row : row + 1, :] = w * weight_y[y]
        copies[1].wait()
        row = dest_ref[...].astype(F32)
        earlier, later = iota((count, count), 0), iota((count, count), 1)
        diagonal = jnp.where(earlier == later, jnp.broadcast_to(row, (count, count)), 0.0)
        along = jnp.sum(diagonal, axis=1, keepdims=True)
        same = jnp.where((along == row) & (earlier < later), 1.0, 0.0)
        arrival = jnp.sum(same, axis=0, keepdims=True).astype(jnp.int32)
        target = row.astype(jnp.int32)
        slot = ((target % sects) * bricks + target // sects) * capacity + arrival
        pick = jnp.where(iota((slots, count), 0) == slot, 1.0, 0.0).astype(BF16)
        half = slots // 2
        for s in range(2):
            pick_ref[s] = pick[s * half : (s + 1) * half]
        copies[2].wait()
        channels = conv_ref.shape[-1]
        group = 9 * channels
        kernel_ref[:channels, 3 * group :] = jnp.zeros((channels, group), BF16)
        kernel_ref[channels:, :group] = jnp.zeros((channels, group), BF16)
        for a in range(3):
            for b in range(3):
                for e in range(3):
                    tile = conv_ref[a, b, e].astype(F32).T.astype(BF16)
                    for j in range(2):
                        lanes = (j + b) * group + (a * 3 + e) * channels
                        kernel_ref[j * channels : (j + 1) * channels, lanes : lanes + channels] = tile
        for copy in copies[3:]:
            copy.wait()

    return body


def taps(tile, inside=True):
    span_z = tile.shape[1]
    lane = iota((1, span_z), 1)
    below, here, above = (
        jnp.where(keep & inside, 1.0, 0.0).astype(BF16)
        for keep in (lane > 0, lane >= 0, lane < span_z - 1)
    )
    pieces = (pltpu.roll(tile, 1, 1) * below, tile * here, pltpu.roll(tile, span_z - 1, 1) * above)
    return jnp.concatenate(pieces, axis=0)


def share(total, units, kernel_ref, wz_ref, wxy_ref):
    channels, span_z = total.shape[0], wz_ref.shape[0]
    for first in range(0, len(units), 4):
        group = units[first : first + 4]
        wide = jnp.concatenate(
            [
                jnp.concatenate([tap(x + a, c) for tap, _, x in group], axis=1)
                for c in range(4)
                for a in range(3)
            ],
            axis=0,
        )
        part = jnp.dot(kernel_ref[...], wide, preferred_element_type=F32)
        tiles, weights = [], []
        for j in range(2):
            centre = jnp.concatenate(
                [tap(x + 1, j + 1)[channels : 2 * channels] for tap, _, x in group], axis=1
            )
            response = part[j * channels : (j + 1) * channels]
            latent = (centre.astype(F32) + gelu(response)).astype(BF16)
            for u, (_, row, x) in enumerate(group):
                tiles.append(latent[:, u * span_z : (u + 1) * span_z])
                weights.append(wxy_ref[pl.ds(row(x) + j, 1), :])
        sampled = jnp.dot(
            jnp.concatenate(tiles, axis=0), wz_ref[...], preferred_element_type=F32
        )
        for k, w in enumerate(weights):
            total += sampled[k * channels : (k + 1) * channels] * w
    return total


def inner_units(layers, span_y, layer_taps):
    return [
        (
            lambda x, c, y=y: layer_taps(x)[y - HALO + c],
            lambda x, y=y: x * (span_y + 2) + y,
            x,
        )
        for x in layers
        for y in range(HALO, span_y, 2)
    ]


def block_body(own_ref, kernel_ref, wz_ref, wxy_ref, taps_ref, total_ref):
    span_x, span_y = own_ref.shape[:2]
    for x in range(span_x):
        for y in range(span_y):
            taps_ref[x, y] = taps(own_ref[x, y])
    units = inner_units(range(HALO, span_x), span_y, lambda x: taps_ref.at[x - HALO])
    total = jnp.zeros(total_ref.shape, F32)
    total_ref[...] = share(total, units, kernel_ref, wz_ref, wxy_ref)


def layer_of(own_ref, halo_ref, x):
    span_x = own_ref.shape[0]
    if HALO <= x < HALO + span_x:
        return own_ref.at[x - HALO]
    return halo_ref.at[x if x < HALO else x - span_x]


def inner_body(
    own_ref, before_ref, after_ref, kernel_ref, wz_ref, wxy_ref, start_ref, halo_ref, total_ref
):
    span_x, span_y = own_ref.shape[:2]
    for x in range(HALO):
        for y in range(span_y):
            halo_ref[x, y] = taps(before_ref[x, y])
            halo_ref[HALO + x, y] = taps(after_ref[x, y])
    layers = [*range(HALO), *range(span_x, span_x + 2)]
    units = inner_units(layers, span_y, lambda x: layer_of(own_ref, halo_ref, x))
    total_ref[...] = share(start_ref[...], units, kernel_ref, wz_ref, wxy_ref)


class Shifted:
    def __init__(self, ref, base):
        self.ref, self.base = ref, base

    def __getitem__(self, at):
        return self.ref[at[0] - self.base, at[1]]

    def __setitem__(self, at, value):
        self.ref[at[0] - self.base, at[1]] = value


def side_units(on_left, inside, layers, halo_tile, own_ref, halo_ref, side_ref, ready_ref=None):
    span_x, span_y = own_ref.shape[:2]
    near = jnp.where(on_left, 0, span_y - HALO)

    def ready(x):
        return ready_ref is not None and HALO <= x < HALO + span_x

    for x in sorted({x + a for x in layers for a in range(3)}):
        if ready(x):
            continue
        for j in range(HALO):
            side_ref[x, jnp.where(on_left, HALO, 0) + j] = layer_of(own_ref, halo_ref, x)[near + j]
            side_ref[x, jnp.where(on_left, 0, HALO) + j] = taps(halo_tile(x)[j], inside)
    base = jnp.where(on_left, 0, span_y)

    def tap(x, c):
        return ready_ref[x - HALO, c] if ready(x) else side_ref[x, c]

    return [(tap, lambda x: x * (span_y + 2) + base, x) for x in layers]


def cross_units(layers, cross_ref, corner_ref, own_ref, halo_ref, side_ref, ready_ref=None):
    line = lax.axis_index(("sect", "slab"))
    inside = (line > 0) & (line < lax.axis_size(("sect", "slab")) - 1)
    return side_units(
        lax.axis_index("slab") == 0, inside, layers, lambda x: layer_of(cross_ref, corner_ref, x),
        own_ref, halo_ref, side_ref, ready_ref,
    )


def beside_body(
    own_ref, halo_ref, partner_ref, cross_ref, kernel_ref, wz_ref, wxy_ref, start_ref,
    total_ref, ready_ref, partner_side,
):
    span_x = own_ref.shape[0]
    units = side_units(
        lax.axis_index("slab") == 1, True, range(span_x + 2), lambda x: partner_ref.at[x],
        own_ref, halo_ref, partner_side,
    )
    units += cross_units(range(HALO, span_x), cross_ref, None, own_ref, halo_ref, Shifted(ready_ref, HALO))
    total_ref[...] = share(start_ref[...], units, kernel_ref, wz_ref, wxy_ref)


def outer_body(
    own_ref, halo_ref, cross_ref, corner_ref, ready_ref, kernel_ref, wz_ref, wxy_ref, start_ref,
    pick_ref, attr_ref, first_ref, middle_ref, last_ref,
    value_ref, table_ref, cross_side,
):
    span_x = own_ref.shape[0]
    layers = [*range(HALO), *range(span_x, span_x + 2)]
    units = cross_units(layers, cross_ref, corner_ref, own_ref, halo_ref, cross_side, ready_ref)
    total = share(start_ref[...], units, kernel_ref, wz_ref, wxy_ref)
    table_ref[...] = jnp.concatenate([total.astype(BF16), attr_ref[...]], axis=0)
    network(
        1 - own_section(), pick_ref, table_ref, first_ref, middle_ref, last_ref, value_ref
    )


def own_section():
    return lax.axis_index("sect") // (lax.axis_size("sect") // 2)


def own_place():
    return (
        lax.axis_index("sect") % (lax.axis_size("sect") // 2) * lax.axis_size("brick")
        + lax.axis_index("brick")
    )


def network(s, pick_ref, table_ref, first_ref, middle_ref, last_ref, value_ref):
    row = lax.dot_general(
        pick_ref[s], table_ref[...], (((1,), (1,)), ((), ())), preferred_element_type=F32
    ).astype(BF16)
    act = gelu(jnp.dot(row, first_ref[s], preferred_element_type=F32)).astype(BF16)
    for i in range(middle_ref.shape[1]):
        act = gelu(jnp.dot(act, middle_ref[s, i], preferred_element_type=F32)).astype(BF16)
    value = lax.dot_general(
        last_ref[s], act, (((1,), (1,)), ((), ())), preferred_element_type=F32
    )
    blocks, _, capacity = value_ref.shape
    place = own_place()
    for q in range(blocks):
        value_ref[q ^ place] = value[:, q * capacity : (q + 1) * capacity]


def own_body(*refs):
    network(own_section(), *refs)


def make_deal_body(sent, kept):
    def body(kept_ref, got_ref, sent_out, kept_out):
        for out, blocks in ((sent_out, sent), (kept_out, kept)):
            for i, (which, at) in enumerate(blocks):
                out[i] = (kept_ref, got_ref)[which][at]

    return body


def make_collect_body(order, bricks, sects):
    def body(kept_ref, got_ref, out_ref, blocks):
        for r, (which, at) in enumerate(order):
            blocks[r] = (kept_ref, got_ref)[which][at]
        capacity = kept_ref.shape[2]
        me = own_section() * (bricks * sects // 2) + own_place()
        for brick in range(bricks):
            for sect in range(sects):
                lane = (brick * sects + sect) * capacity
                out_ref[:, lane : lane + capacity] = blocks[(sect * bricks + brick) ^ me]

    return body


def swap(array, axis, step):
    return lax.ppermute(array, axis, [(i, i ^ step) for i in range(lax.axis_size(axis))])


def swap_pairs(array, axes, start, fill):
    everything = ("case", "brick", "sect", "slab")
    sizes = [lax.axis_size(a) for a in everything]
    pairs = []
    for i, at in enumerate(np.ndindex(*sizes)):
        at = dict(zip(everything, at))
        place, size = 0, 1
        for a in axes:
            place, size = place * lax.axis_size(a) + at[a], size * lax.axis_size(a)
        other = place + 1 if (place - start) % 2 == 0 else place - 1
        if 0 <= other < size:
            for a in reversed(axes):
                other, at[a] = divmod(other, lax.axis_size(a))
        else:
            at[fill] ^= 1
        pairs.append((i, int(np.ravel_multi_index([at[a] for a in everything], sizes))))
    return lax.ppermute(array, everything, pairs)


def on_device(
    geometry,
    conv_kernels,
    point_place,
    point_attr,
    destination,
    dense_first,
    dense_middle,
    dense_last,
):
    channels, span_x, span_y, span_z = geometry.shape
    count = point_place.shape[1]
    bricks, sects = lax.axis_size("brick"), lax.axis_size("sect")
    capacity = 5 * count // (4 * bricks * sects)
    slots = bricks * sects * capacity
    outputs = dense_last.shape[1]
    lines = ("sect", "slab")

    def block(*shape):
        return jax.ShapeDtypeStruct(shape, BF16)

    own, even, odd, facing = call(
        columns_body,
        [
            block(span_x, span_y, channels, span_z),
            block(HALO, span_y, channels, span_z),
            block(HALO, span_y, channels, span_z),
            block(span_x, HALO, channels, span_z),
        ],
        [],
        8,
    )(geometry)
    even = swap_pairs(even, ("brick",), 0, "slab")
    odd = swap_pairs(odd, ("brick",), 1, "slab")
    cross = swap_pairs(facing, lines, 1, "case")
    pick, wz, wxy, kernel, attr, first, middle, last = call(
        make_points_body(span_x, span_y, bricks, sects, capacity),
        [
            block(2, slots // 2, count),
            block(span_z, count),
            jax.ShapeDtypeStruct(((span_x + 2) * (span_y + 2), count), F32),
            block(2 * channels, 36 * channels),
            block(point_attr.shape[1], count),
            block(*dense_first.shape),
            block(*dense_middle.shape),
            block(*dense_last.shape),
        ],
        [
            pltpu.VMEM(point_place.shape, F32),
            pltpu.VMEM((1, count), jnp.int32),
            pltpu.VMEM(conv_kernels.shape[1:], BF16),
            pltpu.SemaphoreType.DMA((7,)),
        ],
        12,
        n_hbm=7,
    )(point_place, destination.reshape(1, count), conv_kernels[0], point_attr.T, dense_first,
      dense_middle, dense_last)
    features = jax.ShapeDtypeStruct((channels, count), F32)
    own_taps, total = call(
        block_body, [block(span_x, span_y, 3 * channels, span_z), features], [], 8
    )(own, kernel, wz, wxy)
    before, after, to_partner, to_cross = call(
        edges_body,
        [
            block(HALO, span_y, channels, span_z),
            block(HALO, span_y, channels, span_z),
            block(span_x + 2 * HALO, HALO, channels, span_z),
            block(2 * HALO, HALO, channels, span_z),
        ],
        [],
        4,
    )(own, even, odd, total)
    partner = swap(to_partner, "slab", 1)
    corner = swap_pairs(to_cross, lines, 1, "case")
    halo_taps, total = call(
        inner_body, [block(2 * HALO, span_y, 3 * channels, span_z), features], [], 8
    )(own_taps, before, after, kernel, wz, wxy, total)
    side = pltpu.VMEM((span_x + 2 * HALO, 2 * HALO, 3 * channels, span_z), BF16)
    ready = block(span_x, 2 * HALO, 3 * channels, span_z)
    total, ready = call(beside_body, [features, ready], [side], 10)(
        own_taps, halo_taps, partner, cross, kernel, wz, wxy, total
    )
    blocks = bricks * sects // 2

    def values(number):
        return jax.ShapeDtypeStruct((number, outputs, capacity), F32)

    sent, table = call(
        outer_body, [values(blocks), block(channels + point_attr.shape[1], count)], [side], 8
    )(own_taps, halo_taps, cross, corner, ready, kernel, wz, wxy, total, pick, attr, first, middle, last)
    got = swap(sent, "sect", sects // 2)
    kept = call(own_body, values(blocks), [], 8)(pick, table, first, middle, last)
    labels = [list(range(blocks)), [blocks + q for q in range(blocks)]]
    step = blocks // 2
    while step:
        found = [(label, w, i) for w in range(2) for i, label in enumerate(labels[w])]
        leaving = [f for f in found if f[0] & step]
        staying = [f for f in found if not f[0] & step]
        sent, kept = call(
            make_deal_body([f[1:] for f in leaving], [f[1:] for f in staying]), [values(blocks)] * 2, [], 2
        )(kept, got)
        axis, distance = ("brick", step) if step < bricks else ("sect", step // bricks)
        got = swap(sent, axis, distance)
        labels = [[f[0] for f in staying], [f[0] for f in leaving]]
        step //= 2
    order = {label: (w, i) for w in range(2) for i, label in enumerate(labels[w])}
    return call(
        make_collect_body([order[r] for r in range(2 * blocks)], bricks, sects),
        jax.ShapeDtypeStruct((outputs, slots), F32),
        [pltpu.VMEM((2 * blocks, outputs, capacity), F32)],
        2,
    )(kept, got)


def solution(mesh):
    in_specs = (
        P(None, ("case", "brick"), ("sect", "slab"), None),
        P(),
        P(None, ("case", "brick", "sect", "slab")),
        P(("case", "brick", "sect", "slab"), None),
        P(("case", "brick", "sect", "slab"), None),
        P(),
        P(),
        P(),
    )
    out_specs = P(None, ("case", "brick", "sect", "slab"))
    return jax.shard_map(on_device, mesh=mesh, in_specs=in_specs, out_specs=out_specs, check_vma=False)
```

```python
import jax
import jax.numpy as jnp
import numpy as np
from jax import lax
from jax.experimental import pallas as pl
from jax.experimental.pallas import tpu as pltpu
from jax.sharding import PartitionSpec as P


F32 = jnp.float32
BF16 = jnp.bfloat16
HALO = 2


def hat(offset):
    return jnp.maximum(0.0, 1.0 - jnp.abs(offset))


def gelu(value):
    half = 0.5 * value
    slope = 0.7978845608028654
    return half + half * jnp.tanh(value * (slope + (slope * 0.044715) * (value * value)))


def iota(shape, axis):
    return lax.broadcasted_iota(jnp.int32, shape, axis)


def call(body, outs, scratch, mib, n_hbm=0):
    def run(*args):
        spaces = [pltpu.VMEM] * (len(args) - n_hbm) + [pltpu.HBM] * n_hbm
        args = [pltpu.with_memory_space_constraint(a, s) if s == pltpu.HBM else a for a, s in zip(args, spaces)]
        return pl.pallas_call(
            body,
            out_shape=outs,
            in_specs=[pl.BlockSpec(memory_space=s) for s in spaces],
            out_specs=jax.tree.map(lambda _: pl.BlockSpec(memory_space=pltpu.VMEM), outs),
            scratch_shapes=scratch,
            compiler_params=pltpu.CompilerParams(vmem_limit_bytes=mib << 20),
        )(*args)

    return run


def columns_body(g_ref, own_ref, even_ref, odd_ref, cross_ref):
    span_x, span_y = g_ref.shape[1:3]
    parity, slab = lax.axis_index("brick") % 2, lax.axis_index("slab")
    for x in range(span_x):
        own_ref[x] = jnp.swapaxes(g_ref[:, x], 0, 1)
    for side in range(2):

        @pl.when(parity == side)
        def _(up=(even_ref, odd_ref)[side], down=(odd_ref, even_ref)[side]):
            up[...] = own_ref[span_x - HALO :]
            down[...] = own_ref[:HALO]

        @pl.when(slab == side)
        def _(side=side):
            cross_ref[...] = own_ref[:, span_y - HALO :] if side else own_ref[:, :HALO]


def edges_body(own_ref, even_ref, odd_ref, _, before_ref, after_ref, partner_ref, cross_ref):
    span_x, span_y = own_ref.shape[:2]
    for side in range(2):

        @pl.when(lax.axis_index("brick") % 2 == side)
        def _(before=(odd_ref, even_ref)[side], after=(even_ref, odd_ref)[side]):
            brick, last = lax.axis_index("brick"), lax.axis_size("brick") - 1
            for ref, source, inside in (
                (before_ref, before, brick > 0),
                (after_ref, after, brick < last),
            ):
                keep = jnp.where(inside, jnp.ones((1, 1, 1, source.shape[3]), F32), 0.0).astype(BF16)
                ref[...] = source[...] * keep

    for slab in range(2):

        @pl.when(lax.axis_index("slab") == slab)
        def _(slab=slab):
            near, far = slice(0, HALO), slice(span_y - HALO, span_y)
            facing, outward = (near, far) if slab else (far, near)
            partner_ref[:HALO] = before_ref[:, facing]
            partner_ref[HALO : HALO + span_x] = own_ref[:, facing]
            partner_ref[HALO + span_x :] = after_ref[:, facing]
            cross_ref[:HALO] = before_ref[:, outward]
            cross_ref[HALO:] = after_ref[:, outward]


def make_points_body(span_x, span_y, bricks, sects, capacity):
    def body(
        place_hbm, dest_hbm, conv_hbm, attr_hbm, first_hbm, middle_hbm, last_hbm,
        pick_ref, wz_ref, wxy_ref, kernel_ref, attr_ref, first_ref, middle_ref, last_ref,
        place_ref, dest_ref, conv_ref, sems,
    ):
        sources = (place_hbm, dest_hbm, conv_hbm, attr_hbm, first_hbm, middle_hbm, last_hbm)
        targets = (place_ref, dest_ref, conv_ref, attr_ref, first_ref, middle_ref, last_ref)
        copies = [
            pltpu.make_async_copy(source, target, sems.at[i])
            for i, (source, target) in enumerate(zip(sources, targets))
        ]
        for copy in copies:
            copy.start()
        copies[0].wait()
        count = place_ref.shape[1]
        span_z = wz_ref.shape[0]
        slots = 2 * pick_ref.shape[1]
        brick, line = lax.axis_index("brick"), lax.axis_index(("sect", "slab"))
        last_brick, last_line = lax.axis_size("brick") - 1, lax.axis_size(("sect", "slab")) - 1
        half = slots // 2
        local_x = place_ref[0:1, :] * span_x
        local_y = place_ref[1:2, :] * span_y
        local_z = place_ref[2:3, :] * span_z
        cell_z = iota((span_z, count), 0).astype(F32) + 0.5
        wz_ref[...] = hat(local_z - cell_z).astype(BF16)
        weight_y = []
        for y in range(span_y + 2):
            w = hat(local_y - (y - 0.5))
            if y == 0:
                w = jnp.where(line > 0, w, 0.0)
            if y == span_y + 1:
                w = jnp.where(line < last_line, w, 0.0)
            weight_y.append(w)
        for x in range(span_x + 2):
            w = hat(local_x - (x - 0.5))
            if x == 0:
                w = jnp.where(brick > 0, w, 0.0)
            if x == span_x + 1:
                w = jnp.where(brick < last_brick, w, 0.0)
            for y in range(span_y + 2):
                row = x * (span_y + 2) + y
                wxy_ref[row : row + 1, :] = w * weight_y[y]
        copies[1].wait()
        row = dest_ref[...].astype(F32)
        earlier, later = iota((count, count), 0), iota((count, count), 1)
        diagonal = jnp.where(earlier == later, jnp.broadcast_to(row, (count, count)), 0.0)
        along = jnp.sum(diagonal, axis=1, keepdims=True)
        same = jnp.where((along == row) & (earlier < later), 1.0, 0.0)
        arrival = jnp.sum(same, axis=0, keepdims=True).astype(jnp.int32)
        target = row.astype(jnp.int32)
        slot = ((target % sects) * bricks + target // sects) * capacity + arrival
        pick = jnp.where(iota((slots, count), 0) == slot, 1.0, 0.0).astype(BF16)
        half = slots // 2
        for s in range(2):
            pick_ref[s] = pick[s * half : (s + 1) * half]
        copies[2].wait()
        channels = conv_ref.shape[-1]
        group = 9 * channels
        kernel_ref[:channels, 3 * group :] = jnp.zeros((channels, group), BF16)
        kernel_ref[channels:, :group] = jnp.zeros((channels, group), BF16)
        for a in range(3):
            for b in range(3):
                for e in range(3):
                    tile = conv_ref[a, b, e].astype(F32).T.astype(BF16)
                    for j in range(2):
                        lanes = (j + b) * group + (a * 3 + e) * channels
                        kernel_ref[j * channels : (j + 1) * channels, lanes : lanes + channels] = tile
        for copy in copies[3:]:
            copy.wait()

    return body


def taps(tile, inside=True):
    span_z = tile.shape[1]
    lane = iota((1, span_z), 1)
    below, here, above = (
        jnp.where(keep & inside, 1.0, 0.0).astype(BF16)
        for keep in (lane > 0, lane >= 0, lane < span_z - 1)
    )
    pieces = (pltpu.roll(tile, 1, 1) * below, tile if inside is True else tile * here, pltpu.roll(tile, span_z - 1, 1) * above)
    return jnp.concatenate(pieces, axis=0)


def share(total, units, kernel_ref, wz_ref, wxy_ref):
    channels, span_z = total.shape[0], wz_ref.shape[0]
    for first in range(0, len(units), 4):
        group = units[first : first + 4]
        wide = jnp.concatenate(
            [
                jnp.concatenate([tap(x + a, c) for tap, _, x in group], axis=1)
                for c in range(4)
                for a in range(3)
            ],
            axis=0,
        )
        part = jnp.dot(kernel_ref[...], wide, preferred_element_type=F32)
        tiles, weights = [], []
        for j in range(2):
            centre = jnp.concatenate(
                [tap(x + 1, j + 1)[channels : 2 * channels] for tap, _, x in group], axis=1
            )
            response = part[j * channels : (j + 1) * channels]
            latent = (centre.astype(F32) + gelu(response)).astype(BF16)
            for u, (_, row, x) in enumerate(group):
                tiles.append(latent[:, u * span_z : (u + 1) * span_z])
                weights.append(wxy_ref[pl.ds(row(x) + j, 1), :])
        sampled = jnp.dot(
            jnp.concatenate(tiles, axis=0), wz_ref[...], preferred_element_type=F32
        )
        for k, w in enumerate(weights):
            total += sampled[k * channels : (k + 1) * channels] * w
    return total


def inner_units(layers, span_y, layer_taps):
    return [
        (
            lambda x, c, y=y: layer_taps(x)[y - HALO + c],
            lambda x, y=y: x * (span_y + 2) + y,
            x,
        )
        for x in layers
        for y in range(HALO, span_y, 2)
    ]


def block_body(own_ref, kernel_ref, wz_ref, wxy_ref, taps_ref, total_ref):
    span_x, span_y = own_ref.shape[:2]
    for x in range(span_x):
        for y in range(span_y):
            taps_ref[x, y] = taps(own_ref[x, y])
    units = inner_units(range(HALO, span_x), span_y, lambda x: taps_ref.at[x - HALO])
    total = jnp.zeros(total_ref.shape, F32)
    total_ref[...] = share(total, units, kernel_ref, wz_ref, wxy_ref)


def layer_of(own_ref, halo_ref, x):
    span_x = own_ref.shape[0]
    if HALO <= x < HALO + span_x:
        return own_ref.at[x - HALO]
    return halo_ref.at[x if x < HALO else x - span_x]


def inner_body(
    own_ref, before_ref, after_ref, kernel_ref, wz_ref, wxy_ref, start_ref, halo_ref, total_ref
):
    span_x, span_y = own_ref.shape[:2]
    for x in range(HALO):
        for y in range(span_y):
            halo_ref[x, y] = taps(before_ref[x, y])
            halo_ref[HALO + x, y] = taps(after_ref[x, y])
    layers = [*range(HALO), *range(span_x, span_x + 2)]
    units = inner_units(layers, span_y, lambda x: layer_of(own_ref, halo_ref, x))
    total_ref[...] = share(start_ref[...], units, kernel_ref, wz_ref, wxy_ref)


class Shifted:
    def __init__(self, ref, base):
        self.ref, self.base = ref, base

    def __getitem__(self, at):
        return self.ref[at[0] - self.base, at[1]]

    def __setitem__(self, at, value):
        self.ref[at[0] - self.base, at[1]] = value


def side_units(on_left, inside, layers, halo_tile, own_ref, halo_ref, side_ref, ready_ref=None):
    span_x, span_y = own_ref.shape[:2]
    near = jnp.where(on_left, 0, span_y - HALO)

    def ready(x):
        return ready_ref is not None and HALO <= x < HALO + span_x

    for x in sorted({x + a for x in layers for a in range(3)}):
        if ready(x):
            continue
        for j in range(HALO):
            side_ref[x, jnp.where(on_left, HALO, 0) + j] = layer_of(own_ref, halo_ref, x)[near + j]
            side_ref[x, jnp.where(on_left, 0, HALO) + j] = taps(halo_tile(x)[j], inside)
    base = jnp.where(on_left, 0, span_y)

    def tap(x, c):
        return ready_ref[x - HALO, c] if ready(x) else side_ref[x, c]

    return [(tap, lambda x: x * (span_y + 2) + base, x) for x in layers]


def cross_units(layers, cross_ref, corner_ref, own_ref, halo_ref, side_ref, ready_ref=None):
    line = lax.axis_index(("sect", "slab"))
    inside = (line > 0) & (line < lax.axis_size(("sect", "slab")) - 1)
    return side_units(
        lax.axis_index("slab") == 0, inside, layers, lambda x: layer_of(cross_ref, corner_ref, x),
        own_ref, halo_ref, side_ref, ready_ref,
    )


def beside_body(
    own_ref, halo_ref, partner_ref, cross_ref, kernel_ref, wz_ref, wxy_ref, start_ref,
    total_ref, ready_ref, partner_side,
):
    span_x = own_ref.shape[0]
    units = side_units(
        lax.axis_index("slab") == 1, True, range(span_x + 2), lambda x: partner_ref.at[x],
        own_ref, halo_ref, partner_side,
    )
    units += cross_units(range(HALO, span_x), cross_ref, None, own_ref, halo_ref, Shifted(ready_ref, HALO))
    total_ref[...] = share(start_ref[...], units, kernel_ref, wz_ref, wxy_ref)


def outer_body(
    own_ref, halo_ref, cross_ref, corner_ref, ready_ref, kernel_ref, wz_ref, wxy_ref, start_ref,
    pick_ref, attr_ref, first_ref, middle_ref, last_ref,
    value_ref, table_ref, cross_side,
):
    span_x = own_ref.shape[0]
    layers = [*range(HALO), *range(span_x, span_x + 2)]
    units = cross_units(layers, cross_ref, corner_ref, own_ref, halo_ref, cross_side, ready_ref)
    total = share(start_ref[...], units, kernel_ref, wz_ref, wxy_ref)
    table_ref[...] = jnp.concatenate([total.astype(BF16), attr_ref[...]], axis=0)
    network(
        1 - own_section(), pick_ref, table_ref, first_ref, middle_ref, last_ref, value_ref
    )


def own_section():
    return lax.axis_index("sect") // (lax.axis_size("sect") // 2)


def own_place():
    return (
        lax.axis_index("sect") % (lax.axis_size("sect") // 2) * lax.axis_size("brick")
        + lax.axis_index("brick")
    )


def network(s, pick_ref, table_ref, first_ref, middle_ref, last_ref, value_ref):
    row = lax.dot_general(
        pick_ref[s], table_ref[...], (((1,), (1,)), ((), ())), preferred_element_type=F32
    ).astype(BF16)
    half = row.shape[0] // 2
    acts = [row[:half], row[half:]]
    for weights in [first_ref[s]] + [middle_ref[s, i] for i in range(middle_ref.shape[1])]:
        acts = [
            gelu(jnp.dot(act, weights, preferred_element_type=F32)).astype(BF16) for act in acts
        ]
    value = lax.dot_general(
        last_ref[s],
        jnp.concatenate(acts, axis=0),
        (((1,), (1,)), ((), ())),
        preferred_element_type=F32,
    )
    blocks, _, capacity = value_ref.shape
    place = own_place()
    for q in range(blocks):
        value_ref[q ^ place] = value[:, q * capacity : (q + 1) * capacity]


def own_body(*refs):
    network(own_section(), *refs)


def make_deal_body(sent, kept):
    def body(kept_ref, got_ref, sent_out, kept_out):
        for out, blocks in ((sent_out, sent), (kept_out, kept)):
            for i, (which, at) in enumerate(blocks):
                out[i] = (kept_ref, got_ref)[which][at]

    return body


def make_collect_body(order, bricks, sects):
    def body(kept_ref, got_ref, out_ref, blocks):
        for r, (which, at) in enumerate(order):
            blocks[r] = (kept_ref, got_ref)[which][at]
        capacity = kept_ref.shape[2]
        me = own_section() * (bricks * sects // 2) + own_place()
        for brick in range(bricks):
            for sect in range(sects):
                lane = (brick * sects + sect) * capacity
                out_ref[:, lane : lane + capacity] = blocks[(sect * bricks + brick) ^ me]

    return body


def swap(array, axis, step):
    return lax.ppermute(array, axis, [(i, i ^ step) for i in range(lax.axis_size(axis))])


def swap_pairs(array, axes, start, fill):
    everything = ("case", "brick", "sect", "slab")
    sizes = [lax.axis_size(a) for a in everything]
    pairs = []
    for i, at in enumerate(np.ndindex(*sizes)):
        at = dict(zip(everything, at))
        place, size = 0, 1
        for a in axes:
            place, size = place * lax.axis_size(a) + at[a], size * lax.axis_size(a)
        other = place + 1 if (place - start) % 2 == 0 else place - 1
        if 0 <= other < size:
            for a in reversed(axes):
                other, at[a] = divmod(other, lax.axis_size(a))
        else:
            at[fill] ^= 1
        pairs.append((i, int(np.ravel_multi_index([at[a] for a in everything], sizes))))
    return lax.ppermute(array, everything, pairs)


def on_device(
    geometry,
    conv_kernels,
    point_place,
    point_attr,
    destination,
    dense_first,
    dense_middle,
    dense_last,
):
    channels, span_x, span_y, span_z = geometry.shape
    count = point_place.shape[1]
    bricks, sects = lax.axis_size("brick"), lax.axis_size("sect")
    capacity = 5 * count // (4 * bricks * sects)
    slots = bricks * sects * capacity
    outputs = dense_last.shape[1]
    lines = ("sect", "slab")

    def block(*shape):
        return jax.ShapeDtypeStruct(shape, BF16)

    own, even, odd, facing = call(
        columns_body,
        [
            block(span_x, span_y, channels, span_z),
            block(HALO, span_y, channels, span_z),
            block(HALO, span_y, channels, span_z),
            block(span_x, HALO, channels, span_z),
        ],
        [],
        8,
    )(geometry)
    even = swap_pairs(even, ("brick",), 0, "slab")
    odd = swap_pairs(odd, ("brick",), 1, "slab")
    cross = swap_pairs(facing, lines, 1, "case")
    pick, wz, wxy, kernel, attr, first, middle, last = call(
        make_points_body(span_x, span_y, bricks, sects, capacity),
        [
            block(2, slots // 2, count),
            block(span_z, count),
            jax.ShapeDtypeStruct(((span_x + 2) * (span_y + 2), count), F32),
            block(2 * channels, 36 * channels),
            block(point_attr.shape[1], count),
            block(*dense_first.shape),
            block(*dense_middle.shape),
            block(*dense_last.shape),
        ],
        [
            pltpu.VMEM(point_place.shape, F32),
            pltpu.VMEM((1, count), jnp.int32),
            pltpu.VMEM(conv_kernels.shape[1:], BF16),
            pltpu.SemaphoreType.DMA((7,)),
        ],
        12,
        n_hbm=7,
    )(point_place, destination.reshape(1, count), conv_kernels[0], point_attr.T, dense_first,
      dense_middle, dense_last)
    features = jax.ShapeDtypeStruct((channels, count), F32)
    own_taps, total = call(
        block_body, [block(span_x, span_y, 3 * channels, span_z), features], [], 8
    )(own, kernel, wz, wxy)
    before, after, to_partner, to_cross = call(
        edges_body,
        [
            block(HALO, span_y, channels, span_z),
            block(HALO, span_y, channels, span_z),
            block(span_x + 2 * HALO, HALO, channels, span_z),
            block(2 * HALO, HALO, channels, span_z),
        ],
        [],
        4,
    )(own, even, odd, total)
    partner = swap(to_partner, "slab", 1)
    corner = swap_pairs(to_cross, lines, 1, "case")
    halo_taps, total = call(
        inner_body, [block(2 * HALO, span_y, 3 * channels, span_z), features], [], 8
    )(own_taps, before, after, kernel, wz, wxy, total)
    side = pltpu.VMEM((span_x + 2 * HALO, 2 * HALO, 3 * channels, span_z), BF16)
    ready = block(span_x, 2 * HALO, 3 * channels, span_z)
    total, ready = call(beside_body, [features, ready], [side], 10)(
        own_taps, halo_taps, partner, cross, kernel, wz, wxy, total
    )
    blocks = bricks * sects // 2

    def values(number):
        return jax.ShapeDtypeStruct((number, outputs, capacity), F32)

    sent, table = call(
        outer_body, [values(blocks), block(channels + point_attr.shape[1], count)], [side], 8
    )(own_taps, halo_taps, cross, corner, ready, kernel, wz, wxy, total, pick, attr, first, middle, last)
    got = swap(sent, "sect", sects // 2)
    kept = call(own_body, values(blocks), [], 8)(pick, table, first, middle, last)
    labels = [list(range(blocks)), [blocks + q for q in range(blocks)]]
    step = blocks // 2
    while step:
        found = [(label, w, i) for w in range(2) for i, label in enumerate(labels[w])]
        leaving = [f for f in found if f[0] & step]
        staying = [f for f in found if not f[0] & step]
        sent, kept = call(
            make_deal_body([f[1:] for f in leaving], [f[1:] for f in staying]), [values(blocks)] * 2, [], 2
        )(kept, got)
        axis, distance = ("brick", step) if step < bricks else ("sect", step // bricks)
        got = swap(sent, axis, distance)
        labels = [[f[0] for f in staying], [f[0] for f in leaving]]
        step //= 2
    order = {label: (w, i) for w in range(2) for i, label in enumerate(labels[w])}
    return call(
        make_collect_body([order[r] for r in range(2 * blocks)], bricks, sects),
        jax.ShapeDtypeStruct((outputs, slots), F32),
        [pltpu.VMEM((2 * blocks, outputs, capacity), F32)],
        2,
    )(kept, got)


def solution(mesh):
    in_specs = (
        P(None, ("case", "brick"), ("sect", "slab"), None),
        P(),
        P(None, ("case", "brick", "sect", "slab")),
        P(("case", "brick", "sect", "slab"), None),
        P(("case", "brick", "sect", "slab"), None),
        P(),
        P(),
        P(),
    )
    out_specs = P(None, ("case", "brick", "sect", "slab"))
    return jax.shard_map(on_device, mesh=mesh, in_specs=in_specs, out_specs=out_specs, check_vma=False)
```
